32 devices in a mesh: expert: 8 (over z, x), shard: 4 (over y, core).
Axes of the slice: x: 2, y: 2, z: 4, core: 2. Of those that a mesh axis runs over, the one named last changes fastest.
Arguments:
- tokens: bfloat16 [25216, 768], P(('expert', 'shard')), may hold values from -6 to 6
- routes: int32 [25216, 2], P(('expert', 'shard')), may hold values from 0 to 7, as said below
- capacity: int32 [8], replicated, may hold values from 100 to 200
- ln1_gain: float32 [768], replicated, may hold values from 0.5 to 1.5
- ln1_bias: float32 [768], replicated, may hold values from -1.5 to 1.5
- ln2_gain: float32 [768], replicated, may hold values from 0.5 to 1.5
- ln2_bias: float32 [768], replicated, may hold values from -1.5 to 1.5
- w_qkv: bfloat16 [768, 2304], P('shard'), may hold values from -0.21875 to 0.21875
- w_proj: bfloat16 [768, 768], P('shard'), may hold values from -0.875 to 0.875
- w_router: bfloat16 [768, 8], P('shard'), may hold values from -1 to 1
- w_in: bfloat16 [8, 768, 3072], P('expert'), may hold values from -0.21875 to 0.21875
- w_out: bfloat16 [8, 3072, 768], P('expert'), may hold values from -0.4375 to 0.4375
- cotangent: bfloat16 [25216, 768], P(('expert', 'shard')), may hold values from -6 to 6
Outputs:
- mixed: bfloat16 [25216, 768], P(('expert', 'shard'))
- balance_loss: float32 [], replicated
- grad_tokens: float32 [25216, 768], P(('expert', 'shard'))
- grad_ln1_gain: float32 [768], P('shard')
- grad_ln1_bias: float32 [768], P('shard')
- grad_ln2_gain: float32 [768], P('shard')
- grad_ln2_bias: float32 [768], P('shard')
- grad_qkv_weight: float32 [768, 2304], P('shard')
- grad_proj: float32 [768, 768], P('shard')
- grad_router: float32 [768, 8], P('shard')
- grad_expert_in: float32 [8, 768, 3072], P('expert', None, 'shard')
- grad_expert_out: float32 [8, 3072, 768], P('expert', 'shard')
The draws below stay inside these ranges and needn't reach their ends.
Inputs may be any that keep to these rules, and one draw needn't show every extreme that they name: `routes`: each row names two different experts.
All inputs are finite; a program needn't handle non-finite values.
Results may differ from the reference program's by a relative error of at most 0.012.
Values may be sent and summed in bfloat16 or wider, within the bound.
No kernel may reach another device: no remote copies, remote signals or barrier semaphores. Data moves between devices by JAX's collectives and lax.ppermute only.
A program may use at most 192 MiB of HBM per device.

```python
import math
import jax
import jax.numpy as jnp
from jax import lax

D = 768
HEADS = 12
HDIM = 64
FF = 3072
EXPERTS = 8
TOP = 2
SEQ = 197
IMG_DEV = 4
TOK_DEV = 788
TOKENS = 25216
CAP = 200


def hot_of(key):
    return jax.random.randint(jax.random.fold_in(key, 12), (), 0, EXPERTS)


def route_table(key):
    blocks = TOKENS // TOK_DEV
    key_weight = jax.random.fold_in(key, 11)
    key_pick = jax.random.fold_in(key, 13)
    key_mark = jax.random.fold_in(key, 14)
    key_other = jax.random.fold_in(key, 15)
    key_limit = jax.random.fold_in(key, 16)
    weights = jax.random.randint(key_weight, (EXPERTS,), 1, 9)
    hot_expert = hot_of(key)
    edges = jnp.cumsum(weights)
    pick = jax.random.randint(key_pick, (TOKENS,), 0, edges[EXPERTS - 1])
    first_choice = jnp.sum((pick[:, None] >= edges[None, :]).astype(jnp.int32), axis=1)
    ranks = jnp.arange(TOK_DEV, dtype=jnp.int32)

    def block_mark(index):
        order = jax.random.permutation(jax.random.fold_in(key_mark, index), TOK_DEV)
        forced = CAP + (TOK_DEV - CAP) * index // max(blocks - 1, 1)
        return jnp.zeros((TOK_DEV,), jnp.int32).at[order].set((ranks < forced).astype(jnp.int32))
    marks = jax.vmap(block_mark)(jnp.arange(blocks, dtype=jnp.int32)).reshape(TOKENS)
    first_choice = jnp.where(marks > 0, hot_expert, first_choice)
    offset = jax.random.randint(key_other, (TOKENS,), 1, EXPERTS)
    second_choice = (first_choice + offset) % EXPERTS
    route_rows = jnp.stack([first_choice, second_choice], axis=1).astype(jnp.int32)
    limits = jax.random.randint(key_limit, (EXPERTS,), CAP // 2, CAP + 1)
    limits = jnp.where(jnp.arange(EXPERTS) == hot_expert, CAP, limits).astype(jnp.int32)
    return (route_rows, limits)


def bias_vector(key):
    key_bias = jax.random.fold_in(key, 21)
    values = jnp.clip(0.3 * jax.random.normal(key_bias, (D,), jnp.float32), -1.5, 1.5)
    return values


def draw_routes(key, part):
    return route_table(key)[0]


def draw_capacity(key, part):
    return route_table(key)[1]


def draw_ln2_bias(key, part):
    return bias_vector(key)


def draw_w_router(key, part):
    key_router = jax.random.fold_in(key, 22)
    base = jax.random.normal(key_router, (D, EXPERTS), jnp.float32) * (0.5 / D ** 0.5)
    base = jnp.clip(base, -0.5, 0.5)
    hot_column = (jnp.arange(EXPERTS) == hot_of(key)).astype(jnp.float32)
    strength = 10.0
    extra = bias_vector(key)[:, None] * hot_column[None, :] * (strength / D)
    return (base + extra).astype(jnp.bfloat16)


def block_levels(rng, extent, shards, least, high):
    level, own = 1.0, jax.random.fold_in(rng, 6)
    for axis_at, blocks in shards:
        steps = jnp.exp(jax.random.uniform(jax.random.fold_in(own, axis_at), (blocks,), jnp.float32, least / len(shards), high / len(shards)))
        level = level * jnp.repeat(steps, extent[axis_at] // blocks).reshape([-1 if axis == axis_at else 1 for axis in range(len(extent))])
    return level


def centred(own_key, shape, width, most, pieces=(), kind=jnp.bfloat16):
    array = width * jax.random.normal(own_key, shape, jnp.float32)
    if pieces:
        array = array * block_levels(own_key, shape, pieces, -0.22, 0.18)
    return jnp.clip(array, -most, most).astype(kind)


def setup_inputs(seed: int = 0) -> dict:
    key_list = jax.random.split(jax.random.key(seed), 14)
    return {
        "tokens": centred(key_list[0], (TOKENS, D), 1.0, 6.0, ((0, 32),)),
        "routes": draw_routes(jax.random.fold_in(key_list[13], 71), 0),
        "capacity": draw_capacity(jax.random.fold_in(key_list[13], 71), 0),
        "ln1_gain": jnp.clip(1.0 + 0.1 * jax.random.normal(key_list[3], (D,), jnp.float32), 0.5, 1.5),
        "ln1_bias": centred(key_list[4], (D,), 0.3, 1.5, (), jnp.float32),
        "ln2_gain": jnp.clip(1.0 + 0.1 * jax.random.normal(key_list[5], (D,), jnp.float32), 0.5, 1.5),
        "ln2_bias": draw_ln2_bias(jax.random.fold_in(key_list[13], 71), 0),
        "w_qkv": centred(key_list[7], (D, 3 * D), D ** -0.5, 0.21875, ((0, 4),)),
        "w_proj": centred(key_list[8], (D, D), (D // 16) ** -0.5, 0.875, ((0, 4),)),
        "w_router": draw_w_router(jax.random.fold_in(key_list[13], 71), 0),
        "w_in": centred(key_list[10], (EXPERTS, D, FF), D ** -0.5, 0.21875, ((0, 8),)),
        "w_out": centred(key_list[11], (EXPERTS, FF, D), (max(4 * FF // (EXPERTS * EXPERTS), 1)) ** -0.5, 0.4375, ((0, 8),)),
        "cotangent": centred(key_list[12], (TOKENS, D), 1.0, 6.0, ((0, 32),)),
    }


PRECISE = lax.Precision.HIGHEST
NORM_EPS = 1e-06
LOSS_WEIGHT = 0.01

@jax.custom_vjp
def low(v):
    return lax.optimization_barrier(v.astype(jnp.bfloat16)).astype(jnp.float32)

@jax.custom_vjp
def low_back(v):
    return v

def low_keep(v):
    return (low(v), None)

def low_pass(kept, grad):
    return (grad,)

def back_keep(v):
    return (v, None)

def back_low(kept, grad):
    return (low(grad),)
low.defvjp(low_keep, low_pass)
low_back.defvjp(back_keep, back_low)

def layer_norm(values, norm_gain, norm_bias):
    row_mean = lax.optimization_barrier(jnp.mean(values, axis=-1, keepdims=True))
    centered = values - row_mean
    variance = lax.optimization_barrier(jnp.mean(centered * centered, axis=-1, keepdims=True))
    return centered * lax.rsqrt(variance + NORM_EPS) * norm_gain + norm_bias

def route_slots(route_rows, capacity, expert_count):
    labels = jnp.arange(expert_count, dtype=jnp.int32)
    first_hit = (route_rows[:, 0:1] == labels[None, :]).astype(jnp.int32)
    second_hit = (route_rows[:, 1:2] == labels[None, :]).astype(jnp.int32)
    before_first = jnp.cumsum(first_hit, axis=0) - first_hit
    before_second = jnp.cumsum(second_hit, axis=0) - second_hit + lax.optimization_barrier(jnp.sum(first_hit, axis=0, keepdims=True))
    slot_first = lax.optimization_barrier(jnp.sum(before_first * first_hit, axis=1))
    slot_second = lax.optimization_barrier(jnp.sum(before_second * second_hit, axis=1))
    limit_first = lax.optimization_barrier(jnp.sum(first_hit * capacity[None, :], axis=1))
    limit_second = lax.optimization_barrier(jnp.sum(second_hit * capacity[None, :], axis=1))
    slot_index = jnp.stack([slot_first, slot_second], axis=1)
    kept_mask = slot_index < jnp.stack([limit_first, limit_second], axis=1)
    return (slot_index, kept_mask, first_hit + second_hit)

def reference(tokens, routes, capacity, ln1_gain, ln1_bias, ln2_gain, ln2_bias, w_qkv, w_proj, w_router, w_in, w_out, cotangent):
    groups = TOKENS // TOK_DEV
    blocks = routes.reshape(groups, TOK_DEV, TOP)
    slot_index, kept_mask, route_hits = jax.vmap(lambda block_rows: route_slots(block_rows, capacity, EXPERTS))(blocks)
    group_ids = jnp.arange(groups, dtype=jnp.int32)[:, None, None]
    buffer_rows = EXPERTS * groups * CAP
    target = (blocks * groups + group_ids) * CAP + slot_index
    target = jnp.where(kept_mask, target, buffer_rows).reshape(TOKENS, TOP).astype(jnp.int32)
    kept_mask = kept_mask.reshape(TOKENS, TOP)
    token_ids = jnp.broadcast_to(jnp.arange(TOKENS, dtype=jnp.int32)[:, None], (TOKENS, TOP))
    table = jnp.full((buffer_rows,), TOKENS, jnp.int32).at[target.reshape(-1)].set(token_ids.reshape(-1), mode='drop')
    safe_target = jnp.minimum(target, buffer_rows - 1)
    counts = lax.optimization_barrier(jnp.sum(route_hits.reshape(TOKENS, EXPERTS), axis=0)).astype(jnp.float32)
    route_share = counts / (2.0 * TOKENS)
    score_scale = 1.0 / math.sqrt(HDIM)

    def attend(group_rows, qkv_weight):
        qkv_rows = low(low_back(jnp.dot(group_rows, qkv_weight, precision=PRECISE)))
        qkv_parts = qkv_rows.reshape(IMG_DEV, SEQ, 3, HEADS, HDIM)
        query_rows = qkv_parts[:, :, 0]
        key_rows = qkv_parts[:, :, 1]
        value_rows = qkv_parts[:, :, 2]
        scores = low_back(jnp.einsum('bqhd,bkhd->bhqk', query_rows, key_rows, precision=PRECISE) * score_scale)
        attention = low(jax.nn.softmax(scores, axis=-1))
        heads_mixed = jnp.einsum('bhqk,bkhd->bqhd', attention, value_rows, precision=PRECISE)
        return low(low_back(heads_mixed.reshape(TOK_DEV, D)))

    def expert_apply(inputs):
        expert_rows, weight_in, weight_out = inputs
        pre_act = low_back(jnp.dot(expert_rows, weight_in, precision=PRECISE))
        hidden = low(jax.nn.gelu(pre_act, approximate=False))
        return low(low_back(jnp.dot(hidden, weight_out, precision=PRECISE)))

    def forward(token_rows, gain_one, bias_one, gain_two, bias_two, qkv_weight, proj_weight, router_weight, weight_in, weight_out):
        first_normed = low(layer_norm(token_rows, gain_one, bias_one))
        heads_out = lax.map(jax.checkpoint(lambda group_rows: attend(group_rows, qkv_weight)), first_normed.reshape(groups, TOK_DEV, D)).reshape(TOKENS, D)
        attn_branch = low_back(jnp.dot(heads_out, proj_weight, precision=PRECISE))
        after_attention = token_rows + attn_branch
        mid_normed = low(layer_norm(after_attention, gain_two, bias_two))
        logits = low_back(jnp.dot(mid_normed, router_weight, precision=PRECISE))
        gate_probs = jax.nn.softmax(logits, axis=-1)
        padded = jnp.concatenate([mid_normed, jnp.zeros((1, D), jnp.float32)], axis=0)
        sent_rows = low_back(jnp.take(padded, table, axis=0))
        expert_made = lax.map(jax.checkpoint(expert_apply), (sent_rows.reshape(EXPERTS, groups * CAP, D), weight_in, weight_out)).reshape(buffer_rows, D)
        picked = jnp.take(expert_made, safe_target, axis=0)
        gates = jnp.take_along_axis(gate_probs, routes, axis=1)
        pair_weight = jnp.where(kept_mask, gates, 0.0)
        moe_branch = lax.optimization_barrier(jnp.sum(picked * pair_weight[..., None], axis=1))
        balance_loss = EXPERTS * jnp.sum(route_share * lax.optimization_barrier(jnp.mean(gate_probs, axis=0)))
        return (after_attention + moe_branch, balance_loss)
    floats = (tokens.astype(jnp.float32), ln1_gain, ln1_bias, ln2_gain, ln2_bias, w_qkv.astype(jnp.float32), w_proj.astype(jnp.float32), w_router.astype(jnp.float32), w_in.astype(jnp.float32), w_out.astype(jnp.float32))
    (layer_out, balance_loss), pull = jax.vjp(forward, *floats)
    grads = pull((cotangent.astype(jnp.float32), jnp.asarray(LOSS_WEIGHT, jnp.float32)))
    return (layer_out.astype(jnp.bfloat16), balance_loss, grads[0], grads[1], grads[2], grads[3], grads[4], grads[5], grads[6], grads[7], grads[8], grads[9])
```

```python
import functools
import math

import jax
import jax.numpy as jnp
from jax import lax
from jax.experimental import pallas as pl
from jax.experimental.pallas import tpu as pltpu
from jax.sharding import PartitionSpec as P

HEADS = 12
SEQ = 197
PAD_SEQ = 208
LANES = 128

NORM_EPS = 1e-06
LOSS_WEIGHT = 0.01
NEG = -1e30
VMEM_LIMIT = 56 * 1024 * 1024
BF = jnp.bfloat16
F32 = jnp.float32


def dot_nn(left, right):
    return lax.dot_general(left, right, (((1,), (0,)), ((), ())), preferred_element_type=F32)


def dot_nt(left, right):
    return lax.dot_general(left, right, (((1,), (1,)), ((), ())), preferred_element_type=F32)


def dot_tn(left, right):
    return lax.dot_general(left, right, (((0,), (0,)), ((), ())), preferred_element_type=F32)


def norm_rows(values):
    row_mean = jnp.mean(values, axis=-1, keepdims=True)
    centered = values - row_mean
    variance = jnp.mean(centered * centered, axis=-1, keepdims=True)
    inverse = lax.rsqrt(variance + NORM_EPS)
    return centered * inverse, inverse


def norm_back(grad_rows, normed, inverse, norm_gain):
    scaled = grad_rows * norm_gain
    return inverse * (
        scaled
        - jnp.mean(scaled, axis=-1, keepdims=True)
        - normed * jnp.mean(scaled * normed, axis=-1, keepdims=True)
    )


def attend_kernel(tok_ref, gain_ref, bias_ref, w_ref, first_ref, qkv_ref, heads_ref):
    width = tok_ref.shape[1]
    normed, _ = norm_rows(tok_ref[...].astype(F32))
    first = (normed * gain_ref[...] + bias_ref[...]).astype(BF)
    first_ref[...] = first
    for part in range(3):
        cols = slice(part * width, (part + 1) * width)
        qkv_ref[:, cols] = dot_nn(first, w_ref[:, cols]).astype(BF)
    rows = tok_ref.shape[0]
    lane = lax.broadcasted_iota(jnp.int32, (rows, LANES), 1)
    key_at = lax.broadcasted_iota(jnp.int32, (rows, rows), 1)
    scale = 1.0 / math.sqrt(width // HEADS)
    for pair in range(width // LANES):
        queries = qkv_ref[:, pair * LANES : (pair + 1) * LANES]
        keys = qkv_ref[:, width + pair * LANES : width + (pair + 1) * LANES]
        values = qkv_ref[:, 2 * width + pair * LANES : 2 * width + (pair + 1) * LANES]
        mixed = None
        for half in range(2):
            mine = (lane < LANES // 2) if half == 0 else (lane >= LANES // 2)
            zero = jnp.zeros_like(queries)
            scores = dot_nt(jnp.where(mine, queries, zero), keys) * scale
            scores = jnp.where(key_at < SEQ, scores, NEG)
            peak = jnp.max(scores, axis=-1, keepdims=True)
            weights = jnp.exp(scores - peak)
            total = jnp.sum(weights, axis=-1, keepdims=True)
            weights = (weights / total).astype(BF)
            term = dot_nn(weights, jnp.where(mine, values, zero))
            mixed = term if mixed is None else mixed + term
        heads_ref[:, pair * LANES : (pair + 1) * LANES] = mixed.astype(BF)


def attend(tok_pad, gain, bias, w_qkv, images):
    rows, width = tok_pad.shape
    whole = lambda i: (0, 0)
    block = lambda i: (i, 0)
    return pl.pallas_call(
        attend_kernel,
        grid=(images,),
        in_specs=[
            pl.BlockSpec((PAD_SEQ, width), block),
            pl.BlockSpec((1, width), whole),
            pl.BlockSpec((1, width), whole),
            pl.BlockSpec((width, 3 * width), whole),
        ],
        out_specs=[
            pl.BlockSpec((PAD_SEQ, width), block),
            pl.BlockSpec((PAD_SEQ, 3 * width), block),
            pl.BlockSpec((PAD_SEQ, width), block),
        ],
        out_shape=[
            jax.ShapeDtypeStruct((rows, width), BF),
            jax.ShapeDtypeStruct((rows, 3 * width), BF),
            jax.ShapeDtypeStruct((rows, width), BF),
        ],
        compiler_params=pltpu.CompilerParams(vmem_limit_bytes=VMEM_LIMIT),
        cost_estimate=pl.CostEstimate(
            flops=2 * rows * width * 3 * width + 4 * rows * PAD_SEQ * width,
            bytes_accessed=2 * (6 * rows * width + 3 * width * width),
            transcendentals=rows * PAD_SEQ * HEADS,
        ),
    )(tok_pad, gain.reshape(1, -1), bias.reshape(1, -1), w_qkv)


def attend_back_kernel(q_ref, k_ref, v_ref, g_ref, dq_ref, dk_ref, dv_ref, *, scale):
    rows, cols = q_ref.shape
    lane = lax.broadcasted_iota(jnp.int32, (rows, LANES), 1)
    key_at = lax.broadcasted_iota(jnp.int32, (rows, rows), 0)
    for pair in range(cols // LANES):
        at = slice(pair * LANES, (pair + 1) * LANES)
        queries, keys, values, grads = q_ref[:, at], k_ref[:, at], v_ref[:, at], g_ref[:, at]
        zero = jnp.zeros_like(queries)
        sums = None
        for half in range(2):
            mine = (lane < LANES // 2) if half == 0 else (lane >= LANES // 2)
            q_half = jnp.where(mine, queries, zero)
            g_half = jnp.where(mine, grads, zero)
            scores = dot_nt(keys, q_half) * scale
            scores = jnp.where(key_at < SEQ, scores, NEG)
            peak = jnp.max(scores, axis=0, keepdims=True)
            weights = jnp.exp(scores - peak)
            probs = weights / jnp.sum(weights, axis=0, keepdims=True)
            grad_attention = dot_nt(values, g_half)
            inner = jnp.sum(probs * grad_attention, axis=0, keepdims=True)
            grad_scores = (probs * (grad_attention - inner)).astype(BF)
            terms = (
                dot_tn(grad_scores, jnp.where(mine, keys, zero)),
                dot_nn(grad_scores, q_half),
                dot_nn(probs.astype(BF), g_half),
            )
            sums = terms if sums is None else tuple(a + b for a, b in zip(sums, terms))
        dq_ref[:, at] = (sums[0] * scale).astype(BF)
        dk_ref[:, at] = (sums[1] * scale).astype(BF)
        dv_ref[:, at] = sums[2].astype(BF)


def attend_back(qkv, grad_heads_out, images, group, groups):
    rows, width = grad_heads_out.shape
    cols = width // groups

    def at(part):
        return pl.BlockSpec((PAD_SEQ, cols), lambda i: (i, part * groups + group))

    out = pl.BlockSpec((PAD_SEQ, cols), lambda i: (i, 0))
    return pl.pallas_call(
        functools.partial(attend_back_kernel, scale=1.0 / math.sqrt(width // HEADS)),
        grid=(images,),
        in_specs=[at(0), at(1), at(2), at(0)],
        out_specs=[out] * 3,
        out_shape=[jax.ShapeDtypeStruct((rows, cols), BF)] * 3,
        compiler_params=pltpu.CompilerParams(vmem_limit_bytes=VMEM_LIMIT),
        cost_estimate=pl.CostEstimate(
            flops=10 * rows * PAD_SEQ * cols,
            bytes_accessed=2 * 7 * rows * cols,
            transcendentals=rows * PAD_SEQ * HEADS // groups,
        ),
    )(qkv, qkv, qkv, grad_heads_out)


def expert_kernel(
    me_ref, x_ref, c_ref, wr_ref, win_ref, wout_ref,
    hid_ref, gp_ref, gm_ref, mg_ref, rows_ref, gr_ref,
    made_ref, acc_ref, p_ref,
    *, experts, block,
):
    step = pl.program_id(0)
    last = pl.num_programs(0) - 1
    count = x_ref.shape[0] // block
    lane = lax.broadcasted_iota(jnp.int32, (block, LANES), 1)
    mine = lane == me_ref[0]

    @pl.when(step == 0)
    def _():
        for b in range(count):
            at = slice(b * block, (b + 1) * block)
            logits = jnp.where(lane < experts, dot_nn(x_ref[at, :], wr_ref[...]), NEG)
            top = jnp.max(logits, axis=-1, keepdims=True)
            weights = jnp.exp(logits - top)
            probs = weights / jnp.sum(weights, axis=-1, keepdims=True)
            p_ref[at, :] = probs
            gate = jnp.sum(jnp.where(mine, probs, 0.0), axis=-1, keepdims=True)
            gm_ref[at, :] = (gate * c_ref[at, :].astype(F32)).astype(BF)

    for b in range(count):
        at = slice(b * block, (b + 1) * block)
        pre = dot_nn(x_ref[at, :], win_ref[...])
        back = dot_nt(gm_ref[at, :], wout_ref[...])
        cdf = 0.5 * (1.0 + lax.erf(pre * (1.0 / math.sqrt(2.0))))
        density = jnp.exp(-0.5 * pre * pre) * (1.0 / math.sqrt(2.0 * math.pi))
        hidden = (pre * cdf).astype(BF)
        grad_pre = (back * (cdf + pre * density)).astype(BF)
        hid_ref[at, :] = hidden
        gp_ref[at, :] = grad_pre
        made = dot_nn(hidden, wout_ref[...])
        rows = dot_nt(grad_pre, win_ref[...])

        @pl.when(step == 0)
        def _():
            made_ref[at, :] = made
            acc_ref[at, :] = rows

        @pl.when(step > 0)
        def _():
            made_ref[at, :] += made
            acc_ref[at, :] += rows

    @pl.when(step == last)
    def _():
        total = None
        for b in range(count):
            at = slice(b * block, (b + 1) * block)
            probs = p_ref[at, :]
            gate = jnp.sum(jnp.where(mine, probs, 0.0), axis=-1, keepdims=True)
            made = made_ref[at, :]
            mg_ref[at, :] = (gate * made).astype(BF)
            gain = jnp.sum(c_ref[at, :].astype(F32) * made.astype(BF).astype(F32), axis=-1, keepdims=True)
            routed = (gain * gate * (jnp.where(mine, 1.0, 0.0) - probs)).astype(BF)
            rows_ref[at, :] = (acc_ref[at, :] + dot_nt(routed, wr_ref[...])).astype(BF)
            part = dot_tn(routed, x_ref[at, :])
            total = part if total is None else total + part
        gr_ref[...] = total


def run_expert(me, x, c, w_router, w_in, w_out, experts):
    rows, width = x.shape
    hidden = w_in.shape[1]
    tile = 256
    block = rows // 4
    whole = lambda j: (0, 0)
    col = lambda j: (0, j)
    row = lambda j: (j, 0)
    big = jax.ShapeDtypeStruct((rows, hidden), BF)
    small = jax.ShapeDtypeStruct((rows, width), BF)
    return pl.pallas_call(
        functools.partial(expert_kernel, experts=experts, block=block),
        grid=(hidden // tile,),
        in_specs=[
            pl.BlockSpec(memory_space=pltpu.SMEM),
            pl.BlockSpec((rows, width), whole),
            pl.BlockSpec((rows, width), whole),
            pl.BlockSpec((width, LANES), whole),
            pl.BlockSpec((width, tile), col),
            pl.BlockSpec((tile, width), row),
        ],
        out_specs=[
            pl.BlockSpec((rows, tile), col),
            pl.BlockSpec((rows, tile), col),
            pl.BlockSpec((rows, width), whole),
            pl.BlockSpec((rows, width), whole),
            pl.BlockSpec((rows, width), whole),
            pl.BlockSpec((LANES, width), whole),
        ],
        out_shape=[big, big, small, small, small, jax.ShapeDtypeStruct((LANES, width), F32)],
        scratch_shapes=[
            pltpu.VMEM((rows, width), F32),
            pltpu.VMEM((rows, width), F32),
            pltpu.VMEM((rows, LANES), F32),
        ],
        compiler_params=pltpu.CompilerParams(vmem_limit_bytes=VMEM_LIMIT),
        cost_estimate=pl.CostEstimate(
            flops=8 * rows * width * hidden,
            bytes_accessed=4 * (rows * hidden + width * hidden + 3 * rows * width),
            transcendentals=2 * rows * hidden,
        ),
    )(me, x, c, w_router, w_in, w_out)


def axis_bits(size):
    return [1 << b for b in range(size.bit_length() - 1)]


def exchange(value, axis, bit):
    size = lax.axis_size(axis)
    return lax.ppermute(value, axis, [(i, i ^ bit) for i in range(size)])


def gather_rows(block, axis):
    size = lax.axis_size(axis)
    me = lax.axis_index(axis)
    held = block[None]
    for bit in reversed(axis_bits(size)):
        got = exchange(held, axis, bit)
        upper = (me // bit) % 2
        both = jnp.where(upper == 0, jnp.stack([held, got]), jnp.stack([got, held]))
        held = jnp.moveaxis(both, 0, 1).reshape((-1,) + block.shape)
    return held.reshape((-1,) + block.shape[1:])


def scatter_rows(value, axis):
    size = lax.axis_size(axis)
    me = lax.axis_index(axis)
    held = value.reshape((size, value.shape[0] // size) + value.shape[1:])
    for bit in axis_bits(size):
        view = held.reshape((held.shape[0] // 2, 2) + held.shape[1:])
        mine = (me // bit) % 2
        away = lax.dynamic_index_in_dim(view, 1 - mine, 1, keepdims=False)
        keep = lax.dynamic_index_in_dim(view, mine, 1, keepdims=False)
        got = exchange(away.astype(BF), axis, bit)
        held = keep.astype(F32) + got.astype(F32)
    return held[0]


def sum_owners(value):
    owners = lax.axis_size("expert")
    rows, cols = value.shape
    parts = value.astype(BF).reshape(owners, rows // owners, cols)
    got = lax.all_to_all(parts, "expert", split_axis=0, concat_axis=0, tiled=True)
    total = jnp.sum(got.astype(F32), axis=0).astype(BF)
    spread = jnp.broadcast_to(total[None], got.shape)
    back = lax.all_to_all(spread, "expert", split_axis=0, concat_axis=0, tiled=True)
    return back.reshape(rows, cols).astype(F32)


def trade(rows):
    owners = lax.axis_size("expert")
    view = rows.reshape(owners, rows.shape[0] // owners, rows.shape[1])
    return lax.all_to_all(view, "expert", split_axis=0, concat_axis=0, tiled=True).reshape(rows.shape)


def body(
    tokens, routes, capacity, ln1_gain, ln1_bias, ln2_gain, ln2_bias,
    w_qkv, w_proj, w_router, w_in, w_out, cotangent,
):
    count, width = tokens.shape
    experts = capacity.shape[0]
    owners = lax.axis_size("expert")
    shards = lax.axis_size("shard")
    hidden = w_in.shape[2]
    images = count // SEQ
    padded = images * PAD_SEQ
    slot_count = 8 * ((2 * count + 8 * experts - 1) // (8 * experts))
    all_tokens = count * owners * shards
    me = lax.axis_index("expert").astype(jnp.int32).reshape(1)

    def pad_rows(values, fill=0):
        spread = values.reshape((images, SEQ) + values.shape[1:])
        room = [(0, 0), (0, PAD_SEQ - SEQ)] + [(0, 0)] * (values.ndim - 1)
        return jnp.pad(spread, room, constant_values=fill).reshape((padded,) + values.shape[1:])

    def cut_rows(values):
        spread = values.reshape((images, PAD_SEQ) + values.shape[1:])
        return spread[:, :SEQ].reshape((count,) + values.shape[1:])

    qkv_full = gather_rows(w_qkv, "shard")
    pack = jnp.concatenate([w_proj, jnp.pad(w_router, ((0, 0), (0, LANES - experts)))], axis=1)
    pack_full = gather_rows(pack, "shard")
    proj_full, router_full = pack_full[:, :width], pack_full[:, width:]

    labels = jnp.arange(experts, dtype=jnp.int32)[:, None]
    first, second = routes[:, 0][None, :], routes[:, 1][None, :]
    hit_first, hit_second = first == labels, second == labels
    hits = jnp.concatenate([hit_first, hit_second], axis=0).astype(BF)
    order = lax.broadcasted_iota(jnp.int32, (count, count), 0) < lax.broadcasted_iota(
        jnp.int32, (count, count), 1
    )
    before = dot_nn(hits, order.astype(BF))
    totals = jnp.sum(hits.astype(F32), axis=1, keepdims=True)
    before_first = before[:experts]
    before_second = before[experts:] + totals[:experts]
    limits = capacity[:, None].astype(F32)

    def slots(hit, ahead, choice):
        slot = jnp.sum(jnp.where(hit, ahead, 0.0), axis=0)
        limit = jnp.sum(jnp.where(hit, limits, 0.0), axis=0)
        kept = slot < limit
        slot = slot.astype(jnp.int32)
        return choice[0], slot, kept

    choices = [slots(hit_first, before_first, first), slots(hit_second, before_second, second)]
    head = 8 * ((slot_count + 15) // 16)
    sizes = (head, slot_count - head)

    def selector(chunk):
        size = sizes[chunk]
        at = lax.broadcasted_iota(jnp.int32, (experts * size, 1), 0)
        found = None
        for choice, slot, kept in choices:
            inside = slot - (0 if chunk == 0 else head)
            valid = kept & (inside >= 0) & (inside < size)
            where = pad_rows(jnp.where(valid, choice * size + inside, -1), -1)
            match = at == where[None, :]
            found = match if found is None else (found | match)
        return found.astype(BF)

    select = [selector(0), selector(1)]

    cot_pad = pad_rows(cotangent)
    cots = [trade(dot_nn(s, cot_pad).astype(BF)) for s in select]

    tok_pad = pad_rows(tokens)
    first_low, qkv_rows, heads_out = attend(tok_pad, ln1_gain, ln1_bias, qkv_full, images)
    token_rows = tok_pad.astype(F32)
    after_attention = token_rows + dot_nn(heads_out, proj_full)
    normed_two, inverse_two = norm_rows(after_attention)
    mid_low = (normed_two * ln2_gain + ln2_bias).astype(BF)

    mids = [trade(dot_nn(s, mid_low).astype(BF)) for s in select]
    done = [
        run_expert(me, mids[i], cots[i], router_full, w_in[0], w_out[0], experts) for i in range(2)
    ]
    backs = [trade(d[4]) for d in done]
    returned = [trade(d[3]) for d in done]
    grad_in_whole = dot_tn(mids[0], done[0][1]) + dot_tn(mids[1], done[1][1])
    grad_out_whole = dot_tn(done[0][0], done[0][2]) + dot_tn(done[1][0], done[1][2])
    grad_expert_in = lax.psum_scatter(
        grad_in_whole.astype(BF), "shard", scatter_dimension=1, tiled=True
    ).astype(F32)
    grad_expert_out = lax.psum_scatter(
        grad_out_whole.astype(BF), "shard", scatter_dimension=0, tiled=True
    ).astype(F32)

    logits = dot_nn(mid_low, router_full)[:, :experts]
    live = (lax.broadcasted_iota(jnp.int32, (padded, 1), 0) % PAD_SEQ) < SEQ
    gate_probs = jnp.where(live, jax.nn.softmax(logits, axis=-1), 0.0)
    counts = (totals[:experts] + totals[experts:])[:, 0]
    count_all, prob_all = lax.psum((counts, jnp.sum(gate_probs, axis=0)), ("expert", "shard"))
    route_share = count_all / (2.0 * all_tokens)
    balance_loss = experts * jnp.sum(route_share * prob_all / all_tokens)
    push = LOSS_WEIGHT * experts * route_share[None, :] / all_tokens
    grad_logits = gate_probs * (push - jnp.sum(gate_probs * push, axis=-1, keepdims=True))
    grad_logits = jnp.pad(grad_logits, ((0, 0), (0, LANES - experts))).astype(BF)
    grad_router = dot_tn(mid_low, grad_logits) + (done[0][5] + done[1][5]).T

    grad_mid = (
        dot_tn(select[0], backs[0]) + dot_tn(select[1], backs[1]) + dot_nt(grad_logits, router_full)
    )
    grad_gain_two = jnp.sum(grad_mid * normed_two, axis=0)
    grad_bias_two = jnp.sum(grad_mid, axis=0)
    grad_after = cot_pad.astype(F32) + norm_back(grad_mid, normed_two, inverse_two, ln2_gain)
    grad_heads = grad_after.astype(BF)
    grad_proj = dot_tn(heads_out, grad_heads)
    grad_heads_out = dot_nt(grad_heads, proj_full).astype(BF)

    mixed = cut_rows(
        after_attention + dot_tn(select[0], returned[0]) + dot_tn(select[1], returned[1])
    ).astype(BF)

    groups = 2
    cols = width // groups
    grad_first = None
    pieces = []
    for group in range(groups):
        grads = attend_back(qkv_rows, grad_heads_out, images, group, groups)
        for part in range(3):
            at = slice(part * width + group * cols, part * width + (group + 1) * cols)
            term = dot_nt(grads[part], qkv_full[:, at])
            grad_first = term if grad_first is None else grad_first + term
        pieces.append(jnp.concatenate([dot_tn(first_low, g) for g in grads], axis=1))
    normed_one, inverse_one = norm_rows(token_rows)
    grad_gain_one = jnp.sum(grad_first * normed_one, axis=0)
    grad_bias_one = jnp.sum(grad_first, axis=0)
    grad_tokens = cut_rows(grad_after + norm_back(grad_first, normed_one, inverse_one, ln1_gain))

    vectors = lax.psum(
        jnp.concatenate(
            [
                jnp.stack([grad_gain_one, grad_bias_one, grad_gain_two, grad_bias_two], axis=0),
                grad_router[:, :experts].T,
            ],
            axis=0,
        ),
        ("expert", "shard"),
    )
    own = width // shards
    vectors = lax.dynamic_slice_in_dim(vectors, lax.axis_index("shard") * own, own, axis=1)

    proj_total = sum_owners(scatter_rows(grad_proj, "shard"))
    totals_qkv = [sum_owners(scatter_rows(p, "shard")) for p in pieces]
    grad_qkv_weight = jnp.concatenate(
        [t[:, part * cols : (part + 1) * cols] for part in range(3) for t in totals_qkv], axis=1
    )
    return (
        mixed,
        balance_loss,
        grad_tokens,
        vectors[0],
        vectors[1],
        vectors[2],
        vectors[3],
        grad_qkv_weight,
        proj_total,
        vectors[4:].T,
        grad_expert_in[None],
        grad_expert_out[None],
    )


def solution(mesh):
    rows = P(("expert", "shard"), None)
    in_specs = (
        rows, rows, P(), P(), P(), P(), P(),
        P("shard", None), P("shard", None), P("shard", None),
        P("expert", None, None), P("expert", None, None), rows,
    )
    out_specs = (
        rows, P(), rows, P("shard"), P("shard"), P("shard"), P("shard"),
        P("shard", None), P("shard", None), P("shard", None),
        P("expert", None, "shard"), P("expert", "shard", None),
    )
    return jax.shard_map(body, mesh=mesh, in_specs=in_specs, out_specs=out_specs, check_vma=False)
```

```python
import functools
import math

import jax
import jax.numpy as jnp
from jax import lax
from jax.experimental import pallas as pl
from jax.experimental.pallas import tpu as pltpu
from jax.sharding import PartitionSpec as P

HEADS = 12
SEQ = 197
PAD_SEQ = 208
LANES = 128

NORM_EPS = 1e-06
LOSS_WEIGHT = 0.01
NEG = -1e30
VMEM_LIMIT = 56 * 1024 * 1024
BF = jnp.bfloat16
F32 = jnp.float32


def dot_nn(left, right):
    return lax.dot_general(left, right, (((1,), (0,)), ((), ())), preferred_element_type=F32)


def dot_nt(left, right):
    return lax.dot_general(left, right, (((1,), (1,)), ((), ())), preferred_element_type=F32)


def dot_tn(left, right):
    return lax.dot_general(left, right, (((0,), (0,)), ((), ())), preferred_element_type=F32)


def norm_rows(values):
    row_mean = jnp.mean(values, axis=-1, keepdims=True)
    centered = values - row_mean
    variance = jnp.mean(centered * centered, axis=-1, keepdims=True)
    inverse = lax.rsqrt(variance + NORM_EPS)
    return centered * inverse, inverse


def norm_back(grad_rows, normed, inverse, norm_gain):
    scaled = grad_rows * norm_gain
    return inverse * (
        scaled
        - jnp.mean(scaled, axis=-1, keepdims=True)
        - normed * jnp.mean(scaled * normed, axis=-1, keepdims=True)
    )


def attend_kernel(tok_ref, gain_ref, bias_ref, w_ref, first_ref, qkv_ref, heads_ref):
    width = tok_ref.shape[1]
    normed, _ = norm_rows(tok_ref[...].astype(F32))
    first = (normed * gain_ref[...] + bias_ref[...]).astype(BF)
    first_ref[...] = first
    for part in range(3):
        cols = slice(part * width, (part + 1) * width)
        qkv_ref[:, cols] = dot_nn(first, w_ref[:, cols]).astype(BF)
    rows = tok_ref.shape[0]
    lane = lax.broadcasted_iota(jnp.int32, (rows, LANES), 1)
    key_at = lax.broadcasted_iota(jnp.int32, (rows, rows), 1)
    scale = 1.0 / math.sqrt(width // HEADS)
    for pair in range(width // LANES):
        queries = qkv_ref[:, pair * LANES : (pair + 1) * LANES]
        keys = qkv_ref[:, width + pair * LANES : width + (pair + 1) * LANES]
        values = qkv_ref[:, 2 * width + pair * LANES : 2 * width + (pair + 1) * LANES]
        mixed = None
        for half in range(2):
            mine = (lane < LANES // 2) if half == 0 else (lane >= LANES // 2)
            zero = jnp.zeros_like(queries)
            scores = dot_nt(jnp.where(mine, queries, zero), keys) * scale
            scores = jnp.where(key_at < SEQ, scores, NEG)
            peak = jnp.max(scores, axis=-1, keepdims=True)
            weights = jnp.exp(scores - peak)
            total = jnp.sum(weights, axis=-1, keepdims=True)
            weights = (weights / total).astype(BF)
            term = dot_nn(weights, jnp.where(mine, values, zero))
            mixed = term if mixed is None else mixed + term
        heads_ref[:, pair * LANES : (pair + 1) * LANES] = mixed.astype(BF)


def attend(tok_pad, gain, bias, w_qkv, images):
    rows, width = tok_pad.shape
    whole = lambda i: (0, 0)
    block = lambda i: (i, 0)
    return pl.pallas_call(
        attend_kernel,
        grid=(images,),
        in_specs=[
            pl.BlockSpec((PAD_SEQ, width), block),
            pl.BlockSpec((1, width), whole),
            pl.BlockSpec((1, width), whole),
            pl.BlockSpec((width, 3 * width), whole),
        ],
        out_specs=[
            pl.BlockSpec((PAD_SEQ, width), block),
            pl.BlockSpec((PAD_SEQ, 3 * width), block),
            pl.BlockSpec((PAD_SEQ, width), block),
        ],
        out_shape=[
            jax.ShapeDtypeStruct((rows, width), BF),
            jax.ShapeDtypeStruct((rows, 3 * width), BF),
            jax.ShapeDtypeStruct((rows, width), BF),
        ],
        compiler_params=pltpu.CompilerParams(vmem_limit_bytes=VMEM_LIMIT),
        cost_estimate=pl.CostEstimate(
            flops=2 * rows * width * 3 * width + 4 * rows * PAD_SEQ * width,
            bytes_accessed=2 * (6 * rows * width + 3 * width * width),
            transcendentals=rows * PAD_SEQ * HEADS,
        ),
    )(tok_pad, gain.reshape(1, -1), bias.reshape(1, -1), w_qkv)


def attend_back_kernel(q_ref, k_ref, v_ref, g_ref, out_ref, *, scale):
    rows, cols = q_ref.shape
    lane = lax.broadcasted_iota(jnp.int32, (rows, LANES), 1)
    key_at = lax.broadcasted_iota(jnp.int32, (rows, rows), 0)
    for pair in range(cols // LANES):
        at = slice(pair * LANES, (pair + 1) * LANES)
        queries, keys, values, grads = q_ref[:, at], k_ref[:, at], v_ref[:, at], g_ref[:, at]
        zero = jnp.zeros_like(queries)
        sums = None
        for half in range(2):
            mine = (lane < LANES // 2) if half == 0 else (lane >= LANES // 2)
            q_half = jnp.where(mine, queries, zero)
            g_half = jnp.where(mine, grads, zero)
            scores = dot_nt(keys, q_half) * scale
            scores = jnp.where(key_at < SEQ, scores, NEG)
            peak = jnp.max(scores, axis=0, keepdims=True)
            weights = jnp.exp(scores - peak)
            probs = weights / jnp.sum(weights, axis=0, keepdims=True)
            grad_attention = dot_nt(values, g_half)
            inner = jnp.sum(probs * grad_attention, axis=0, keepdims=True)
            grad_scores = (probs * (grad_attention - inner)).astype(BF)
            terms = (
                dot_tn(grad_scores, jnp.where(mine, keys, zero)),
                dot_nn(grad_scores, q_half),
                dot_nn(probs.astype(BF), g_half),
            )
            sums = terms if sums is None else tuple(a + b for a, b in zip(sums, terms))
        for part, value in enumerate((sums[0] * scale, sums[1] * scale, sums[2])):
            out_ref[:, part * cols + pair * LANES : part * cols + (pair + 1) * LANES] = (
                value.astype(BF)
            )


def attend_back(qkv, grad_heads_out, images, start, cols):
    rows, width = grad_heads_out.shape
    first, step = start // cols, width // cols
    at = lambda part: pl.BlockSpec((PAD_SEQ, cols), lambda i: (i, part * step + first))
    return pl.pallas_call(
        functools.partial(attend_back_kernel, scale=1.0 / math.sqrt(width // HEADS)),
        grid=(images,),
        in_specs=[at(0), at(1), at(2), at(0)],
        out_specs=pl.BlockSpec((PAD_SEQ, 3 * cols), lambda i: (i, 0)),
        out_shape=jax.ShapeDtypeStruct((rows, 3 * cols), BF),
        compiler_params=pltpu.CompilerParams(vmem_limit_bytes=VMEM_LIMIT),
        cost_estimate=pl.CostEstimate(
            flops=20 * rows * PAD_SEQ * cols,
            bytes_accessed=2 * 7 * rows * cols,
            transcendentals=rows * PAD_SEQ * cols // 64,
        ),
    )(qkv, qkv, qkv, grad_heads_out)


def expert_kernel(
    me_ref, x_ref, c_ref, wr_ref, win_ref, wout_ref, win_rows_ref, wout_cols_ref,
    hid_ref, gp_ref, gm_ref, mg_ref, rows_ref, gr_ref,
    hid_all, gp_all, p_ref, gain_ref, routed_ref,
    *, experts, up_steps, down_steps,
):
    step = pl.program_id(0)
    rows = x_ref.shape[0]
    tile = win_ref.shape[1]
    piece = win_rows_ref.shape[0]
    lane = lax.broadcasted_iota(jnp.int32, (rows, LANES), 1)
    mine = lane == me_ref[0]

    def gate():
        return jnp.sum(jnp.where(mine, p_ref[...], 0.0), axis=-1, keepdims=True)

    @pl.when(step == 0)
    def _():
        logits = jnp.where(lane < experts, dot_nn(x_ref[...], wr_ref[...]), NEG)
        top = jnp.max(logits, axis=-1, keepdims=True)
        weights = jnp.exp(logits - top)
        p_ref[...] = weights / jnp.sum(weights, axis=-1, keepdims=True)
        gm_ref[...] = (gate() * c_ref[...].astype(F32)).astype(BF)

    @pl.when(step < up_steps)
    def _():
        col = pl.ds(pl.multiple_of(step * tile, tile), tile)
        pre = dot_nn(x_ref[...], win_ref[...])
        back = dot_nt(gm_ref[...], wout_ref[...])
        cdf = 0.5 * (1.0 + lax.erf(pre * (1.0 / math.sqrt(2.0))))
        density = jnp.exp(-0.5 * pre * pre) * (1.0 / math.sqrt(2.0 * math.pi))
        hidden = (pre * cdf).astype(BF)
        grad_pre = (back * (cdf + pre * density)).astype(BF)
        hid_ref[...] = hidden
        gp_ref[...] = grad_pre
        hid_all[:, col] = hidden
        gp_all[:, col] = grad_pre

    @pl.when((step >= up_steps) & (step < up_steps + down_steps))
    def _():
        part = step - up_steps
        col = pl.ds(pl.multiple_of(part * piece, piece), piece)
        made = dot_nn(hid_all[...], wout_cols_ref[...])
        mg_ref[...] = (gate() * made).astype(BF)
        gain = c_ref[:, col].astype(F32) * made.astype(BF).astype(F32)
        gain = jnp.broadcast_to(jnp.sum(gain, axis=-1, keepdims=True), (rows, LANES))
        gain_ref[...] = jnp.where(part == 0, gain, gain_ref[...] + gain)

    @pl.when(step == up_steps + down_steps)
    def _():
        probs = p_ref[...]
        routed = gain_ref[...] * gate() * (jnp.where(mine, 1.0, 0.0) - probs)
        routed_ref[...] = routed.astype(BF)
        gr_ref[...] = dot_tn(routed_ref[...], x_ref[...])

    @pl.when(step >= up_steps + down_steps)
    def _():
        part = step - up_steps - down_steps
        router = wr_ref[pl.ds(pl.multiple_of(part * piece, piece), piece), :]
        back = dot_nt(gp_all[...], win_rows_ref[...]) + dot_nt(routed_ref[...], router)
        rows_ref[...] = back.astype(BF)


def run_expert(me, x, c, w_router, w_in, w_out, experts):
    rows, width = x.shape
    hidden = w_in.shape[1]
    tile, piece = 512, 256
    up_steps, down_steps = hidden // tile, width // piece
    whole = lambda j: (0, 0)
    up = lambda j: jnp.minimum(j, up_steps - 1)
    made = lambda j: jnp.clip(j - up_steps, 0, down_steps - 1)
    back = lambda j: jnp.clip(j - up_steps - down_steps, 0, down_steps - 1)
    big = jax.ShapeDtypeStruct((rows, hidden), BF)
    small = jax.ShapeDtypeStruct((rows, width), BF)
    return pl.pallas_call(
        functools.partial(
            expert_kernel, experts=experts, up_steps=up_steps, down_steps=down_steps
        ),
        grid=(up_steps + 2 * down_steps,),
        in_specs=[
            pl.BlockSpec(memory_space=pltpu.SMEM),
            pl.BlockSpec((rows, width), whole),
            pl.BlockSpec((rows, width), whole),
            pl.BlockSpec((width, LANES), whole),
            pl.BlockSpec((width, tile), lambda j: (0, up(j))),
            pl.BlockSpec((tile, width), lambda j: (up(j), 0)),
            pl.BlockSpec((piece, hidden), lambda j: (back(j), 0)),
            pl.BlockSpec((hidden, piece), lambda j: (0, made(j))),
        ],
        out_specs=[
            pl.BlockSpec((rows, tile), lambda j: (0, up(j))),
            pl.BlockSpec((rows, tile), lambda j: (0, up(j))),
            pl.BlockSpec((rows, width), whole),
            pl.BlockSpec((rows, piece), lambda j: (0, made(j))),
            pl.BlockSpec((rows, piece), lambda j: (0, back(j))),
            pl.BlockSpec((LANES, width), whole),
        ],
        out_shape=[big, big, small, small, small, jax.ShapeDtypeStruct((LANES, width), F32)],
        scratch_shapes=[
            pltpu.VMEM((rows, hidden), BF),
            pltpu.VMEM((rows, hidden), BF),
            pltpu.VMEM((rows, LANES), F32),
            pltpu.VMEM((rows, LANES), F32),
            pltpu.VMEM((rows, LANES), BF),
        ],
        compiler_params=pltpu.CompilerParams(vmem_limit_bytes=VMEM_LIMIT),
        cost_estimate=pl.CostEstimate(
            flops=16 * rows * width * hidden,
            bytes_accessed=4 * (rows * hidden + 2 * width * hidden + 3 * rows * width),
            transcendentals=2 * rows * hidden,
        ),
    )(me, x, c, w_router, w_in, w_out, w_in, w_out)


def weight_grad_kernel(left_a, left_b, right_a, right_b, out_ref):
    total = dot_tn(left_a[...], right_a[...]) + dot_tn(left_b[...], right_b[...])
    out_ref[...] = total.astype(BF)


def weight_grad(lefts, rights, tile_left):
    tile = 512
    wide = lefts[0].shape[1] if tile_left else rights[0].shape[1]
    held = lambda a: pl.BlockSpec(a.shape, lambda j: (0, 0))
    tiled = lambda a: pl.BlockSpec((a.shape[0], tile), lambda j: (0, j))
    rows, cols = lefts[0].shape[1], rights[0].shape[1]
    flops = 2 * rows * cols * (lefts[0].shape[0] + lefts[1].shape[0])
    return pl.pallas_call(
        weight_grad_kernel,
        grid=(wide // tile,),
        in_specs=[(tiled if tile_left else held)(a) for a in lefts]
        + [(held if tile_left else tiled)(a) for a in rights],
        out_specs=pl.BlockSpec((tile, cols), lambda j: (j, 0))
        if tile_left
        else pl.BlockSpec((rows, tile), lambda j: (0, j)),
        out_shape=jax.ShapeDtypeStruct((rows, cols), BF),
        compiler_params=pltpu.CompilerParams(vmem_limit_bytes=VMEM_LIMIT),
        cost_estimate=pl.CostEstimate(
            flops=2 * flops, bytes_accessed=4 * rows * cols, transcendentals=0
        ),
    )(*lefts, *rights)


def axis_bits(size):
    return [1 << b for b in range(size.bit_length() - 1)]


def exchange(value, axis, bit):
    size = lax.axis_size(axis)
    return lax.ppermute(value, axis, [(i, i ^ bit) for i in range(size)])


def bit_of(axis, bit):
    return (lax.axis_index(axis) // bit) % 2


def add_everywhere(value):
    for axis in ("shard", "expert"):
        for bit in axis_bits(lax.axis_size(axis)):
            value = value + exchange(value, axis, bit)
    return value


def in_order(axis, bit, held, got):
    return jnp.where(bit_of(axis, bit) == 0, jnp.stack([held, got]), jnp.stack([got, held]))


def gather_rows(block, axis):
    held = block[None]
    for bit in reversed(axis_bits(lax.axis_size(axis))):
        both = in_order(axis, bit, held, exchange(held, axis, bit))
        held = jnp.moveaxis(both, 0, 1).reshape((-1,) + block.shape)
    return held.reshape((-1,) + block.shape[1:])


def split_columns(values):
    shards = lax.axis_size("shard")
    rows, cols = values.shape
    view = values.reshape(rows, shards // 2, 2, cols // shards)
    mine = bit_of("shard", 1)
    pick = lambda at: lax.dynamic_index_in_dim(view, at, 2, keepdims=False).reshape(rows, cols // 2)
    return pick(1 - mine), pick(mine)


def reduce_rows(away, keep):
    shards, owners = lax.axis_size("shard"), lax.axis_size("expert")
    cols = keep.shape[1]
    held = keep.astype(F32) + exchange(away.astype(BF), "shard", 1).astype(F32)
    held = held.reshape(shards // 2, -1, cols)
    halvings = [("shard", bit) for bit in axis_bits(shards)[1:]]
    for axis, bit in halvings:
        view = held.reshape((-1, 2) + held.shape[1:])
        mine = bit_of(axis, bit)
        send = lax.dynamic_index_in_dim(view, 1 - mine, 1, keepdims=False).astype(BF)
        stay = lax.dynamic_index_in_dim(view, mine, 1, keepdims=False)
        held = stay + exchange(send, axis, bit).astype(F32)
    held = held[0]
    for bit in axis_bits(owners):
        view = held.reshape(2, -1, cols)
        mine = bit_of("expert", bit)
        send = lax.dynamic_index_in_dim(view, 1 - mine, 0, keepdims=False).astype(BF)
        stay = lax.dynamic_index_in_dim(view, mine, 0, keepdims=False)
        held = stay + exchange(send, "expert", bit).astype(F32)
    held = held.astype(BF)
    for bit in reversed(axis_bits(owners)):
        held = in_order("expert", bit, held, exchange(held, "expert", bit)).reshape(-1, cols)
    return held.astype(F32)


def trade(view):
    return lax.all_to_all(view, "expert", split_axis=0, concat_axis=0, tiled=True)


def after(value, *others):
    return lax.optimization_barrier((value,) + others)[0]


def body(
    tokens, routes, capacity, ln1_gain, ln1_bias, ln2_gain, ln2_bias,
    w_qkv, w_proj, w_router, w_in, w_out, cotangent,
):
    count, width = tokens.shape
    experts = capacity.shape[0]
    owners = lax.axis_size("expert")
    shards = lax.axis_size("shard")
    images = count // SEQ
    padded = images * PAD_SEQ
    slot_count = 8 * ((2 * count + 8 * experts - 1) // (8 * experts))
    all_tokens = count * owners * shards
    me = lax.axis_index("expert").astype(jnp.int32).reshape(1)

    def pad_rows(values, fill=0):
        spread = values.reshape((images, SEQ) + values.shape[1:])
        room = [(0, 0), (0, PAD_SEQ - SEQ)] + [(0, 0)] * (values.ndim - 1)
        return jnp.pad(spread, room, constant_values=fill).reshape((padded,) + values.shape[1:])

    def cut_rows(values):
        spread = values.reshape((images, PAD_SEQ) + values.shape[1:])
        return spread[:, :SEQ].reshape((count,) + values.shape[1:])

    qkv_full = gather_rows(w_qkv, "shard")
    pack = jnp.concatenate([w_proj, jnp.pad(w_router, ((0, 0), (0, LANES - experts)))], axis=1)
    pack_full = gather_rows(pack, "shard")
    proj_full, router_full = pack_full[:, :width], pack_full[:, width:]

    labels = jnp.arange(experts, dtype=jnp.int32)[:, None]
    first, second = routes[:, 0][None, :], routes[:, 1][None, :]
    hit_first, hit_second = first == labels, second == labels
    hits = jnp.concatenate([hit_first, hit_second], axis=0).astype(BF)
    order = lax.broadcasted_iota(jnp.int32, (count, count), 0) < lax.broadcasted_iota(
        jnp.int32, (count, count), 1
    )
    before = dot_nn(hits, order.astype(BF))
    totals = jnp.sum(hits.astype(F32), axis=1, keepdims=True)
    before_first = before[:experts]
    before_second = before[experts:] + totals[:experts]
    limits = capacity[:, None].astype(F32)

    def slots(hit, ahead, choice):
        slot = jnp.sum(jnp.where(hit, ahead, 0.0), axis=0)
        limit = jnp.sum(jnp.where(hit, limits, 0.0), axis=0)
        kept = slot < limit
        slot = slot.astype(jnp.int32)
        return choice[0], slot, kept

    choices = [slots(hit_first, before_first, first), slots(hit_second, before_second, second)]
    head = 8 * ((slot_count + 15) // 16)
    spans = ((0, head), (head, slot_count - head))

    def selector(start, size):
        at = lax.broadcasted_iota(jnp.int32, (experts * size, 1), 0)
        found = None
        for choice, slot, kept in choices:
            inside = slot - start
            valid = kept & (inside >= 0) & (inside < size)
            where = pad_rows(jnp.where(valid, choice * size + inside, -1), -1)
            match = at == where[None, :]
            found = match if found is None else (found | match)
        return found.astype(BF)

    def send(select, rows):
        return dot_nn(select, rows).astype(BF).reshape(experts, -1, width)

    select_all = selector(0, slot_count)
    select = [selector(start, size) for start, size in spans]
    cot_pad = pad_rows(cotangent)
    cot_rows = trade(send(select_all, cot_pad))

    counts = (totals[:experts] + totals[experts:]).reshape(1, experts)
    counts = add_everywhere(jnp.pad(counts, ((0, 0), (0, LANES - experts))))[:, :experts]
    route_share = counts / (2.0 * all_tokens)

    tok_pad = pad_rows(tokens)
    first_low, qkv_rows, heads_out = attend(tok_pad, ln1_gain, ln1_bias, qkv_full, images)
    token_rows = tok_pad.astype(F32)
    after_attention = token_rows + dot_nn(heads_out, proj_full)
    normed_two, inverse_two = norm_rows(after_attention)
    mid_low = (normed_two * ln2_gain + ln2_bias).astype(BF)

    arrived = []
    last = cot_rows
    for pick in select:
        arrived.append(trade(after(send(pick, mid_low), last)))
        last = arrived[-1]
    made = [
        run_expert(
            me,
            arrived[i].reshape(-1, width),
            cot_rows[:, start : start + size].reshape(-1, width),
            router_full, w_in[0], w_out[0], experts,
        )
        for i, (start, size) in enumerate(spans)
    ]
    hidden, grad_pre, grad_made, gated, grad_rows, router_parts = zip(*made)
    grad_rows = [g.reshape(experts, -1, width) for g in grad_rows]
    backs = [trade(after(grad_rows[0], last))]
    backs.append(trade(after(grad_rows[1], backs[0])))
    gated = jnp.concatenate([g.reshape(experts, -1, width) for g in gated], axis=1)
    returned = trade(after(gated, backs[1])).reshape(-1, width)

    mids = [a.reshape(-1, width) for a in arrived]
    mids[0] = after(mids[0], backs[0])
    grad_in_whole = weight_grad(mids, grad_pre, False)
    grad_expert_in = lax.psum_scatter(
        grad_in_whole, "shard", scatter_dimension=1, tiled=True
    ).astype(F32)
    hidden = [after(hidden[0], grad_in_whole), hidden[1]]
    grad_out_whole = weight_grad(hidden, grad_made, True)
    grad_expert_out = lax.psum_scatter(
        grad_out_whole, "shard", scatter_dimension=0, tiled=True
    ).astype(F32)

    logits = dot_nn(mid_low, router_full)[:, :experts]
    live = (lax.broadcasted_iota(jnp.int32, (padded, 1), 0) % PAD_SEQ) < SEQ
    gate_probs = jnp.where(live, jax.nn.softmax(logits, axis=-1), 0.0)
    push = LOSS_WEIGHT * experts * route_share / all_tokens
    grad_logits = gate_probs * (push - jnp.sum(gate_probs * push, axis=-1, keepdims=True))
    grad_logits = jnp.pad(grad_logits, ((0, 0), (0, LANES - experts))).astype(BF)
    grad_router = dot_tn(grad_logits, mid_low) + router_parts[0] + router_parts[1]

    grad_mid = (
        dot_tn(select[0], backs[0].reshape(-1, width))
        + dot_tn(select[1], backs[1].reshape(-1, width))
        + dot_nt(grad_logits, router_full)
    )
    grad_gain_two = jnp.sum(grad_mid * normed_two, axis=0)
    grad_bias_two = jnp.sum(grad_mid, axis=0)
    grad_after = cot_pad.astype(F32) + norm_back(grad_mid, normed_two, inverse_two, ln2_gain)
    grad_heads = grad_after.astype(BF)
    grad_heads_out = dot_nt(grad_heads, proj_full).astype(BF)
    mixed = cut_rows(after_attention + dot_tn(select_all, returned)).astype(BF)

    heads_split = split_columns(heads_out)
    first_split = split_columns(first_low)
    payload = [[dot_tn(part, grad_heads)] for part in heads_split]
    starts, cols = (0, width // 2), width // 2
    grad_first = None
    reduced = []
    for start in starts:
        grads = attend_back(qkv_rows, grad_heads_out, images, start, cols)
        weights = jnp.concatenate(
            [qkv_full[:, p * width + start : p * width + start + cols] for p in range(3)], axis=1
        )
        term = dot_nt(grads, weights)
        grad_first = term if grad_first is None else grad_first + term
        for at, part in enumerate(first_split):
            payload[at].append(dot_tn(part, grads))
        reduced.append(reduce_rows(*[jnp.concatenate(p, axis=1) for p in payload]))
        payload = [[], []]
    normed_one, inverse_one = norm_rows(token_rows)
    grad_gain_one = jnp.sum(grad_first * normed_one, axis=0)
    grad_bias_one = jnp.sum(grad_first, axis=0)
    grad_tokens = cut_rows(grad_after + norm_back(grad_first, normed_one, inverse_one, ln1_gain))

    prob_sum = jnp.pad(jnp.sum(gate_probs, axis=0), (0, width - experts))
    vectors = jnp.stack(
        [grad_gain_one, grad_bias_one, grad_gain_two, grad_bias_two, prob_sum], axis=0
    )
    vectors = add_everywhere(jnp.concatenate([vectors, grad_router[:experts]], axis=0))
    balance_loss = experts * jnp.sum(route_share[0] * vectors[4, :experts] / all_tokens)
    own = width // shards
    vectors = lax.dynamic_slice_in_dim(vectors, lax.axis_index("shard") * own, own, axis=1)

    proj_total = reduced[0][:, :width]
    halves = (reduced[0][:, width:], reduced[1])
    grad_qkv_weight = jnp.concatenate(
        [t[:, part * cols : (part + 1) * cols] for part in range(3) for t in halves], axis=1
    )
    return (
        mixed,
        balance_loss,
        grad_tokens,
        vectors[0],
        vectors[1],
        vectors[2],
        vectors[3],
        grad_qkv_weight,
        proj_total,
        vectors[5:].T,
        grad_expert_in[None],
        grad_expert_out[None],
    )


def solution(mesh):
    rows = P(("expert", "shard"), None)
    in_specs = (
        rows, rows, P(), P(), P(), P(), P(),
        P("shard", None), P("shard", None), P("shard", None),
        P("expert", None, None), P("expert", None, None), rows,
    )
    out_specs = (
        rows, P(), rows, P("shard"), P("shard"), P("shard"), P("shard"),
        P("shard", None), P("shard", None), P("shard", None),
        P("expert", None, "shard"), P("expert", "shard", None),
    )
    return jax.shard_map(body, mesh=mesh, in_specs=in_specs, out_specs=out_specs, check_vma=False)
```

```python
import functools
import math

import jax
import jax.numpy as jnp
from jax import lax
from jax.experimental import pallas as pl
from jax.experimental.pallas import tpu as pltpu
from jax.sharding import PartitionSpec as P

HEADS = 12
SEQ = 197
PAD_SEQ = 208
LANES = 128

NORM_EPS = 1e-06
LOSS_WEIGHT = 0.01
NEG = -1e30
COUNT_BASE = 128
VMEM_LIMIT = 56 * 1024 * 1024
BF = jnp.bfloat16
F32 = jnp.float32


def dot_nn(left, right):
    return lax.dot_general(left, right, (((1,), (0,)), ((), ())), preferred_element_type=F32)


def dot_nt(left, right):
    return lax.dot_general(left, right, (((1,), (1,)), ((), ())), preferred_element_type=F32)


def dot_tn(left, right):
    return lax.dot_general(left, right, (((0,), (0,)), ((), ())), preferred_element_type=F32)


def norm_rows(values):
    row_mean = jnp.mean(values, axis=-1, keepdims=True)
    centered = values - row_mean
    variance = jnp.mean(centered * centered, axis=-1, keepdims=True)
    inverse = lax.rsqrt(variance + NORM_EPS)
    return centered * inverse, inverse


def norm_back(grad_rows, normed, inverse, norm_gain):
    scaled = grad_rows * norm_gain
    return inverse * (
        scaled
        - jnp.mean(scaled, axis=-1, keepdims=True)
        - normed * jnp.mean(scaled * normed, axis=-1, keepdims=True)
    )


def attend_kernel(tok_ref, gain_ref, bias_ref, *refs, shards):
    pieces, refs = refs[:shards], refs[shards:]
    first_ref, qkv_ref, heads_ref, full_ref, w_ref, sems = refs
    step = pl.program_id(0)
    width = tok_ref.shape[1]
    own = width // shards
    me = lax.axis_index("shard")

    def place(k):
        at = 0
        for bit in axis_bits(shards):
            mine = lax.rem(me // bit, 2)
            at = at + bit * (1 - mine if k & bit else mine)
        rows = pl.ds(pl.multiple_of(at * own, own), own)
        return pltpu.make_async_copy(pieces[k], w_ref.at[rows, :], sems.at[k])

    whole_copy = pltpu.make_async_copy(w_ref, full_ref, sems.at[shards])

    @pl.when(step == 0)
    def _():
        for k in range(shards):
            place(k).start()

    normed, _ = norm_rows(tok_ref[...].astype(F32))
    first = (normed * gain_ref[...] + bias_ref[...]).astype(BF)
    first_ref[...] = first

    @pl.when(step == 0)
    def _():
        for k in range(shards):
            place(k).wait()
        whole_copy.start()

    for part in range(3):
        cols = slice(part * width, (part + 1) * width)
        qkv_ref[:, cols] = dot_nn(first, w_ref[:, cols]).astype(BF)
    rows = tok_ref.shape[0]
    lane = lax.broadcasted_iota(jnp.int32, (rows, LANES), 1)
    key_at = lax.broadcasted_iota(jnp.int32, (rows, rows), 1)
    scale = 1.0 / math.sqrt(width // HEADS)
    for pair in range(width // LANES):
        queries = qkv_ref[:, pair * LANES : (pair + 1) * LANES]
        keys = qkv_ref[:, width + pair * LANES : width + (pair + 1) * LANES]
        values = qkv_ref[:, 2 * width + pair * LANES : 2 * width + (pair + 1) * LANES]
        mixed = None
        for half in range(2):
            mine = (lane < LANES // 2) if half == 0 else (lane >= LANES // 2)
            zero = jnp.zeros_like(queries)
            scores = dot_nt(jnp.where(mine, queries, zero), keys) * scale
            scores = jnp.where(key_at < SEQ, scores, NEG)
            peak = jnp.max(scores, axis=-1, keepdims=True)
            weights = jnp.exp(scores - peak)
            total = jnp.sum(weights, axis=-1, keepdims=True)
            weights = (weights / total).astype(BF)
            term = dot_nn(weights, jnp.where(mine, values, zero))
            mixed = term if mixed is None else mixed + term
        heads_ref[:, pair * LANES : (pair + 1) * LANES] = mixed.astype(BF)

    @pl.when(step == pl.num_programs(0) - 1)
    def _():
        whole_copy.wait()


def attend(tok_pad, gain, bias, pieces, images):
    rows, width = tok_pad.shape
    shards = len(pieces)
    own, cols = pieces[0].shape
    whole = lambda i: (0, 0)
    block = lambda i: (i, 0)
    return pl.pallas_call(
        functools.partial(attend_kernel, shards=shards),
        grid=(images,),
        in_specs=[
            pl.BlockSpec((PAD_SEQ, width), block),
            pl.BlockSpec((1, width), whole),
            pl.BlockSpec((1, width), whole),
        ]
        + [pl.BlockSpec(memory_space=pl.ANY)] * shards,
        out_specs=[
            pl.BlockSpec((PAD_SEQ, width), block),
            pl.BlockSpec((PAD_SEQ, 3 * width), block),
            pl.BlockSpec((PAD_SEQ, width), block),
            pl.BlockSpec(memory_space=pl.ANY),
        ],
        out_shape=[
            jax.ShapeDtypeStruct((rows, width), BF),
            jax.ShapeDtypeStruct((rows, 3 * width), BF),
            jax.ShapeDtypeStruct((rows, width), BF),
            jax.ShapeDtypeStruct((shards * own, cols), BF),
        ],
        scratch_shapes=[
            pltpu.VMEM((shards * own, cols), BF),
            pltpu.SemaphoreType.DMA((shards + 1,)),
        ],
        compiler_params=pltpu.CompilerParams(vmem_limit_bytes=VMEM_LIMIT),
        cost_estimate=pl.CostEstimate(
            flops=rows * width * width, bytes_accessed=rows * width, transcendentals=0
        ),
    )(tok_pad, gain.reshape(1, -1), bias.reshape(1, -1), *pieces)


def heads_back(q_ref, k_ref, v_ref, g_ref, out_ref, at_rows, scale):
    rows, cols = q_ref.shape
    lane = lax.broadcasted_iota(jnp.int32, (rows, LANES), 1)
    key_at = lax.broadcasted_iota(jnp.int32, (rows, rows), 0)
    for pair in range(cols // LANES):
        at = slice(pair * LANES, (pair + 1) * LANES)
        queries, keys, values, grads = q_ref[:, at], k_ref[:, at], v_ref[:, at], g_ref[:, at]
        zero = jnp.zeros_like(queries)
        sums = None
        for half in range(2):
            mine = (lane < LANES // 2) if half == 0 else (lane >= LANES // 2)
            q_half = jnp.where(mine, queries, zero)
            g_half = jnp.where(mine, grads, zero)
            scores = dot_nt(keys, q_half) * scale
            scores = jnp.where(key_at < SEQ, scores, NEG)
            peak = jnp.max(scores, axis=0, keepdims=True)
            weights = jnp.exp(scores - peak)
            probs = weights / jnp.sum(weights, axis=0, keepdims=True)
            grad_attention = dot_nt(values, g_half)
            inner = jnp.sum(probs * grad_attention, axis=0, keepdims=True)
            grad_scores = (probs * (grad_attention - inner)).astype(BF)
            terms = (
                dot_tn(grad_scores, jnp.where(mine, keys, zero)),
                dot_nn(grad_scores, q_half),
                dot_nn(probs.astype(BF), g_half),
            )
            sums = terms if sums is None else tuple(a + b for a, b in zip(sums, terms))
        for part, value in enumerate((sums[0] * scale, sums[1] * scale, sums[2])):
            start = part * cols + pair * LANES
            out_ref[at_rows, start : start + LANES] = value.astype(BF)


def attend_back_kernel(
    core_ref, q_ref, k_ref, v_ref, g_ref, wq_ref, wk_ref, wv_ref, first_ref, *refs, scale, final
):
    step = pl.program_id(0)
    rows, cols = q_ref.shape
    at_rows = pl.ds(pl.multiple_of(step * rows, rows), rows)
    if final:
        before_ref, tok_ref, after_ref, gain_ref, vec_ref = refs[:5]
        out_ref, away_ref, keep_ref, grads_ref, whole_ref, sums_ref = refs[5:]
    else:
        heads_ref, low_ref, out_ref, away_ref, keep_ref, grads_ref, whole_ref = refs
    heads_back(q_ref, k_ref, v_ref, g_ref, grads_ref, at_rows, scale)
    grad_first = None
    for part, w_ref in enumerate((wq_ref, wk_ref, wv_ref)):
        term = dot_nt(grads_ref[at_rows, part * cols : (part + 1) * cols], w_ref[...])
        grad_first = term if grad_first is None else grad_first + term
    if final:
        grad_first = grad_first + before_ref[...]
        normed, inverse = norm_rows(tok_ref[...].astype(F32))
        out_ref[...] = after_ref[...] + norm_back(grad_first, normed, inverse, gain_ref[...])
        row = lax.broadcasted_iota(jnp.int32, sums_ref.shape, 0)
        gain_sum = jnp.sum(grad_first * normed, axis=0, keepdims=True)
        bias_sum = jnp.sum(grad_first, axis=0, keepdims=True)
        sums = jnp.where(row == 0, gain_sum, jnp.where(row == 1, bias_sum, 0.0))
        sums_ref[...] = jnp.where(step == 0, sums, sums_ref[...] + sums)
    else:
        out_ref[...] = grad_first

    @pl.when(step == pl.num_programs(0) - 1)
    def _():
        half, own, _ = away_ref.shape
        whole_ref[:, : 3 * cols] = dot_tn(first_ref[...], grads_ref[...])
        if final:
            sums = sums_ref[...]
            rest = jnp.zeros((LANES - sums.shape[0], sums.shape[1]), F32)
            whole_ref[:, 3 * cols :] = (jnp.concatenate([sums, rest], axis=0) + vec_ref[...]).T
        else:
            whole_ref[:, 3 * cols :] = dot_tn(heads_ref[...], low_ref[...])
        core = core_ref[0]
        for chip in range(half):
            away = pl.ds(pl.multiple_of((2 * chip + 1 - core) * own, own), own)
            keep = pl.ds(pl.multiple_of((2 * chip + core) * own, own), own)
            away_ref[chip] = whole_ref[away, :].astype(BF)
            keep_ref[chip] = whole_ref[keep, :].astype(BF)


def attend_back(core, qkv, grad_heads_out, full, first, images, shards, group, extra, final):
    rows, width = grad_heads_out.shape
    cols = width // 2
    wide = 3 * cols + (LANES if final else width)
    half, own = shards // 2, width // shards
    at = lambda part: pl.BlockSpec((PAD_SEQ, cols), lambda i: (i, 2 * part + group))
    weight = lambda part: pl.BlockSpec((width, cols), lambda i: (0, 2 * part + group))
    held = lambda a: pl.BlockSpec(a.shape, lambda i: (0, 0))
    block = pl.BlockSpec((PAD_SEQ, width), lambda i: (i, 0))
    share = pl.BlockSpec((half, own, wide), lambda i: (0, 0, 0))
    share_shape = jax.ShapeDtypeStruct((half, own, wide), BF)
    return pl.pallas_call(
        functools.partial(
            attend_back_kernel, scale=1.0 / math.sqrt(width // HEADS), final=final
        ),
        grid=(images,),
        in_specs=[pl.BlockSpec(memory_space=pltpu.SMEM), at(0), at(1), at(2), at(0)]
        + [weight(0), weight(1), weight(2), held(first)]
        + ([block, block, block] + [held(a) for a in extra[3:]] if final else [held(a) for a in extra]),
        out_specs=[block, share, share],
        out_shape=[jax.ShapeDtypeStruct((rows, width), F32), share_shape, share_shape],
        scratch_shapes=[pltpu.VMEM((rows, 3 * cols), BF), pltpu.VMEM((width, wide), F32)]
        + ([pltpu.VMEM((8, width), F32)] if final else []),
        compiler_params=pltpu.CompilerParams(vmem_limit_bytes=VMEM_LIMIT),
        cost_estimate=pl.CostEstimate(
            flops=40 * rows * PAD_SEQ * cols,
            bytes_accessed=rows * cols,
            transcendentals=0,
        ),
    )(core, qkv, qkv, qkv, grad_heads_out, full, full, full, first, *extra)


def expert_kernel(
    me_ref, x_ref, c_ref, wr_ref, win_ref, wout_ref, win_rows_ref, wout_cols_ref,
    hid_ref, gp_ref, gm_ref, mg_ref, rows_ref, gr_ref,
    hid_all, gp_all, p_ref, gain_ref, routed_ref,
    *, experts, up_steps, down_steps,
):
    step = pl.program_id(0)
    rows = x_ref.shape[0]
    tile = win_ref.shape[1]
    piece = win_rows_ref.shape[0]
    lane = lax.broadcasted_iota(jnp.int32, (rows, LANES), 1)
    mine = lane == me_ref[0]

    def gate():
        return jnp.sum(jnp.where(mine, p_ref[...], 0.0), axis=-1, keepdims=True)

    @pl.when(step == 0)
    def _():
        logits = jnp.where(lane < experts, dot_nn(x_ref[...], wr_ref[...]), NEG)
        top = jnp.max(logits, axis=-1, keepdims=True)
        weights = jnp.exp(logits - top)
        p_ref[...] = weights / jnp.sum(weights, axis=-1, keepdims=True)
        gm_ref[...] = (gate() * c_ref[...].astype(F32)).astype(BF)

    @pl.when(step < up_steps)
    def _():
        col = pl.ds(pl.multiple_of(step * tile, tile), tile)
        pre = dot_nn(x_ref[...], win_ref[...])
        back = dot_nt(gm_ref[...], wout_ref[...])
        cdf = 0.5 * (1.0 + lax.erf(pre * (1.0 / math.sqrt(2.0))))
        density = jnp.exp(-0.5 * pre * pre) * (1.0 / math.sqrt(2.0 * math.pi))
        hidden = (pre * cdf).astype(BF)
        grad_pre = (back * (cdf + pre * density)).astype(BF)
        hid_ref[...] = hidden
        gp_ref[...] = grad_pre
        hid_all[:, col] = hidden
        gp_all[:, col] = grad_pre

    @pl.when((step >= up_steps) & (step < up_steps + down_steps))
    def _():
        part = step - up_steps
        col = pl.ds(pl.multiple_of(part * piece, piece), piece)
        made = dot_nn(hid_all[...], wout_cols_ref[...])
        mg_ref[...] = (gate() * made).astype(BF)
        gain = c_ref[:, col].astype(F32) * made.astype(BF).astype(F32)
        gain = jnp.broadcast_to(jnp.sum(gain, axis=-1, keepdims=True), (rows, LANES))
        gain_ref[...] = jnp.where(part == 0, gain, gain_ref[...] + gain)

    @pl.when(step == up_steps + down_steps)
    def _():
        probs = p_ref[...]
        routed = gain_ref[...] * gate() * (jnp.where(mine, 1.0, 0.0) - probs)
        routed_ref[...] = routed.astype(BF)
        gr_ref[...] = dot_tn(routed_ref[...], x_ref[...])

    @pl.when(step >= up_steps + down_steps)
    def _():
        part = step - up_steps - down_steps
        router = wr_ref[pl.ds(pl.multiple_of(part * piece, piece), piece), :]
        back = dot_nt(gp_all[...], win_rows_ref[...]) + dot_nt(routed_ref[...], router)
        rows_ref[...] = back.astype(BF)


def run_expert(me, x, c, w_router, w_in, w_out, experts):
    rows, width = x.shape
    hidden = w_in.shape[1]
    tile, piece = 512, 256
    up_steps, down_steps = hidden // tile, width // piece
    whole = lambda j: (0, 0)
    up = lambda j: jnp.minimum(j, up_steps - 1)
    made = lambda j: jnp.clip(j - up_steps, 0, down_steps - 1)
    back = lambda j: jnp.clip(j - up_steps - down_steps, 0, down_steps - 1)
    big = jax.ShapeDtypeStruct((rows, hidden), BF)
    small = jax.ShapeDtypeStruct((rows, width), BF)
    return pl.pallas_call(
        functools.partial(
            expert_kernel, experts=experts, up_steps=up_steps, down_steps=down_steps
        ),
        grid=(up_steps + 2 * down_steps,),
        in_specs=[
            pl.BlockSpec(memory_space=pltpu.SMEM),
            pl.BlockSpec((rows, width), whole),
            pl.BlockSpec((rows, width), whole),
            pl.BlockSpec((width, LANES), whole),
            pl.BlockSpec((width, tile), lambda j: (0, up(j))),
            pl.BlockSpec((tile, width), lambda j: (up(j), 0)),
            pl.BlockSpec((piece, hidden), lambda j: (back(j), 0)),
            pl.BlockSpec((hidden, piece), lambda j: (0, made(j))),
        ],
        out_specs=[
            pl.BlockSpec((rows, tile), lambda j: (0, up(j))),
            pl.BlockSpec((rows, tile), lambda j: (0, up(j))),
            pl.BlockSpec((rows, width), whole),
            pl.BlockSpec((rows, piece), lambda j: (0, made(j))),
            pl.BlockSpec((rows, piece), lambda j: (0, back(j))),
            pl.BlockSpec((LANES, width), whole),
        ],
        out_shape=[big, big, small, small, small, jax.ShapeDtypeStruct((LANES, width), F32)],
        scratch_shapes=[
            pltpu.VMEM((rows, hidden), BF),
            pltpu.VMEM((rows, hidden), BF),
            pltpu.VMEM((rows, LANES), F32),
            pltpu.VMEM((rows, LANES), F32),
            pltpu.VMEM((rows, LANES), BF),
        ],
        compiler_params=pltpu.CompilerParams(vmem_limit_bytes=VMEM_LIMIT),
        cost_estimate=pl.CostEstimate(
            flops=16 * rows * width * hidden,
            bytes_accessed=rows * hidden,
            transcendentals=0,
        ),
    )(me, x, c, w_router, w_in, w_out, w_in, w_out)


def weight_grad_kernel(x_a, x_b, gm_a, gm_b, gp_a, gp_b, hid_a, hid_b, in_ref, out_ref):
    in_ref[...] = (dot_tn(x_a[...], gp_a[...]) + dot_tn(x_b[...], gp_b[...])).astype(BF)
    out_ref[...] = (dot_tn(hid_a[...], gm_a[...]) + dot_tn(hid_b[...], gm_b[...])).astype(BF)


def weight_grads(x, grad_made, grad_pre, hidden):
    width, hid = x[0].shape[1], hidden[0].shape[1]
    tile = 512
    count = x[0].shape[0] + x[1].shape[0]
    held = lambda a: pl.BlockSpec(a.shape, lambda j: (0, 0))
    tiled = lambda a: pl.BlockSpec((a.shape[0], tile), lambda j: (0, j))
    return pl.pallas_call(
        weight_grad_kernel,
        grid=(hid // tile,),
        in_specs=[held(a) for a in (*x, *grad_made)] + [tiled(a) for a in (*grad_pre, *hidden)],
        out_specs=[
            pl.BlockSpec((width, tile), lambda j: (0, j)),
            pl.BlockSpec((tile, width), lambda j: (j, 0)),
        ],
        out_shape=[
            jax.ShapeDtypeStruct((width, hid), BF),
            jax.ShapeDtypeStruct((hid, width), BF),
        ],
        compiler_params=pltpu.CompilerParams(vmem_limit_bytes=VMEM_LIMIT),
        cost_estimate=pl.CostEstimate(
            flops=8 * count * width * hid, bytes_accessed=width * hid, transcendentals=0
        ),
    )(*x, *grad_made, *grad_pre, *hidden)


def combine_kernel(
    at_ref, back_a_ref, back_b_ref, glog_ref, router_ref, proj_ref, after_ref, cot_ref, gain_ref,
    grad_ref, low_ref, heads_ref, sums_ref,
):
    rows = at_ref.shape[0]

    def picked(first, back_ref):
        slot = lax.broadcasted_iota(jnp.int32, (rows, back_ref.shape[0]), 1)
        match = (slot == at_ref[:, first : first + 1]) | (slot == at_ref[:, first + 1 : first + 2])
        return dot_nn(jnp.where(match, 1.0, 0.0).astype(BF), back_ref[...])

    grad_mid = picked(0, back_a_ref) + picked(2, back_b_ref) + dot_nt(glog_ref[...], router_ref[...])
    normed, inverse = norm_rows(after_ref[...])
    grad = cot_ref[...].astype(F32) + norm_back(grad_mid, normed, inverse, gain_ref[...])
    grad_ref[...] = grad
    low = grad.astype(BF)
    low_ref[...] = low
    heads_ref[...] = dot_nt(low, proj_ref[...]).astype(BF)
    row = lax.broadcasted_iota(jnp.int32, sums_ref.shape, 0)
    gain_sum = jnp.sum(grad_mid * normed, axis=0, keepdims=True)
    bias_sum = jnp.sum(grad_mid, axis=0, keepdims=True)
    sums = jnp.where(row == 0, gain_sum, jnp.where(row == 1, bias_sum, 0.0))

    @pl.when(pl.program_id(0) == 0)
    def _():
        sums_ref[...] = sums

    @pl.when(pl.program_id(0) > 0)
    def _():
        sums_ref[...] += sums


def combine(places, backs, grad_logits, full, after_attention, cot_pad, gain, images):
    rows, width = after_attention.shape
    block = lambda cols: pl.BlockSpec((PAD_SEQ, cols), lambda i: (i, 0))
    held = lambda a: pl.BlockSpec(a.shape, lambda i: (0, 0))
    return pl.pallas_call(
        combine_kernel,
        grid=(images,),
        in_specs=[
            block(LANES),
            held(backs[0]),
            held(backs[1]),
            block(LANES),
            pl.BlockSpec((width, LANES), lambda i: (0, 4 * width // LANES)),
            pl.BlockSpec((width, width), lambda i: (0, 3)),
            block(width),
            block(width),
            pl.BlockSpec((1, width), lambda i: (0, 0)),
        ],
        out_specs=[block(width)] * 3 + [pl.BlockSpec((8, width), lambda i: (0, 0))],
        out_shape=[
            jax.ShapeDtypeStruct((rows, width), F32),
            jax.ShapeDtypeStruct((rows, width), BF),
            jax.ShapeDtypeStruct((rows, width), BF),
            jax.ShapeDtypeStruct((8, width), F32),
        ],
        compiler_params=pltpu.CompilerParams(vmem_limit_bytes=VMEM_LIMIT),
        cost_estimate=pl.CostEstimate(
            flops=28 * rows * width * width, bytes_accessed=rows * width, transcendentals=0
        ),
    )(places, *backs, grad_logits, full, full, after_attention, cot_pad, gain.reshape(1, -1))


def axis_bits(size):
    return [1 << b for b in range(size.bit_length() - 1)]


def exchange(value, axis, bit):
    size = lax.axis_size(axis)
    return lax.ppermute(value, axis, [(i, i ^ bit) for i in range(size)])


def bit_of(axis, bit):
    return (lax.axis_index(axis) // bit) % 2


def in_order(axis, bit, held, got):
    return jnp.where(bit_of(axis, bit) == 0, jnp.stack([held, got]), jnp.stack([got, held]))


def gather_pieces(block, axis):
    pieces = {0: block}
    for bit in reversed(axis_bits(lax.axis_size(axis))):
        for k in list(pieces):
            pieces[k | bit] = exchange(pieces[k], axis, bit)
    return [pieces[k] for k in sorted(pieces)]


def reduce_cores(away, keep):
    return (keep.astype(F32) + exchange(away, "shard", 1).astype(F32)).astype(BF)


def halve(held, bit):
    view = held.reshape((-1, 2) + held.shape[1:])
    mine = bit_of("shard", bit)
    pick = lambda at: lax.dynamic_index_in_dim(view, at, 1, keepdims=False)
    return pick(1 - mine).astype(BF), pick(mine).astype(F32)


def reduce_chips(send, stay):
    bits = axis_bits(lax.axis_size("shard"))[1:]
    for at, bit in enumerate(bits):
        held = stay + exchange(send, "shard", bit).astype(F32)
        if at + 1 < len(bits):
            send, stay = halve(held, bits[at + 1])
    return held[0]


def over_owners_by_halves(held):
    owners = lax.axis_size("expert")
    cols = held.shape[1]
    groups = [list(range(low, owners, 2)) for low in range(2)]
    spread = lambda parts: lax.all_to_all(
        parts, "expert", split_axis=0, concat_axis=0, tiled=True, axis_index_groups=groups
    )
    view = held.reshape(2, -1, cols)
    mine = bit_of("expert", 1)
    send = lax.dynamic_index_in_dim(view, 1 - mine, 0, keepdims=False).astype(BF)
    stay = lax.dynamic_index_in_dim(view, mine, 0, keepdims=False)
    held = (stay + exchange(send, "expert", 1).astype(F32)).astype(BF)
    got = spread(held.reshape(owners // 2, -1, cols))
    total = jnp.sum(got.astype(F32), axis=0).astype(BF)
    held = spread(jnp.broadcast_to(total[None], got.shape)).reshape(-1, cols)
    held = in_order("expert", 1, held, exchange(held, "expert", 1))
    return held.reshape(-1, cols).astype(F32)


def over_owners_by_parts(held):
    owners = lax.axis_size("expert")
    rows, cols = held.shape
    got = trade(held.astype(BF).reshape(owners, rows // owners, cols))
    total = jnp.sum(got.astype(F32), axis=0).astype(BF)
    return trade(jnp.broadcast_to(total[None], got.shape)).reshape(rows, cols).astype(F32)


def trade(view):
    return lax.all_to_all(view, "expert", split_axis=0, concat_axis=0, tiled=True)


def tie(*values):
    return lax.optimization_barrier(values)


def body(
    tokens, routes, capacity, ln1_gain, ln1_bias, ln2_gain, ln2_bias,
    w_qkv, w_proj, w_router, w_in, w_out, cotangent,
):
    count, width = tokens.shape
    experts = capacity.shape[0]
    owners = lax.axis_size("expert")
    shards = lax.axis_size("shard")
    images = count // SEQ
    padded = images * PAD_SEQ
    slot_count = 8 * ((2 * count + 8 * experts - 1) // (8 * experts))
    all_tokens = count * owners * shards
    me = lax.axis_index("expert").astype(jnp.int32).reshape(1)

    def pad_rows(values, fill=0):
        spread = values.reshape((images, SEQ) + values.shape[1:])
        room = [(0, 0), (0, PAD_SEQ - SEQ)] + [(0, 0)] * (values.ndim - 1)
        return jnp.pad(spread, room, constant_values=fill).reshape((padded,) + values.shape[1:])

    def cut_rows(values):
        spread = values.reshape((images, PAD_SEQ) + values.shape[1:])
        return spread[:, :SEQ].reshape((count,) + values.shape[1:])

    labels = jnp.arange(experts, dtype=jnp.int32)[:, None]
    first, second = routes[:, 0][None, :], routes[:, 1][None, :]
    hit_first, hit_second = first == labels, second == labels
    hits = jnp.concatenate([hit_first, hit_second], axis=0).astype(BF)
    order = lax.broadcasted_iota(jnp.int32, (count, count), 0) < lax.broadcasted_iota(
        jnp.int32, (count, count), 1
    )
    before = dot_nn(hits, order.astype(BF))
    totals = jnp.sum(hits.astype(F32), axis=1, keepdims=True)
    before_first = before[:experts]

    counts = (totals[:experts] + totals[experts:]).reshape(1, experts)
    high = jnp.floor(counts * (1.0 / COUNT_BASE))
    note = jnp.concatenate([high, counts - COUNT_BASE * high], axis=1).astype(BF)
    note = jnp.pad(note, ((0, w_router.shape[0] - 1), (0, 0)))
    room = jnp.zeros((w_router.shape[0], LANES - 3 * experts), BF)
    pieces = gather_pieces(
        jnp.concatenate([w_qkv, w_proj, w_router, note, room], axis=1), "shard"
    )

    before_second = before[experts:] + totals[:experts]
    limits = capacity[:, None].astype(F32)

    def slots(hit, ahead, choice):
        slot = jnp.sum(jnp.where(hit, ahead, 0.0), axis=0)
        limit = jnp.sum(jnp.where(hit, limits, 0.0), axis=0)
        kept = slot < limit
        slot = slot.astype(jnp.int32)
        return choice[0], slot, kept

    choices = [slots(hit_first, before_first, first), slots(hit_second, before_second, second)]
    head = 8 * ((slot_count + 15) // 16)
    spans = ((0, head), (head, slot_count - head))

    def chosen(start, size):
        found = []
        for choice, slot, kept in choices:
            inside = slot - start
            valid = kept & (inside >= 0) & (inside < size)
            found.append(pad_rows(jnp.where(valid, choice * size + inside, -1), -1))
        return found

    def selector(start, size):
        at = lax.broadcasted_iota(jnp.int32, (experts * size, 1), 0)
        first, second = chosen(start, size)
        return ((at == first[None, :]) | (at == second[None, :])).astype(BF)

    def send(select, rows):
        return dot_nn(select, rows).astype(BF).reshape(experts, -1, width)

    select_all = selector(0, slot_count)
    select = [selector(start, size) for start, size in spans]
    cot_pad = pad_rows(cotangent)
    cot_rows = trade(send(select_all, cot_pad))

    tok_pad = pad_rows(tokens)
    first_low, qkv_rows, heads_out, full = attend(tok_pad, ln1_gain, ln1_bias, pieces, images)
    proj_full = full[:, 3 * width : 4 * width]
    router_full = full[:, 4 * width :]
    notes = router_full[:: width // shards, experts : 3 * experts].astype(F32)
    notes = jnp.sum(notes, axis=0, keepdims=True)
    counts = COUNT_BASE * notes[:, :experts] + notes[:, experts:]
    counts = jnp.pad(counts, ((0, 0), (0, LANES - experts)))
    for bit in axis_bits(owners):
        counts = counts + exchange(counts, "expert", bit)
    route_share = counts[:, :experts] / (2.0 * all_tokens)
    token_rows = tok_pad.astype(F32)
    after_attention = token_rows + dot_nn(heads_out, proj_full)
    normed_two, inverse_two = norm_rows(after_attention)
    mid_low = (normed_two * ln2_gain + ln2_bias).astype(BF)

    logits = dot_nn(mid_low, router_full)[:, :experts]
    live = (lax.broadcasted_iota(jnp.int32, (padded, 1), 0) % PAD_SEQ) < SEQ
    gate_probs = jnp.where(live, jax.nn.softmax(logits, axis=-1), 0.0)
    push = LOSS_WEIGHT * experts * route_share / all_tokens
    grad_logits = gate_probs * (push - jnp.sum(gate_probs * push, axis=-1, keepdims=True))
    grad_logits = jnp.pad(grad_logits, ((0, 0), (0, LANES - experts))).astype(BF)
    grad_router = dot_tn(grad_logits, mid_low)

    sent, cot_rows = tie(send(select[0], mid_low), cot_rows)
    arrived = [trade(sent)]
    sent, arrived[0] = tie(send(select[1], mid_low), arrived[0])
    arrived.append(trade(sent))
    places = jnp.stack([p for span in spans for p in chosen(*span)], axis=0)
    places = jnp.pad(places, ((0, LANES - places.shape[0]), (0, 0)), constant_values=-1).T
    arrived[0], grad_logits, grad_router, places = tie(
        arrived[0], grad_logits, grad_router, places
    )
    made = [
        run_expert(
            me,
            arrived[i].reshape(-1, width),
            cot_rows[:, start : start + size].reshape(-1, width),
            router_full, w_in[0], w_out[0], experts,
        )
        for i, (start, size) in enumerate(spans)
    ]
    hidden, grad_pre, grad_made, gated, grad_rows, router_parts = zip(*made)
    grad_rows = [g.reshape(experts, -1, width) for g in grad_rows]
    backs = [trade(grad_rows[0])]
    gated = jnp.concatenate([g.reshape(experts, -1, width) for g in gated], axis=1)
    sent, backs[0], gated = tie(grad_rows[1], backs[0], gated)
    backs.append(trade(sent))
    mids = [a.reshape(-1, width) for a in arrived]
    mids[0], backs[0] = tie(mids[0], backs[0])
    core = (lax.axis_index("shard") % 2).astype(jnp.int32).reshape(1)
    grad_in, grad_out = weight_grads(mids, grad_made, grad_pre, hidden)
    gated, backs[1], grad_in, grad_out = tie(gated, backs[1], grad_in, grad_out)
    grad_expert_in = lax.psum_scatter(grad_in, "shard", scatter_dimension=1, tiled=True)
    grad_expert_out = lax.psum_scatter(grad_out, "shard", scatter_dimension=0, tiled=True)
    returned = trade(gated)

    backs = [b.reshape(-1, width) for b in backs]
    grad_after, grad_heads, grad_heads_out, sums_two = combine(
        places, backs, grad_logits, full, after_attention, cot_pad, ln2_gain, images
    )
    grad_router = grad_router + router_parts[0] + router_parts[1]
    own = width // shards
    prob_sum = jnp.tile(jnp.pad(jnp.sum(gate_probs, axis=0), (0, own - experts)), shards)
    small = jnp.concatenate([sums_two[:2], prob_sum[None], grad_router[:experts]], axis=0)
    small = jnp.pad(small, ((2, LANES - 2 - small.shape[0]), (0, 0)))
    back = functools.partial(
        attend_back, core, qkv_rows, grad_heads_out, full, first_low, images, shards
    )
    grad_first, *share = back(0, (heads_out, grad_heads), False)
    send, stay = halve(reduce_cores(*share), 2)
    total = reduce_chips(send, stay)
    rest = (grad_first, tok_pad, grad_after, ln1_gain.reshape(1, -1), small)
    grad_tokens, *share = back(1, rest, True)
    share[0], share[1], returned, total = tie(*share, returned, total)
    reduced = [over_owners_by_halves(total)]
    total = reduce_chips(*halve(reduce_cores(*share), 2))
    reduced.append(over_owners_by_parts(total))
    grad_tokens = cut_rows(grad_tokens)

    mixed = cut_rows(after_attention + dot_tn(select_all, returned.reshape(-1, width))).astype(BF)
    cols = width // 2
    grad_qkv_weight = jnp.concatenate(
        [t[:, part * cols : (part + 1) * cols] for part in range(3) for t in reduced], axis=1
    )
    proj_total = reduced[0][:, 3 * cols :]
    vectors = reduced[1][:, 3 * cols : 3 * cols + 5 + experts].T
    balance_loss = experts * jnp.sum(route_share[0] * vectors[4, :experts] / all_tokens)
    return (
        mixed,
        balance_loss,
        grad_tokens,
        vectors[0],
        vectors[1],
        vectors[2],
        vectors[3],
        grad_qkv_weight,
        proj_total,
        vectors[5:].T,
        grad_expert_in.astype(F32)[None],
        grad_expert_out.astype(F32)[None],
    )


def solution(mesh):
    rows = P(("expert", "shard"), None)
    in_specs = (
        rows, rows, P(), P(), P(), P(), P(),
        P("shard", None), P("shard", None), P("shard", None),
        P("expert", None, None), P("expert", None, None), rows,
    )
    out_specs = (
        rows, P(), rows, P("shard"), P("shard"), P("shard"), P("shard"),
        P("shard", None), P("shard", None), P("shard", None),
        P("expert", None, "shard"), P("expert", "shard", None),
    )
    return jax.shard_map(body, mesh=mesh, in_specs=in_specs, out_specs=out_specs, check_vma=False)
```

```python
import functools
import math

import jax
import jax.numpy as jnp
from jax import lax
from jax.experimental import pallas as pl
from jax.experimental.pallas import tpu as pltpu
from jax.sharding import PartitionSpec as P

HEADS = 12
SEQ = 197
PAD_SEQ = 208
LANES = 128

NORM_EPS = 1e-06
LOSS_WEIGHT = 0.01
NEG = -1e30
COUNT_BASE = 128
VMEM_LIMIT = 56 * 1024 * 1024
BF = jnp.bfloat16
F32 = jnp.float32


def dot_nn(left, right):
    return lax.dot_general(left, right, (((1,), (0,)), ((), ())), preferred_element_type=F32)


def dot_nt(left, right):
    return lax.dot_general(left, right, (((1,), (1,)), ((), ())), preferred_element_type=F32)


def dot_tn(left, right):
    return lax.dot_general(left, right, (((0,), (0,)), ((), ())), preferred_element_type=F32)


def norm_rows(values):
    row_mean = jnp.mean(values, axis=-1, keepdims=True)
    centered = values - row_mean
    variance = jnp.mean(centered * centered, axis=-1, keepdims=True)
    inverse = lax.rsqrt(variance + NORM_EPS)
    return centered * inverse, inverse


def norm_back(grad_rows, normed, inverse, norm_gain):
    scaled = grad_rows * norm_gain
    return inverse * (
        scaled
        - jnp.mean(scaled, axis=-1, keepdims=True)
        - normed * jnp.mean(scaled * normed, axis=-1, keepdims=True)
    )


def attend_kernel(tok_ref, gain_ref, bias_ref, *refs, shards):
    pieces, refs = refs[:shards], refs[shards:]
    first_ref, qkv_ref, heads_ref, full_ref, w_ref, sems = refs
    step = pl.program_id(0)
    width = tok_ref.shape[1]
    own = width // shards
    me = lax.axis_index("shard")

    def place(k):
        at = 0
        for bit in axis_bits(shards):
            mine = lax.rem(me // bit, 2)
            at = at + bit * (1 - mine if k & bit else mine)
        rows = pl.ds(pl.multiple_of(at * own, own), own)
        return pltpu.make_async_copy(pieces[k], w_ref.at[rows, :], sems.at[k])

    whole_copy = pltpu.make_async_copy(w_ref, full_ref, sems.at[shards])

    @pl.when(step == 0)
    def _():
        for k in range(shards):
            place(k).start()

    normed, _ = norm_rows(tok_ref[...].astype(F32))
    first = (normed * gain_ref[...] + bias_ref[...]).astype(BF)
    first_ref[...] = first

    @pl.when(step == 0)
    def _():
        for k in range(shards):
            place(k).wait()
        whole_copy.start()

    for part in range(3):
        cols = slice(part * width, (part + 1) * width)
        qkv_ref[:, cols] = dot_nn(first, w_ref[:, cols]).astype(BF)
    rows = tok_ref.shape[0]
    lane = lax.broadcasted_iota(jnp.int32, (rows, LANES), 1)
    key_at = lax.broadcasted_iota(jnp.int32, (rows, rows), 1)
    scale = 1.0 / math.sqrt(width // HEADS)
    for pair in range(width // LANES):
        queries = qkv_ref[:, pair * LANES : (pair + 1) * LANES]
        keys = qkv_ref[:, width + pair * LANES : width + (pair + 1) * LANES]
        values = qkv_ref[:, 2 * width + pair * LANES : 2 * width + (pair + 1) * LANES]
        mixed = None
        for half in range(2):
            mine = (lane < LANES // 2) if half == 0 else (lane >= LANES // 2)
            zero = jnp.zeros_like(queries)
            scores = dot_nt(jnp.where(mine, queries, zero), keys) * scale
            scores = jnp.where(key_at < SEQ, scores, NEG)
            peak = jnp.max(scores, axis=-1, keepdims=True)
            weights = jnp.exp(scores - peak)
            total = jnp.sum(weights, axis=-1, keepdims=True)
            weights = (weights / total).astype(BF)
            term = dot_nn(weights, jnp.where(mine, values, zero))
            mixed = term if mixed is None else mixed + term
        heads_ref[:, pair * LANES : (pair + 1) * LANES] = mixed.astype(BF)

    @pl.when(step == pl.num_programs(0) - 1)
    def _():
        whole_copy.wait()


def attend(tok_pad, gain, bias, pieces, images):
    rows, width = tok_pad.shape
    shards = len(pieces)
    own, cols = pieces[0].shape
    whole = lambda i: (0, 0)
    block = lambda i: (i, 0)
    return pl.pallas_call(
        functools.partial(attend_kernel, shards=shards),
        grid=(images,),
        in_specs=[
            pl.BlockSpec((PAD_SEQ, width), block),
            pl.BlockSpec((1, width), whole),
            pl.BlockSpec((1, width), whole),
        ]
        + [pl.BlockSpec(memory_space=pl.ANY)] * shards,
        out_specs=[
            pl.BlockSpec((PAD_SEQ, width), block),
            pl.BlockSpec((PAD_SEQ, 3 * width), block),
            pl.BlockSpec((PAD_SEQ, width), block),
            pl.BlockSpec(memory_space=pl.ANY),
        ],
        out_shape=[
            jax.ShapeDtypeStruct((rows, width), BF),
            jax.ShapeDtypeStruct((rows, 3 * width), BF),
            jax.ShapeDtypeStruct((rows, width), BF),
            jax.ShapeDtypeStruct((shards * own, cols), BF),
        ],
        scratch_shapes=[
            pltpu.VMEM((shards * own, cols), BF),
            pltpu.SemaphoreType.DMA((shards + 1,)),
        ],
        compiler_params=pltpu.CompilerParams(vmem_limit_bytes=VMEM_LIMIT),
        cost_estimate=pl.CostEstimate(
            flops=rows * width * width, bytes_accessed=rows * width, transcendentals=0
        ),
    )(tok_pad, gain.reshape(1, -1), bias.reshape(1, -1), *pieces)


def heads_back(q_ref, k_ref, v_ref, g_ref, out_ref, at_rows, scale):
    rows, cols = q_ref.shape
    lane = lax.broadcasted_iota(jnp.int32, (rows, LANES), 1)
    key_at = lax.broadcasted_iota(jnp.int32, (rows, rows), 0)
    for pair in range(cols // LANES):
        at = slice(pair * LANES, (pair + 1) * LANES)
        queries, keys, values, grads = q_ref[:, at], k_ref[:, at], v_ref[:, at], g_ref[:, at]
        zero = jnp.zeros_like(queries)
        sums = None
        for half in range(2):
            mine = (lane < LANES // 2) if half == 0 else (lane >= LANES // 2)
            q_half = jnp.where(mine, queries, zero)
            g_half = jnp.where(mine, grads, zero)
            scores = dot_nt(keys, q_half) * scale
            scores = jnp.where(key_at < SEQ, scores, NEG)
            peak = jnp.max(scores, axis=0, keepdims=True)
            weights = jnp.exp(scores - peak)
            probs = weights / jnp.sum(weights, axis=0, keepdims=True)
            grad_attention = dot_nt(values, g_half)
            inner = jnp.sum(probs * grad_attention, axis=0, keepdims=True)
            grad_scores = (probs * (grad_attention - inner)).astype(BF)
            terms = (
                dot_tn(grad_scores, jnp.where(mine, keys, zero)),
                dot_nn(grad_scores, q_half),
                dot_nn(probs.astype(BF), g_half),
            )
            sums = terms if sums is None else tuple(a + b for a, b in zip(sums, terms))
        for part, value in enumerate((sums[0] * scale, sums[1] * scale, sums[2])):
            start = part * cols + pair * LANES
            out_ref[at_rows, start : start + LANES] = value.astype(BF)


def attend_back_kernel(
    core_ref, q_ref, k_ref, v_ref, g_ref, wq_ref, wk_ref, wv_ref, *refs, scale, final
):
    step = pl.program_id(0)
    rows, cols = q_ref.shape
    at_rows = pl.ds(pl.multiple_of(step * rows, rows), rows)
    late = 1 if final else 3
    sources, refs = refs[:late], refs[late:]
    held, sems, refs = refs[-late - 1 : -1], refs[-1], refs[: -late - 1]
    copies = [
        pltpu.make_async_copy(source, target, sems.at[at])
        for at, (source, target) in enumerate(zip(sources, held))
    ]

    @pl.when(step == 0)
    def _():
        for copy in copies:
            copy.start()

    if final:
        before_ref, tok_ref, after_ref, gain_ref, two_ref, vec_ref = refs[:6]
        out_ref, away_ref, keep_ref, grads_ref, whole_ref, sums_ref = refs[6:]
    else:
        out_ref, away_ref, keep_ref, grads_ref, whole_ref = refs
    heads_back(q_ref, k_ref, v_ref, g_ref, grads_ref, at_rows, scale)
    grad_first = None
    for part, w_ref in enumerate((wq_ref, wk_ref, wv_ref)):
        term = dot_nt(grads_ref[at_rows, part * cols : (part + 1) * cols], w_ref[...])
        grad_first = term if grad_first is None else grad_first + term
    if final:
        grad_first = grad_first + before_ref[...]
        normed, inverse = norm_rows(tok_ref[...].astype(F32))
        out_ref[...] = after_ref[...] + norm_back(grad_first, normed, inverse, gain_ref[...])
        row = lax.broadcasted_iota(jnp.int32, sums_ref.shape, 0)
        gain_sum = jnp.sum(grad_first * normed, axis=0, keepdims=True)
        bias_sum = jnp.sum(grad_first, axis=0, keepdims=True)
        sums = jnp.where(row == 0, gain_sum, jnp.where(row == 1, bias_sum, 0.0))
        sums_ref[...] = jnp.where(step == 0, sums, sums_ref[...] + sums)
    else:
        out_ref[...] = grad_first

    @pl.when(step == pl.num_programs(0) - 1)
    def _():
        half, own, _ = away_ref.shape
        for copy in copies:
            copy.wait()
        whole_ref[:, : 3 * cols] = dot_tn(held[0][...], grads_ref[...])
        if final:
            sums = sums_ref[...] + pltpu.roll(two_ref[...], 2, 0)
            rest = jnp.zeros((LANES - sums.shape[0], sums.shape[1]), F32)
            whole_ref[:, 3 * cols :] = (jnp.concatenate([sums, rest], axis=0) + vec_ref[...]).T
        else:
            whole_ref[:, 3 * cols :] = dot_tn(held[1][...], held[2][...])
        core = core_ref[0]
        for chip in range(half):
            away = pl.ds(pl.multiple_of((2 * chip + 1 - core) * own, own), own)
            keep = pl.ds(pl.multiple_of((2 * chip + core) * own, own), own)
            away_ref[chip] = whole_ref[away, :].astype(BF)
            keep_ref[chip] = whole_ref[keep, :].astype(BF)


def attend_back(core, qkv, grad_heads_out, full, first, images, shards, group, extra, final):
    rows, width = grad_heads_out.shape
    cols = width // 2
    wide = 3 * cols + (LANES if final else width)
    half, own = shards // 2, width // shards
    late = 1 if final else 3
    at = lambda part: pl.BlockSpec((PAD_SEQ, cols), lambda i: (i, 2 * part + group))
    weight = lambda part: pl.BlockSpec((width, cols), lambda i: (0, 2 * part + group))
    held = lambda a: pl.BlockSpec(a.shape, lambda i: (0, 0))
    block = pl.BlockSpec((PAD_SEQ, width), lambda i: (i, 0))
    share = pl.BlockSpec((half, own, wide), lambda i: (0, 0, 0))
    share_shape = jax.ShapeDtypeStruct((half, own, wide), BF)
    return pl.pallas_call(
        functools.partial(
            attend_back_kernel, scale=1.0 / math.sqrt(width // HEADS), final=final
        ),
        grid=(images,),
        in_specs=[pl.BlockSpec(memory_space=pltpu.SMEM), at(0), at(1), at(2), at(0)]
        + [weight(0), weight(1), weight(2)]
        + [pl.BlockSpec(memory_space=pl.ANY)] * late
        + ([block, block, block] + [held(a) for a in extra[3:]] if final else []),
        out_specs=[block, share, share],
        out_shape=[jax.ShapeDtypeStruct((rows, width), F32), share_shape, share_shape],
        scratch_shapes=[pltpu.VMEM((rows, 3 * cols), BF), pltpu.VMEM((width, wide), F32)]
        + ([pltpu.VMEM((8, width), F32)] if final else [])
        + [pltpu.VMEM((rows, width), BF)] * late
        + [pltpu.SemaphoreType.DMA((late,))],
        compiler_params=pltpu.CompilerParams(vmem_limit_bytes=VMEM_LIMIT),
        cost_estimate=pl.CostEstimate(
            flops=40 * rows * PAD_SEQ * cols,
            bytes_accessed=rows * cols,
            transcendentals=0,
        ),
    )(core, qkv, qkv, qkv, grad_heads_out, full, full, full, first, *extra)


def assemble_kernel(left_ref, right_ref, share_ref, qkv_ref, proj_ref, small_ref, loss_ref, *, scale):
    rows, width = proj_ref.shape
    cols = width // 2
    for part in range(3):
        at = slice(part * cols, (part + 1) * cols)
        qkv_ref[:, part * width : part * width + cols] = left_ref[:, at].astype(F32)
        qkv_ref[:, part * width + cols : (part + 1) * width] = right_ref[:rows, at].astype(F32)
    proj_ref[...] = left_ref[:, 3 * cols :].astype(F32)
    small = right_ref[:, 3 * cols :].astype(F32).T
    small_ref[...] = small
    product = small[4:5, :LANES] * share_ref[...]
    loss_ref[...] = jnp.broadcast_to(jnp.sum(product, axis=-1, keepdims=True) * scale, (1, LANES))


def assemble(left, right, route_share, scale):
    rows = left.shape[0]
    width = 2 * left.shape[1] // 5
    spec = pl.BlockSpec(memory_space=pltpu.VMEM)
    padded = max(rows, LANES)
    share = jnp.pad(route_share, ((0, 0), (0, LANES - route_share.shape[1])))
    right = jnp.pad(right, ((0, padded - rows), (0, 0)))
    return pl.pallas_call(
        functools.partial(assemble_kernel, scale=scale),
        in_specs=[spec] * 3,
        out_specs=[spec] * 4,
        out_shape=[
            jax.ShapeDtypeStruct((rows, 3 * width), F32),
            jax.ShapeDtypeStruct((rows, width), F32),
            jax.ShapeDtypeStruct((LANES, padded), F32),
            jax.ShapeDtypeStruct((1, LANES), F32),
        ],
    )(left, right, share)


def expert_kernel(
    me_ref, x_ref, cots_ref, wr_ref, win_ref, wout_ref, win_rows_ref, wout_cols_ref,
    hid_ref, gp_ref, gm_ref, mg_ref, rows_ref, gr_ref,
    hid_all, gp_all, p_ref, gain_ref, routed_ref, c_ref,
    *, experts, up_steps, down_steps, start,
):
    step = pl.program_id(0)
    rows = x_ref.shape[0]
    tile = win_ref.shape[1]
    piece = win_rows_ref.shape[0]
    lane = lax.broadcasted_iota(jnp.int32, (rows, LANES), 1)
    mine = lane == me_ref[0]

    def gate():
        return jnp.sum(jnp.where(mine, p_ref[...], 0.0), axis=-1, keepdims=True)

    @pl.when(step == 0)
    def _():
        logits = jnp.where(lane < experts, dot_nn(x_ref[...], wr_ref[...]), NEG)
        top = jnp.max(logits, axis=-1, keepdims=True)
        weights = jnp.exp(logits - top)
        p_ref[...] = weights / jnp.sum(weights, axis=-1, keepdims=True)
        size = rows // cots_ref.shape[0]
        cots = cots_ref[:, start : start + size, :].astype(F32).reshape(rows, -1)
        c_ref[...] = cots.astype(BF)
        gm_ref[...] = (gate() * cots).astype(BF)

    @pl.when(step < up_steps)
    def _():
        col = pl.ds(pl.multiple_of(step * tile, tile), tile)
        pre = dot_nn(x_ref[...], win_ref[...])
        back = dot_nt(gm_ref[...], wout_ref[...])
        cdf = 0.5 * (1.0 + lax.erf(pre * (1.0 / math.sqrt(2.0))))
        density = jnp.exp(-0.5 * pre * pre) * (1.0 / math.sqrt(2.0 * math.pi))
        hidden = (pre * cdf).astype(BF)
        grad_pre = (back * (cdf + pre * density)).astype(BF)
        hid_ref[...] = hidden
        gp_ref[...] = grad_pre
        hid_all[:, col] = hidden
        gp_all[:, col] = grad_pre

    @pl.when((step >= up_steps) & (step < up_steps + down_steps))
    def _():
        part = step - up_steps
        col = pl.ds(pl.multiple_of(part * piece, piece), piece)
        made = dot_nn(hid_all[...], wout_cols_ref[...])
        mg_ref[...] = (gate() * made).astype(BF)
        gain = c_ref[:, col].astype(F32) * made.astype(BF).astype(F32)
        gain = jnp.broadcast_to(jnp.sum(gain, axis=-1, keepdims=True), (rows, LANES))
        gain_ref[...] = jnp.where(part == 0, gain, gain_ref[...] + gain)

    @pl.when(step == up_steps + down_steps)
    def _():
        probs = p_ref[...]
        routed = gain_ref[...] * gate() * (jnp.where(mine, 1.0, 0.0) - probs)
        routed_ref[...] = routed.astype(BF)
        gr_ref[...] = dot_tn(routed_ref[...], x_ref[...])

    @pl.when(step >= up_steps + down_steps)
    def _():
        part = step - up_steps - down_steps
        router = wr_ref[pl.ds(pl.multiple_of(part * piece, piece), piece), :]
        back = dot_nt(gp_all[...], win_rows_ref[...]) + dot_nt(routed_ref[...], router)
        rows_ref[...] = back.astype(BF)


def run_expert(me, x, cots, start, w_router, w_in, w_out, experts):
    rows, width = x.shape
    hidden = w_in.shape[1]
    tile, piece = 512, 256
    up_steps, down_steps = hidden // tile, width // piece
    whole = lambda j: (0, 0)
    up = lambda j: jnp.minimum(j, up_steps - 1)
    made = lambda j: jnp.clip(j - up_steps, 0, down_steps - 1)
    back = lambda j: jnp.clip(j - up_steps - down_steps, 0, down_steps - 1)
    big = jax.ShapeDtypeStruct((rows, hidden), BF)
    small = jax.ShapeDtypeStruct((rows, width), BF)
    return pl.pallas_call(
        functools.partial(
            expert_kernel, experts=experts, up_steps=up_steps, down_steps=down_steps, start=start
        ),
        grid=(up_steps + 2 * down_steps,),
        in_specs=[
            pl.BlockSpec(memory_space=pltpu.SMEM),
            pl.BlockSpec((rows, width), whole),
            pl.BlockSpec(cots.shape, lambda j: (0, 0, 0)),
            pl.BlockSpec((width, LANES), lambda j: (0, w_router.shape[1] // LANES - 1)),
            pl.BlockSpec((width, tile), lambda j: (0, up(j))),
            pl.BlockSpec((tile, width), lambda j: (up(j), 0)),
            pl.BlockSpec((piece, hidden), lambda j: (back(j), 0)),
            pl.BlockSpec((hidden, piece), lambda j: (0, made(j))),
        ],
        out_specs=[
            pl.BlockSpec((rows, tile), lambda j: (0, up(j))),
            pl.BlockSpec((rows, tile), lambda j: (0, up(j))),
            pl.BlockSpec((rows, width), whole),
            pl.BlockSpec((rows, piece), lambda j: (0, made(j))),
            pl.BlockSpec((rows, piece), lambda j: (0, back(j))),
            pl.BlockSpec((LANES, width), whole),
        ],
        out_shape=[big, big, small, small, small, jax.ShapeDtypeStruct((LANES, width), F32)],
        scratch_shapes=[
            pltpu.VMEM((rows, hidden), BF),
            pltpu.VMEM((rows, hidden), BF),
            pltpu.VMEM((rows, LANES), F32),
            pltpu.VMEM((rows, LANES), F32),
            pltpu.VMEM((rows, LANES), BF),
            pltpu.VMEM((rows, width), BF),
        ],
        compiler_params=pltpu.CompilerParams(vmem_limit_bytes=VMEM_LIMIT),
        cost_estimate=pl.CostEstimate(
            flops=16 * rows * width * hidden,
            bytes_accessed=rows * hidden,
            transcendentals=0,
        ),
    )(me, x, cots, w_router, w_in, w_out, w_in, w_out)


def weight_grad_kernel(
    core_ref, x_a, x_b, gm_a, gm_b, gp_a, gp_b, hid_a, hid_b, in_away, in_keep, out_away, out_keep
):
    half = pl.num_programs(0) // 2
    grad_in = (dot_tn(x_a[...], gp_a[...]) + dot_tn(x_b[...], gp_b[...])).astype(BF)
    grad_out = (dot_tn(hid_a[...], gm_a[...]) + dot_tn(hid_b[...], gm_b[...])).astype(BF)

    @pl.when(pl.program_id(0) < half)
    def _():
        in_away[0] = grad_in
        out_away[0] = grad_out

    @pl.when(pl.program_id(0) >= half)
    def _():
        in_keep[0] = grad_in
        out_keep[0] = grad_out


def weight_grads(core, x, grad_made, grad_pre, hidden, shards):
    width, hid = x[0].shape[1], hidden[0].shape[1]
    tile, half = hid // shards, shards // 2
    count = x[0].shape[0] + x[1].shape[0]

    def source(j, core_ref):
        parity = jnp.where(j < half, 1 - core_ref[0], core_ref[0])
        return (0, 2 * lax.rem(j, half) + parity)

    held = lambda a: pl.BlockSpec(a.shape, lambda j, core_ref: (0, 0))
    tiled = lambda a: pl.BlockSpec((a.shape[0], tile), source)
    away = lambda j, core_ref: (jnp.minimum(j, half - 1), 0, 0)
    keep = lambda j, core_ref: (jnp.maximum(j - half, 0), 0, 0)
    in_shape = jax.ShapeDtypeStruct((half, width, tile), BF)
    out_shape = jax.ShapeDtypeStruct((half, tile, width), BF)
    return pl.pallas_call(
        weight_grad_kernel,
        grid_spec=pltpu.PrefetchScalarGridSpec(
            num_scalar_prefetch=1,
            grid=(shards,),
            in_specs=[held(a) for a in (*x, *grad_made)]
            + [tiled(a) for a in (*grad_pre, *hidden)],
            out_specs=[
                pl.BlockSpec((1, width, tile), away),
                pl.BlockSpec((1, width, tile), keep),
                pl.BlockSpec((1, tile, width), away),
                pl.BlockSpec((1, tile, width), keep),
            ],
        ),
        out_shape=[in_shape, in_shape, out_shape, out_shape],
        compiler_params=pltpu.CompilerParams(vmem_limit_bytes=VMEM_LIMIT),
        cost_estimate=pl.CostEstimate(
            flops=8 * count * width * hid, bytes_accessed=width * hid, transcendentals=0
        ),
    )(core, *x, *grad_made, *grad_pre, *hidden)


def combine_kernel(
    at_ref, back_a_ref, back_b_ref, glog_ref, router_ref, proj_ref, after_ref, cot_ref, gain_ref,
    grad_ref, low_ref, heads_ref, sums_ref,
):
    rows = at_ref.shape[0]

    def picked(first, back_ref):
        slot = lax.broadcasted_iota(jnp.int32, (rows, back_ref.shape[0]), 1)
        match = (slot == at_ref[:, first : first + 1]) | (slot == at_ref[:, first + 1 : first + 2])
        return dot_nn(jnp.where(match, 1.0, 0.0).astype(BF), back_ref[...])

    grad_mid = picked(0, back_a_ref) + picked(2, back_b_ref) + dot_nt(glog_ref[...], router_ref[...])
    normed, inverse = norm_rows(after_ref[...])
    grad = cot_ref[...].astype(F32) + norm_back(grad_mid, normed, inverse, gain_ref[...])
    grad_ref[...] = grad
    low = grad.astype(BF)
    low_ref[...] = low
    heads_ref[...] = dot_nt(low, proj_ref[...]).astype(BF)
    row = lax.broadcasted_iota(jnp.int32, sums_ref.shape, 0)
    gain_sum = jnp.sum(grad_mid * normed, axis=0, keepdims=True)
    bias_sum = jnp.sum(grad_mid, axis=0, keepdims=True)
    sums = jnp.where(row == 0, gain_sum, jnp.where(row == 1, bias_sum, 0.0))

    @pl.when(pl.program_id(0) == 0)
    def _():
        sums_ref[...] = sums

    @pl.when(pl.program_id(0) > 0)
    def _():
        sums_ref[...] += sums


def combine(places, backs, grad_logits, full, after_attention, cot_pad, gain, images):
    rows, width = after_attention.shape
    block = lambda cols: pl.BlockSpec((PAD_SEQ, cols), lambda i: (i, 0))
    held = lambda a: pl.BlockSpec(a.shape, lambda i: (0, 0))
    return pl.pallas_call(
        combine_kernel,
        grid=(images,),
        in_specs=[
            block(LANES),
            held(backs[0]),
            held(backs[1]),
            block(LANES),
            pl.BlockSpec((width, LANES), lambda i: (0, 4 * width // LANES)),
            pl.BlockSpec((width, width), lambda i: (0, 3)),
            block(width),
            block(width),
            pl.BlockSpec((1, width), lambda i: (0, 0)),
        ],
        out_specs=[block(width)] * 3 + [pl.BlockSpec((8, width), lambda i: (0, 0))],
        out_shape=[
            jax.ShapeDtypeStruct((rows, width), F32),
            jax.ShapeDtypeStruct((rows, width), BF),
            jax.ShapeDtypeStruct((rows, width), BF),
            jax.ShapeDtypeStruct((8, width), F32),
        ],
        compiler_params=pltpu.CompilerParams(vmem_limit_bytes=VMEM_LIMIT),
        cost_estimate=pl.CostEstimate(
            flops=28 * rows * width * width, bytes_accessed=rows * width, transcendentals=0
        ),
    )(places, *backs, grad_logits, full, full, after_attention, cot_pad, gain.reshape(1, -1))


def axis_bits(size):
    return [1 << b for b in range(size.bit_length() - 1)]


def exchange(value, axis, bit):
    size = lax.axis_size(axis)
    return lax.ppermute(value, axis, [(i, i ^ bit) for i in range(size)])


def bit_of(axis, bit):
    return (lax.axis_index(axis) // bit) % 2


def in_order(axis, bit, held, got):
    return jnp.where(bit_of(axis, bit) == 0, jnp.stack([held, got]), jnp.stack([got, held]))


def gather_pieces(block, axis):
    pieces = {0: block}
    for bit in reversed(axis_bits(lax.axis_size(axis))):
        for k in list(pieces):
            pieces[k | bit] = exchange(pieces[k], axis, bit)
    return [pieces[k] for k in sorted(pieces)]


def reduce_cores(away, keep):
    return (keep.astype(F32) + exchange(away, "shard", 1).astype(F32)).astype(BF)


def halve(held, bit):
    view = held.reshape((-1, 2) + held.shape[1:])
    mine = bit_of("shard", bit)
    pick = lambda at: lax.dynamic_index_in_dim(view, at, 1, keepdims=False)
    return pick(1 - mine).astype(BF), pick(mine).astype(F32)


def reduce_chips(send, stay):
    bits = axis_bits(lax.axis_size("shard"))[1:]
    for at, bit in enumerate(bits):
        held = stay + exchange(send, "shard", bit).astype(F32)
        if at + 1 < len(bits):
            send, stay = halve(held, bits[at + 1])
    return held[0]


def over_owners_by_halves(held):
    owners = lax.axis_size("expert")
    cols = held.shape[1]
    groups = [list(range(low, owners, 2)) for low in range(2)]
    spread = lambda parts: lax.all_to_all(
        parts, "expert", split_axis=0, concat_axis=0, tiled=True, axis_index_groups=groups
    )
    view = held.reshape(2, -1, cols)
    mine = bit_of("expert", 1)
    send = lax.dynamic_index_in_dim(view, 1 - mine, 0, keepdims=False).astype(BF)
    stay = lax.dynamic_index_in_dim(view, mine, 0, keepdims=False)
    held = (stay + exchange(send, "expert", 1).astype(F32)).astype(BF)
    got = spread(held.reshape(owners // 2, -1, cols))
    total = jnp.sum(got.astype(F32), axis=0).astype(BF)
    held = spread(jnp.broadcast_to(total[None], got.shape)).reshape(-1, cols)
    held = in_order("expert", 1, held, exchange(held, "expert", 1))
    return held.reshape(-1, cols)


def owners_parts(held):
    owners = lax.axis_size("expert")
    rows, cols = held.shape
    got = trade(held.astype(BF).reshape(owners, rows // owners, cols))
    return jnp.sum(got.astype(F32), axis=0).astype(BF)


def owners_all(part):
    owners = lax.axis_size("expert")
    rows, cols = part.shape
    return trade(jnp.broadcast_to(part[None], (owners, rows, cols))).reshape(owners * rows, cols)


def trade(view):
    return lax.all_to_all(view, "expert", split_axis=0, concat_axis=0, tiled=True)


def tie(*values):
    return lax.optimization_barrier(values)


def body(
    tokens, routes, capacity, ln1_gain, ln1_bias, ln2_gain, ln2_bias,
    w_qkv, w_proj, w_router, w_in, w_out, cotangent,
):
    count, width = tokens.shape
    experts = capacity.shape[0]
    owners = lax.axis_size("expert")
    shards = lax.axis_size("shard")
    images = count // SEQ
    padded = images * PAD_SEQ
    slot_count = 8 * ((2 * count + 8 * experts - 1) // (8 * experts))
    all_tokens = count * owners * shards
    me = lax.axis_index("expert").astype(jnp.int32).reshape(1)

    def pad_rows(values, fill=0):
        spread = values.reshape((images, SEQ) + values.shape[1:])
        room = [(0, 0), (0, PAD_SEQ - SEQ)] + [(0, 0)] * (values.ndim - 1)
        return jnp.pad(spread, room, constant_values=fill).reshape((padded,) + values.shape[1:])

    def cut_rows(values):
        spread = values.reshape((images, PAD_SEQ) + values.shape[1:])
        return spread[:, :SEQ].reshape((count,) + values.shape[1:])

    labels = jnp.arange(experts, dtype=jnp.int32)[:, None]
    first, second = routes[:, 0][None, :], routes[:, 1][None, :]
    hit_first, hit_second = first == labels, second == labels
    hits = jnp.concatenate([hit_first, hit_second], axis=0).astype(BF)
    order = lax.broadcasted_iota(jnp.int32, (count, count), 0) < lax.broadcasted_iota(
        jnp.int32, (count, count), 1
    )
    before = dot_nn(hits, order.astype(BF))
    totals = jnp.sum(hits.astype(F32), axis=1, keepdims=True)
    before_first = before[:experts]

    counts = (totals[:experts] + totals[experts:]).reshape(1, experts)
    high = jnp.floor(counts * (1.0 / COUNT_BASE))
    note = jnp.concatenate([high, counts - COUNT_BASE * high], axis=1).astype(BF)
    note = jnp.pad(note, ((0, w_router.shape[0] - 1), (0, 0)))
    room = jnp.zeros((w_router.shape[0], LANES - 3 * experts), BF)
    pieces = gather_pieces(
        jnp.concatenate([w_qkv, w_proj, w_router, note, room], axis=1), "shard"
    )

    before_second = before[experts:] + totals[:experts]
    limits = capacity[:, None].astype(F32)

    def slots(hit, ahead, choice):
        slot = jnp.sum(jnp.where(hit, ahead, 0.0), axis=0)
        limit = jnp.sum(jnp.where(hit, limits, 0.0), axis=0)
        kept = slot < limit
        slot = slot.astype(jnp.int32)
        return choice[0], slot, kept

    choices = [slots(hit_first, before_first, first), slots(hit_second, before_second, second)]
    head = 8 * ((slot_count + 15) // 16)
    spans = ((0, head), (head, slot_count - head))

    def chosen(start, size):
        found = []
        for choice, slot, kept in choices:
            inside = slot - start
            valid = kept & (inside >= 0) & (inside < size)
            found.append(pad_rows(jnp.where(valid, choice * size + inside, -1), -1))
        return found

    def selector(start, size):
        at = lax.broadcasted_iota(jnp.int32, (experts * size, 1), 0)
        first, second = chosen(start, size)
        return ((at == first[None, :]) | (at == second[None, :])).astype(BF)

    def send(select, rows):
        return dot_nn(select, rows).astype(BF).reshape(experts, -1, width)

    select_all = selector(0, slot_count)
    select = [selector(start, size) for start, size in spans]
    cot_pad = pad_rows(cotangent)
    cot_rows = trade(send(select_all, cot_pad))

    tok_pad = pad_rows(tokens)
    first_low, qkv_rows, heads_out, full = attend(tok_pad, ln1_gain, ln1_bias, pieces, images)
    proj_full = full[:, 3 * width : 4 * width]
    router_full = full[:, 4 * width :]
    notes = router_full[:: width // shards, experts : 3 * experts].astype(F32)
    notes = jnp.sum(notes, axis=0, keepdims=True)
    counts = COUNT_BASE * notes[:, :experts] + notes[:, experts:]
    counts = jnp.pad(counts, ((0, 0), (0, LANES - experts)))
    for bit in axis_bits(owners):
        counts = counts + exchange(counts, "expert", bit)
    route_share = counts[:, :experts] / (2.0 * all_tokens)
    token_rows = tok_pad.astype(F32)
    after_attention = token_rows + dot_nn(heads_out, proj_full)
    normed_two, inverse_two = norm_rows(after_attention)
    mid_low = (normed_two * ln2_gain + ln2_bias).astype(BF)

    sent, cot_rows, route_share = tie(send(select[0], mid_low), cot_rows, route_share)
    arrived = [trade(sent)]
    sent, arrived[0] = tie(send(select[1], mid_low), arrived[0])
    arrived.append(trade(sent))
    logits = dot_nn(mid_low, router_full)[:, :experts]
    live = (lax.broadcasted_iota(jnp.int32, (padded, 1), 0) % PAD_SEQ) < SEQ
    gate_probs = jnp.where(live, jax.nn.softmax(logits, axis=-1), 0.0)
    push = LOSS_WEIGHT * experts * route_share / all_tokens
    grad_logits = gate_probs * (push - jnp.sum(gate_probs * push, axis=-1, keepdims=True))
    grad_logits = jnp.pad(grad_logits, ((0, 0), (0, LANES - experts))).astype(BF)
    own = width // shards
    prob_sum = jnp.tile(jnp.pad(jnp.sum(gate_probs, axis=0), (0, own - experts)), shards)
    small = jnp.concatenate([prob_sum[None], dot_tn(grad_logits, mid_low)[:experts]], axis=0)
    small = jnp.pad(small, ((4, LANES - 4 - small.shape[0]), (0, 0)))

    places = jnp.stack([p for span in spans for p in chosen(*span)], axis=0)
    places = jnp.pad(places, ((0, LANES - places.shape[0]), (0, 0)), constant_values=-1).T
    arrived[0], grad_logits, small, places = tie(arrived[0], grad_logits, small, places)
    made = [
        run_expert(
            me,
            arrived[i].reshape(-1, width),
            cot_rows, start, full, w_in[0], w_out[0], experts,
        )
        for i, (start, _) in enumerate(spans)
    ]
    hidden, grad_pre, grad_made, gated, grad_rows, router_parts = zip(*made)
    grad_rows = [g.reshape(experts, -1, width) for g in grad_rows]
    backs = [trade(grad_rows[0])]
    gated = jnp.concatenate([g.reshape(experts, -1, width) for g in gated], axis=1)
    sent, backs[0], gated = tie(grad_rows[1], backs[0], gated)
    backs.append(trade(sent))
    mids = [a.reshape(-1, width) for a in arrived]
    mids[0], backs[0] = tie(mids[0], backs[0])
    core = (lax.axis_index("shard") % 2).astype(jnp.int32).reshape(1)
    in_away, in_keep, out_away, out_keep = weight_grads(
        core, mids, grad_made, grad_pre, hidden, shards
    )
    parts = router_parts[0] + router_parts[1]
    small = small + jnp.pad(parts[: LANES - 5], ((5, 0), (0, 0)))
    gated, backs[1], in_keep, out_keep, small = tie(gated, backs[1], in_keep, out_keep, small)
    returned = trade(gated)

    backs = [b.reshape(-1, width) for b in backs]
    grad_after, grad_heads, grad_heads_out, sums_two = combine(
        places, backs, grad_logits, full, after_attention, cot_pad, ln2_gain, images
    )
    back = functools.partial(
        attend_back, core, qkv_rows, grad_heads_out, full, first_low, images, shards
    )
    grad_first, *share = back(0, (heads_out, grad_heads), False)
    send, stay = halve(reduce_cores(*share), 2)
    total = reduce_chips(send, stay)
    rest = (grad_first, tok_pad, grad_after, ln1_gain.reshape(1, -1), sums_two, small)
    grad_tokens, *share = back(1, rest, True)
    share[0], share[1], returned, total = tie(*share, returned, total)
    send, stay = halve(reduce_cores(*share), 2)
    total, send = tie(total, send)
    last = reduce_chips(send, stay)
    last, in_keep, out_keep = tie(last, in_keep, out_keep)
    grad_expert_in = reduce_chips(*halve(reduce_cores(in_away, in_keep), 2))
    part = owners_parts(last)
    grad_expert_out = reduce_chips(*halve(reduce_cores(out_away, out_keep), 2))
    reduced = [over_owners_by_halves(total), owners_all(part)]
    grad_tokens = cut_rows(grad_tokens)

    mixed = cut_rows(after_attention + dot_tn(select_all, returned.reshape(-1, width))).astype(BF)
    grad_qkv_weight, proj_total, vectors, balance_loss = assemble(
        *reduced, route_share, experts / all_tokens
    )
    balance_loss = balance_loss[0, 0]
    vectors = vectors[:, :own]
    return (
        mixed,
        balance_loss,
        grad_tokens,
        vectors[0],
        vectors[1],
        vectors[2],
        vectors[3],
        grad_qkv_weight,
        proj_total,
        vectors[5 : 5 + experts].T,
        grad_expert_in[None],
        grad_expert_out[None],
    )


def solution(mesh):
    rows = P(("expert", "shard"), None)
    in_specs = (
        rows, rows, P(), P(), P(), P(), P(),
        P("shard", None), P("shard", None), P("shard", None),
        P("expert", None, None), P("expert", None, None), rows,
    )
    out_specs = (
        rows, P(), rows, P("shard"), P("shard"), P("shard"), P("shard"),
        P("shard", None), P("shard", None), P("shard", None),
        P("expert", None, "shard"), P("expert", "shard", None),
    )
    return jax.shard_map(body, mesh=mesh, in_specs=in_specs, out_specs=out_specs, check_vma=False)
```

```python
import functools
import math

import jax
import jax.numpy as jnp
from jax import lax
from jax.experimental import pallas as pl
from jax.experimental.pallas import tpu as pltpu
from jax.sharding import PartitionSpec as P

HEADS = 12
SEQ = 197
PAD_SEQ = 208
LANES = 128

NORM_EPS = 1e-06
LOSS_WEIGHT = 0.01
NEG = -1e30
COUNT_BASE = 128
VMEM_LIMIT = 56 * 1024 * 1024
BF = jnp.bfloat16
F32 = jnp.float32


def dot_nn(left, right):
    return lax.dot_general(left, right, (((1,), (0,)), ((), ())), preferred_element_type=F32)


def dot_nt(left, right):
    return lax.dot_general(left, right, (((1,), (1,)), ((), ())), preferred_element_type=F32)


def dot_tn(left, right):
    return lax.dot_general(left, right, (((0,), (0,)), ((), ())), preferred_element_type=F32)


def norm_rows(values):
    row_mean = jnp.mean(values, axis=-1, keepdims=True)
    centered = values - row_mean
    variance = jnp.mean(centered * centered, axis=-1, keepdims=True)
    inverse = lax.rsqrt(variance + NORM_EPS)
    return centered * inverse, inverse


def norm_back(grad_rows, normed, inverse, norm_gain):
    scaled = grad_rows * norm_gain
    return inverse * (
        scaled
        - jnp.mean(scaled, axis=-1, keepdims=True)
        - normed * jnp.mean(scaled * normed, axis=-1, keepdims=True)
    )


def attend_kernel(tok_ref, gain_ref, bias_ref, *refs, shards):
    pieces, refs = refs[:shards], refs[shards:]
    first_ref, qkv_ref, heads_ref, full_ref, w_ref, sems = refs
    step = pl.program_id(0)
    width = tok_ref.shape[1]
    own = width // shards
    me = lax.axis_index("shard")

    def place(k):
        at = 0
        for bit in axis_bits(shards):
            mine = lax.rem(me // bit, 2)
            at = at + bit * (1 - mine if k & bit else mine)
        rows = pl.ds(pl.multiple_of(at * own, own), own)
        return pltpu.make_async_copy(pieces[k], w_ref.at[rows, :], sems.at[k])

    whole_copy = pltpu.make_async_copy(w_ref, full_ref, sems.at[shards])

    @pl.when(step == 0)
    def _():
        for k in range(shards):
            place(k).start()

    normed, _ = norm_rows(tok_ref[...].astype(F32))
    first = (normed * gain_ref[...] + bias_ref[...]).astype(BF)
    first_ref[...] = first

    @pl.when(step == 0)
    def _():
        for k in range(shards):
            place(k).wait()
        whole_copy.start()

    for part in range(3):
        cols = slice(part * width, (part + 1) * width)
        qkv_ref[:, cols] = dot_nn(first, w_ref[:, cols]).astype(BF)
    rows = tok_ref.shape[0]
    lane = lax.broadcasted_iota(jnp.int32, (rows, LANES), 1)
    key_at = lax.broadcasted_iota(jnp.int32, (rows, rows), 1)
    scale = 1.0 / math.sqrt(width // HEADS)
    for pair in range(width // LANES):
        queries = qkv_ref[:, pair * LANES : (pair + 1) * LANES]
        keys = qkv_ref[:, width + pair * LANES : width + (pair + 1) * LANES]
        values = qkv_ref[:, 2 * width + pair * LANES : 2 * width + (pair + 1) * LANES]
        mixed = None
        for half in range(2):
            mine = (lane < LANES // 2) if half == 0 else (lane >= LANES // 2)
            zero = jnp.zeros_like(queries)
            scores = dot_nt(jnp.where(mine, queries, zero), keys) * scale
            scores = jnp.where(key_at < SEQ, scores, NEG)
            peak = jnp.max(scores, axis=-1, keepdims=True)
            weights = jnp.exp(scores - peak)
            total = jnp.sum(weights, axis=-1, keepdims=True)
            weights = (weights / total).astype(BF)
            term = dot_nn(weights, jnp.where(mine, values, zero))
            mixed = term if mixed is None else mixed + term
        heads_ref[:, pair * LANES : (pair + 1) * LANES] = mixed.astype(BF)

    @pl.when(step == pl.num_programs(0) - 1)
    def _():
        whole_copy.wait()


def attend(tok_pad, gain, bias, pieces, images):
    rows, width = tok_pad.shape
    shards = len(pieces)
    own, cols = pieces[0].shape
    whole = lambda i: (0, 0)
    block = lambda i: (i, 0)
    return pl.pallas_call(
        functools.partial(attend_kernel, shards=shards),
        grid=(images,),
        in_specs=[
            pl.BlockSpec((PAD_SEQ, width), block),
            pl.BlockSpec((1, width), whole),
            pl.BlockSpec((1, width), whole),
        ]
        + [pl.BlockSpec(memory_space=pl.ANY)] * shards,
        out_specs=[
            pl.BlockSpec((PAD_SEQ, width), block),
            pl.BlockSpec((PAD_SEQ, 3 * width), block),
            pl.BlockSpec((PAD_SEQ, width), block),
            pl.BlockSpec(memory_space=pl.ANY),
        ],
        out_shape=[
            jax.ShapeDtypeStruct((rows, width), BF),
            jax.ShapeDtypeStruct((rows, 3 * width), BF),
            jax.ShapeDtypeStruct((rows, width), BF),
            jax.ShapeDtypeStruct((shards * own, cols), BF),
        ],
        scratch_shapes=[
            pltpu.VMEM((shards * own, cols), BF),
            pltpu.SemaphoreType.DMA((shards + 1,)),
        ],
        compiler_params=pltpu.CompilerParams(vmem_limit_bytes=VMEM_LIMIT),
        cost_estimate=pl.CostEstimate(
            flops=rows * width * width, bytes_accessed=rows * width, transcendentals=0
        ),
    )(tok_pad, gain.reshape(1, -1), bias.reshape(1, -1), *pieces)


def owner_block(group, at, place):
    core, chip = place[0], place[1]
    return 4 * at + 2 * (chip if group % 2 else 1 - chip) + (core if group > 1 else 1 - core)


def heads_back(q_ref, k_ref, v_ref, g_ref, out_ref, at_rows, scale):
    rows, cols = q_ref.shape
    lane = lax.broadcasted_iota(jnp.int32, (rows, LANES), 1)
    key_at = lax.broadcasted_iota(jnp.int32, (rows, rows), 0)
    for pair in range(cols // LANES):
        at = slice(pair * LANES, (pair + 1) * LANES)
        queries, keys, values, grads = q_ref[:, at], k_ref[:, at], v_ref[:, at], g_ref[:, at]
        zero = jnp.zeros_like(queries)
        sums = None
        for half in range(2):
            mine = (lane < LANES // 2) if half == 0 else (lane >= LANES // 2)
            q_half = jnp.where(mine, queries, zero)
            g_half = jnp.where(mine, grads, zero)
            scores = dot_nt(keys, q_half) * scale
            scores = jnp.where(key_at < SEQ, scores, NEG)
            peak = jnp.max(scores, axis=0, keepdims=True)
            weights = jnp.exp(scores - peak)
            probs = weights / jnp.sum(weights, axis=0, keepdims=True)
            grad_attention = dot_nt(values, g_half)
            inner = jnp.sum(probs * grad_attention, axis=0, keepdims=True)
            grad_scores = (probs * (grad_attention - inner)).astype(BF)
            terms = (
                dot_tn(grad_scores, jnp.where(mine, keys, zero)),
                dot_nn(grad_scores, q_half),
                dot_nn(probs.astype(BF), g_half),
            )
            sums = terms if sums is None else tuple(a + b for a, b in zip(sums, terms))
        for part, value in enumerate((sums[0] * scale, sums[1] * scale, sums[2])):
            start = part * cols + pair * LANES
            out_ref[at_rows, start : start + LANES] = value.astype(BF)


def attend_back_kernel(
    core_ref, q_ref, k_ref, v_ref, g_ref, wq_ref, wk_ref, wv_ref, *refs, scale, final
):
    step = pl.program_id(0)
    rows, cols = q_ref.shape
    at_rows = pl.ds(pl.multiple_of(step * rows, rows), rows)
    late = 1 if final else 3
    sources, refs = refs[:late], refs[late:]
    held, sems, refs = refs[-late - 1 : -1], refs[-1], refs[: -late - 1]
    copies = [
        pltpu.make_async_copy(source, target, sems.at[at])
        for at, (source, target) in enumerate(zip(sources, held))
    ]

    @pl.when(step == 0)
    def _():
        for copy in copies:
            copy.start()

    if final:
        before_ref, tok_ref, after_ref, gain_ref, two_ref, vec_ref = refs[:6]
        out_ref, *share_refs, grads_ref, whole_ref, sums_ref = refs[6:]
    else:
        out_ref, *share_refs, grads_ref, whole_ref = refs
    heads_back(q_ref, k_ref, v_ref, g_ref, grads_ref, at_rows, scale)
    grad_first = None
    for part, w_ref in enumerate((wq_ref, wk_ref, wv_ref)):
        term = dot_nt(grads_ref[at_rows, part * cols : (part + 1) * cols], w_ref[...])
        grad_first = term if grad_first is None else grad_first + term
    if final:
        grad_first = grad_first + before_ref[...]
        normed, inverse = norm_rows(tok_ref[...].astype(F32))
        grad = after_ref[...] + norm_back(grad_first, normed, inverse, gain_ref[...])
        for image in range(out_ref.shape[0] // SEQ):

            @pl.when(step == image)
            def _():
                out_ref[image * SEQ : (image + 1) * SEQ, :] = grad[:SEQ]

        row = lax.broadcasted_iota(jnp.int32, sums_ref.shape, 0)
        gain_sum = jnp.sum(grad_first * normed, axis=0, keepdims=True)
        bias_sum = jnp.sum(grad_first, axis=0, keepdims=True)
        sums = jnp.where(row == 0, gain_sum, jnp.where(row == 1, bias_sum, 0.0))
        sums_ref[...] = jnp.where(step == 0, sums, sums_ref[...] + sums)
    else:
        out_ref[...] = grad_first

    @pl.when(step == pl.num_programs(0) - 1)
    def _():
        for copy in copies:
            copy.wait()
        whole_ref[:, : 3 * cols] = dot_tn(held[0][...], grads_ref[...])
        if final:
            sums = sums_ref[...] + pltpu.roll(two_ref[...], 2, 0)
            rest = jnp.zeros((LANES - sums.shape[0], sums.shape[1]), F32)
            whole_ref[:, 3 * cols :] = (jnp.concatenate([sums, rest], axis=0) + vec_ref[...]).T
        else:
            whole_ref[:, 3 * cols :] = dot_tn(held[1][...], held[2][...])
        count, own, _ = share_refs[0].shape
        for group, share_ref in enumerate(share_refs):
            for at in range(count):
                block = owner_block(group, at, core_ref)
                rows_of = pl.ds(pl.multiple_of(block * own, own), own)
                share_ref[at] = whole_ref[rows_of, :].astype(BF)


def attend_back(core, qkv, grad_heads_out, full, first, images, shards, group, extra, final):
    rows, width = grad_heads_out.shape
    cols = width // 2
    wide = 3 * cols + (LANES if final else width)
    own = width // shards
    late = 1 if final else 3
    at = lambda part: pl.BlockSpec((PAD_SEQ, cols), lambda i: (i, 2 * part + group))
    weight = lambda part: pl.BlockSpec((width, cols), lambda i: (0, 2 * part + group))
    held = lambda a: pl.BlockSpec(a.shape, lambda i: (0, 0))
    block = pl.BlockSpec((PAD_SEQ, width), lambda i: (i, 0))
    share = pl.BlockSpec((shards // 4, own, wide), lambda i: (0, 0, 0))
    share_shape = jax.ShapeDtypeStruct((shards // 4, own, wide), BF)
    return pl.pallas_call(
        functools.partial(
            attend_back_kernel, scale=1.0 / math.sqrt(width // HEADS), final=final
        ),
        grid=(images,),
        in_specs=[pl.BlockSpec(memory_space=pltpu.SMEM), at(0), at(1), at(2), at(0)]
        + [weight(0), weight(1), weight(2)]
        + [pl.BlockSpec(memory_space=pl.ANY)] * late
        + ([block, block, block] + [held(a) for a in extra[3:]] if final else []),
        out_specs=[
            pl.BlockSpec((images * SEQ, width), lambda i: (0, 0)) if final else block,
        ]
        + [share] * 4,
        out_shape=[
            jax.ShapeDtypeStruct((images * SEQ if final else rows, width), F32),
        ]
        + [share_shape] * 4,
        scratch_shapes=[pltpu.VMEM((rows, 3 * cols), BF), pltpu.VMEM((width, wide), F32)]
        + ([pltpu.VMEM((8, width), F32)] if final else [])
        + [pltpu.VMEM((rows, width), BF)] * late
        + [pltpu.SemaphoreType.DMA((late,))],
        compiler_params=pltpu.CompilerParams(vmem_limit_bytes=VMEM_LIMIT),
        cost_estimate=pl.CostEstimate(
            flops=40 * rows * PAD_SEQ * cols,
            bytes_accessed=rows * cols,
            transcendentals=0,
        ),
    )(core, qkv, qkv, qkv, grad_heads_out, full, full, full, first, *extra)


def assemble_kernel(left_ref, right_ref, share_ref, qkv_ref, proj_ref, small_ref, loss_ref, *, scale):
    rows, width = proj_ref.shape
    cols = width // 2
    for part in range(3):
        at = slice(part * cols, (part + 1) * cols)
        qkv_ref[:, part * width : part * width + cols] = left_ref[:, at].astype(F32)
        qkv_ref[:, part * width + cols : (part + 1) * width] = right_ref[:rows, at].astype(F32)
    proj_ref[...] = left_ref[:, 3 * cols :].astype(F32)
    small = right_ref[:, 3 * cols :].astype(F32).T
    small_ref[...] = small
    product = small[4:5, :LANES] * share_ref[...]
    loss_ref[...] = jnp.broadcast_to(jnp.sum(product, axis=-1, keepdims=True) * scale, (1, LANES))


def assemble(left, right, route_share, scale):
    rows = left.shape[0]
    width = 2 * left.shape[1] // 5
    spec = pl.BlockSpec(memory_space=pltpu.VMEM)
    padded = max(rows, LANES)
    share = jnp.pad(route_share, ((0, 0), (0, LANES - route_share.shape[1])))
    right = jnp.pad(right, ((0, padded - rows), (0, 0)))
    return pl.pallas_call(
        functools.partial(assemble_kernel, scale=scale),
        in_specs=[spec] * 3,
        out_specs=[spec] * 4,
        out_shape=[
            jax.ShapeDtypeStruct((rows, 3 * width), F32),
            jax.ShapeDtypeStruct((rows, width), F32),
            jax.ShapeDtypeStruct((LANES, padded), F32),
            jax.ShapeDtypeStruct((1, LANES), F32),
        ],
    )(left, right, share)


def expert_kernel(
    me_ref, x_ref, cots_ref, wr_ref, win_ref, wout_ref, win_rows_ref, wout_cols_ref,
    hid_ref, gp_ref, gm_ref, mg_ref, rows_ref, gr_ref,
    hid_all, gp_all, p_ref, gain_ref, routed_ref, c_ref,
    *, experts, up_steps, down_steps, start,
):
    step = pl.program_id(0)
    rows = x_ref.shape[0]
    tile = win_ref.shape[1]
    piece = win_rows_ref.shape[0]
    lane = lax.broadcasted_iota(jnp.int32, (rows, LANES), 1)
    mine = lane == me_ref[0]

    def gate():
        return jnp.sum(jnp.where(mine, p_ref[...], 0.0), axis=-1, keepdims=True)

    @pl.when(step == 0)
    def _():
        logits = jnp.where(lane < experts, dot_nn(x_ref[...], wr_ref[...]), NEG)
        top = jnp.max(logits, axis=-1, keepdims=True)
        weights = jnp.exp(logits - top)
        p_ref[...] = weights / jnp.sum(weights, axis=-1, keepdims=True)
        size = rows // cots_ref.shape[0]
        cots = cots_ref[:, start : start + size, :].astype(F32).reshape(rows, -1)
        c_ref[...] = cots.astype(BF)
        gm_ref[...] = (gate() * cots).astype(BF)

    @pl.when(step < up_steps)
    def _():
        col = pl.ds(pl.multiple_of(step * tile, tile), tile)
        pre = dot_nn(x_ref[...], win_ref[...])
        back = dot_nt(gm_ref[...], wout_ref[...])
        cdf = 0.5 * (1.0 + lax.erf(pre * (1.0 / math.sqrt(2.0))))
        density = jnp.exp(-0.5 * pre * pre) * (1.0 / math.sqrt(2.0 * math.pi))
        hidden = (pre * cdf).astype(BF)
        grad_pre = (back * (cdf + pre * density)).astype(BF)
        hid_ref[...] = hidden
        gp_ref[...] = grad_pre
        hid_all[:, col] = hidden
        gp_all[:, col] = grad_pre

    @pl.when((step >= up_steps) & (step < up_steps + down_steps))
    def _():
        part = step - up_steps
        col = pl.ds(pl.multiple_of(part * piece, piece), piece)
        made = dot_nn(hid_all[...], wout_cols_ref[...])
        mg_ref[...] = (gate() * made).astype(BF)
        gain = c_ref[:, col].astype(F32) * made.astype(BF).astype(F32)
        gain = jnp.broadcast_to(jnp.sum(gain, axis=-1, keepdims=True), (rows, LANES))
        gain_ref[...] = jnp.where(part == 0, gain, gain_ref[...] + gain)

    @pl.when(step == up_steps + down_steps)
    def _():
        probs = p_ref[...]
        routed = gain_ref[...] * gate() * (jnp.where(mine, 1.0, 0.0) - probs)
        routed_ref[...] = routed.astype(BF)
        gr_ref[...] = dot_tn(routed_ref[...], x_ref[...])

    @pl.when(step >= up_steps + down_steps)
    def _():
        part = step - up_steps - down_steps
        router = wr_ref[pl.ds(pl.multiple_of(part * piece, piece), piece), :]
        back = dot_nt(gp_all[...], win_rows_ref[...]) + dot_nt(routed_ref[...], router)
        rows_ref[...] = back.astype(BF)


def run_expert(me, x, cots, start, w_router, w_in, w_out, experts):
    rows, width = x.shape
    hidden = w_in.shape[1]
    tile, piece = 512, 256
    up_steps, down_steps = hidden // tile, width // piece
    whole = lambda j: (0, 0)
    up = lambda j: jnp.minimum(j, up_steps - 1)
    made = lambda j: jnp.clip(j - up_steps, 0, down_steps - 1)
    back = lambda j: jnp.clip(j - up_steps - down_steps, 0, down_steps - 1)
    big = jax.ShapeDtypeStruct((rows, hidden), BF)
    small = jax.ShapeDtypeStruct((rows, width), BF)
    return pl.pallas_call(
        functools.partial(
            expert_kernel, experts=experts, up_steps=up_steps, down_steps=down_steps, start=start
        ),
        grid=(up_steps + 2 * down_steps,),
        in_specs=[
            pl.BlockSpec(memory_space=pltpu.SMEM),
            pl.BlockSpec((rows, width), whole),
            pl.BlockSpec(cots.shape, lambda j: (0, 0, 0)),
            pl.BlockSpec((width, LANES), lambda j: (0, w_router.shape[1] // LANES - 1)),
            pl.BlockSpec((width, tile), lambda j: (0, up(j))),
            pl.BlockSpec((tile, width), lambda j: (up(j), 0)),
            pl.BlockSpec((piece, hidden), lambda j: (back(j), 0)),
            pl.BlockSpec((hidden, piece), lambda j: (0, made(j))),
        ],
        out_specs=[
            pl.BlockSpec((rows, tile), lambda j: (0, up(j))),
            pl.BlockSpec((rows, tile), lambda j: (0, up(j))),
            pl.BlockSpec((rows, width), whole),
            pl.BlockSpec((rows, piece), lambda j: (0, made(j))),
            pl.BlockSpec((rows, piece), lambda j: (0, back(j))),
            pl.BlockSpec((LANES, width), whole),
        ],
        out_shape=[big, big, small, small, small, jax.ShapeDtypeStruct((LANES, width), F32)],
        scratch_shapes=[
            pltpu.VMEM((rows, hidden), BF),
            pltpu.VMEM((rows, hidden), BF),
            pltpu.VMEM((rows, LANES), F32),
            pltpu.VMEM((rows, LANES), F32),
            pltpu.VMEM((rows, LANES), BF),
            pltpu.VMEM((rows, width), BF),
        ],
        compiler_params=pltpu.CompilerParams(vmem_limit_bytes=VMEM_LIMIT),
        cost_estimate=pl.CostEstimate(
            flops=16 * rows * width * hidden,
            bytes_accessed=rows * hidden,
            transcendentals=0,
        ),
    )(me, x, cots, w_router, w_in, w_out, w_in, w_out)


def weight_grad_kernel(place_ref, x_a, x_b, gm_a, gm_b, gp_a, gp_b, hid_a, hid_b, *out_refs):
    grad_in = (dot_tn(x_a[...], gp_a[...]) + dot_tn(x_b[...], gp_b[...])).astype(BF)
    grad_out = (dot_tn(hid_a[...], gm_a[...]) + dot_tn(hid_b[...], gm_b[...])).astype(BF)
    each = pl.num_programs(0) // 4
    for group in range(4):

        @pl.when(pl.program_id(0) // each == group)
        def _():
            out_refs[group][0] = grad_in
            out_refs[4 + group][0] = grad_out


def weight_grads(place, x, grad_made, grad_pre, hidden, shards):
    width, hid = x[0].shape[1], hidden[0].shape[1]
    tile, each = hid // shards, shards // 4
    count = x[0].shape[0] + x[1].shape[0]

    def source(j, place_ref):
        group, at = j // each, lax.rem(j, each)
        core = jnp.where(group > 1, place_ref[0], 1 - place_ref[0])
        chip = jnp.where(lax.rem(group, 2) == 1, place_ref[1], 1 - place_ref[1])
        return (0, 4 * at + 2 * chip + core)

    held = lambda a: pl.BlockSpec(a.shape, lambda j, place_ref: (0, 0))
    tiled = lambda a: pl.BlockSpec((a.shape[0], tile), source)

    def out(group, *block):
        at = lambda j, place_ref: (jnp.clip(j - group * each, 0, each - 1), 0, 0)
        return pl.BlockSpec((1,) + block, at)

    return pl.pallas_call(
        weight_grad_kernel,
        grid_spec=pltpu.PrefetchScalarGridSpec(
            num_scalar_prefetch=1,
            grid=(shards,),
            in_specs=[held(a) for a in (*x, *grad_made)]
            + [tiled(a) for a in (*grad_pre, *hidden)],
            out_specs=[out(group, width, tile) for group in range(4)]
            + [out(group, tile, width) for group in range(4)],
        ),
        out_shape=[jax.ShapeDtypeStruct((each, width, tile), BF)] * 4
        + [jax.ShapeDtypeStruct((each, tile, width), BF)] * 4,
        compiler_params=pltpu.CompilerParams(vmem_limit_bytes=VMEM_LIMIT),
        cost_estimate=pl.CostEstimate(
            flops=8 * count * width * hid, bytes_accessed=width * hid, transcendentals=0
        ),
    )(place, *x, *grad_made, *grad_pre, *hidden)


def combine_kernel(
    at_ref, back_a_ref, back_b_ref, glog_ref, router_ref, proj_ref, after_ref, cot_ref, gain_ref,
    grad_ref, low_ref, heads_ref, sums_ref,
):
    rows = at_ref.shape[0]

    def picked(first, back_ref):
        slot = lax.broadcasted_iota(jnp.int32, (rows, back_ref.shape[0]), 1)
        match = (slot == at_ref[:, first : first + 1]) | (slot == at_ref[:, first + 1 : first + 2])
        return dot_nn(jnp.where(match, 1.0, 0.0).astype(BF), back_ref[...])

    grad_mid = picked(0, back_a_ref) + picked(2, back_b_ref) + dot_nt(glog_ref[...], router_ref[...])
    normed, inverse = norm_rows(after_ref[...])
    grad = cot_ref[...].astype(F32) + norm_back(grad_mid, normed, inverse, gain_ref[...])
    grad_ref[...] = grad
    low = grad.astype(BF)
    low_ref[...] = low
    heads_ref[...] = dot_nt(low, proj_ref[...]).astype(BF)
    row = lax.broadcasted_iota(jnp.int32, sums_ref.shape, 0)
    gain_sum = jnp.sum(grad_mid * normed, axis=0, keepdims=True)
    bias_sum = jnp.sum(grad_mid, axis=0, keepdims=True)
    sums = jnp.where(row == 0, gain_sum, jnp.where(row == 1, bias_sum, 0.0))

    @pl.when(pl.program_id(0) == 0)
    def _():
        sums_ref[...] = sums

    @pl.when(pl.program_id(0) > 0)
    def _():
        sums_ref[...] += sums


def combine(places, backs, grad_logits, full, after_attention, cot_pad, gain, images):
    rows, width = after_attention.shape
    block = lambda cols: pl.BlockSpec((PAD_SEQ, cols), lambda i: (i, 0))
    held = lambda a: pl.BlockSpec(a.shape, lambda i: (0, 0))
    return pl.pallas_call(
        combine_kernel,
        grid=(images,),
        in_specs=[
            block(LANES),
            held(backs[0]),
            held(backs[1]),
            block(LANES),
            pl.BlockSpec((width, LANES), lambda i: (0, 4 * width // LANES)),
            pl.BlockSpec((width, width), lambda i: (0, 3)),
            block(width),
            block(width),
            pl.BlockSpec((1, width), lambda i: (0, 0)),
        ],
        out_specs=[block(width)] * 3 + [pl.BlockSpec((8, width), lambda i: (0, 0))],
        out_shape=[
            jax.ShapeDtypeStruct((rows, width), F32),
            jax.ShapeDtypeStruct((rows, width), BF),
            jax.ShapeDtypeStruct((rows, width), BF),
            jax.ShapeDtypeStruct((8, width), F32),
        ],
        compiler_params=pltpu.CompilerParams(vmem_limit_bytes=VMEM_LIMIT),
        cost_estimate=pl.CostEstimate(
            flops=28 * rows * width * width, bytes_accessed=rows * width, transcendentals=0
        ),
    )(places, *backs, grad_logits, full, full, after_attention, cot_pad, gain.reshape(1, -1))


def axis_bits(size):
    return [1 << b for b in range(size.bit_length() - 1)]


def exchange(value, axis, bit):
    size = lax.axis_size(axis)
    return lax.ppermute(value, axis, [(i, i ^ bit) for i in range(size)])


def bit_of(axis, bit):
    return (lax.axis_index(axis) // bit) % 2


def in_order(axis, bit, held, got):
    return jnp.where(bit_of(axis, bit) == 0, jnp.stack([held, got]), jnp.stack([got, held]))


def gather_pieces(block, axis):
    pieces = {0: block}
    for bit in reversed(axis_bits(lax.axis_size(axis))):
        for k in list(pieces):
            pieces[k | bit] = exchange(pieces[k], axis, bit)
    return [pieces[k] for k in sorted(pieces)]


def other_core(value):
    return exchange(value, "shard", 1)


def other_chip(value):
    return exchange(value, "shard", 2)


def other_chip_in_turns(far, near, turns=2):
    size = far.shape[1] // turns
    got = []
    for turn in range(turns):
        rows = slice(turn * size, (turn + 1) * size)
        send = (far[:, rows].astype(F32) + near[:, rows].astype(F32)).astype(BF)
        if got:
            send, got[-1] = tie(send, got[-1])
        got.append(other_chip(send))
    return jnp.concatenate(got, axis=1)


def reduce_chips(got, stay):
    held = stay + got.astype(F32)
    for bit in axis_bits(lax.axis_size("shard"))[2:]:
        view = held.reshape((-1, 2) + held.shape[1:])
        mine = bit_of("shard", bit)
        pick = lambda which: lax.dynamic_index_in_dim(view, which, 1, keepdims=False)
        held = pick(mine) + exchange(pick(1 - mine).astype(BF), "shard", bit).astype(F32)
    return held[0]


def owners_parts(held):
    owners = lax.axis_size("expert")
    rows, cols = held.shape
    got = trade(held.astype(BF).reshape(owners, rows // owners, cols))
    return jnp.sum(got.astype(F32), axis=0).astype(BF)


def owners_all(part):
    owners = lax.axis_size("expert")
    rows, cols = part.shape
    return trade(jnp.broadcast_to(part[None], (owners, rows, cols))).reshape(owners * rows, cols)


def owners_all_in_two(part):
    owners = lax.axis_size("expert")
    rows, cols = part.shape
    groups = [list(range(low, owners, 2)) for low in range(2)]
    held = lax.all_to_all(
        jnp.broadcast_to(part[None], (owners // 2, rows, cols)),
        "expert", split_axis=0, concat_axis=0, tiled=True, axis_index_groups=groups,
    )
    both = in_order("expert", 1, held, exchange(held, "expert", 1))
    return jnp.moveaxis(both, 0, 1).reshape(owners * rows, cols)


def trade(view):
    return lax.all_to_all(view, "expert", split_axis=0, concat_axis=0, tiled=True)


def tie(*values):
    return lax.optimization_barrier(values)


def body(
    tokens, routes, capacity, ln1_gain, ln1_bias, ln2_gain, ln2_bias,
    w_qkv, w_proj, w_router, w_in, w_out, cotangent,
):
    count, width = tokens.shape
    experts = capacity.shape[0]
    owners = lax.axis_size("expert")
    shards = lax.axis_size("shard")
    images = count // SEQ
    padded = images * PAD_SEQ
    slot_count = 8 * ((2 * count + 8 * experts - 1) // (8 * experts))
    all_tokens = count * owners * shards
    me = lax.axis_index("expert").astype(jnp.int32).reshape(1)

    def pad_rows(values, fill=0):
        spread = values.reshape((images, SEQ) + values.shape[1:])
        room = [(0, 0), (0, PAD_SEQ - SEQ)] + [(0, 0)] * (values.ndim - 1)
        return jnp.pad(spread, room, constant_values=fill).reshape((padded,) + values.shape[1:])

    def cut_rows(values):
        spread = values.reshape((images, PAD_SEQ) + values.shape[1:])
        return spread[:, :SEQ].reshape((count,) + values.shape[1:])

    labels = jnp.arange(experts, dtype=jnp.int32)[:, None]
    first, second = routes[:, 0][None, :], routes[:, 1][None, :]
    hit_first, hit_second = first == labels, second == labels
    hits = jnp.concatenate([hit_first, hit_second], axis=0).astype(BF)
    order = lax.broadcasted_iota(jnp.int32, (count, count), 0) < lax.broadcasted_iota(
        jnp.int32, (count, count), 1
    )
    before = dot_nn(hits, order.astype(BF))
    totals = jnp.sum(hits.astype(F32), axis=1, keepdims=True)
    before_first = before[:experts]

    counts = (totals[:experts] + totals[experts:]).reshape(1, experts)
    high = jnp.floor(counts * (1.0 / COUNT_BASE))
    note = jnp.concatenate([high, counts - COUNT_BASE * high], axis=1).astype(BF)
    note = jnp.pad(note, ((0, w_router.shape[0] - 1), (0, 0)))
    room = jnp.zeros((w_router.shape[0], LANES - 3 * experts), BF)
    pieces = gather_pieces(
        jnp.concatenate([w_qkv, w_proj, w_router, note, room], axis=1), "shard"
    )

    before_second = before[experts:] + totals[:experts]
    limits = capacity[:, None].astype(F32)

    def slots(hit, ahead, choice):
        slot = jnp.sum(jnp.where(hit, ahead, 0.0), axis=0)
        limit = jnp.sum(jnp.where(hit, limits, 0.0), axis=0)
        kept = slot < limit
        slot = slot.astype(jnp.int32)
        return choice[0], slot, kept

    choices = [slots(hit_first, before_first, first), slots(hit_second, before_second, second)]
    head = 8 * ((slot_count + 15) // 16)
    spans = ((0, head), (head, slot_count - head))

    def chosen(start, size):
        found = []
        for choice, slot, kept in choices:
            inside = slot - start
            valid = kept & (inside >= 0) & (inside < size)
            found.append(pad_rows(jnp.where(valid, choice * size + inside, -1), -1))
        return found

    def selector(start, size):
        at = lax.broadcasted_iota(jnp.int32, (experts * size, 1), 0)
        first, second = chosen(start, size)
        return ((at == first[None, :]) | (at == second[None, :])).astype(BF)

    def send(select, rows):
        return dot_nn(select, rows).astype(BF).reshape(experts, -1, width)

    select_all = selector(0, slot_count)
    select = [selector(start, size) for start, size in spans]
    cot_pad = pad_rows(cotangent)
    cot_rows = trade(send(select_all, cot_pad))

    tok_pad = pad_rows(tokens)
    first_low, qkv_rows, heads_out, full = attend(tok_pad, ln1_gain, ln1_bias, pieces, images)
    proj_full = full[:, 3 * width : 4 * width]
    router_full = full[:, 4 * width :]
    notes = router_full[:: width // shards, experts : 3 * experts].astype(F32)
    notes = jnp.sum(notes, axis=0, keepdims=True)
    counts = COUNT_BASE * notes[:, :experts] + notes[:, experts:]
    counts = jnp.pad(counts, ((0, 0), (0, LANES - experts)))
    for bit in axis_bits(owners):
        counts = counts + exchange(counts, "expert", bit)
    route_share = counts[:, :experts] / (2.0 * all_tokens)
    token_rows = tok_pad.astype(F32)
    after_attention = token_rows + dot_nn(heads_out, proj_full)
    normed_two, inverse_two = norm_rows(after_attention)
    mid_low = (normed_two * ln2_gain + ln2_bias).astype(BF)

    sent, cot_rows, route_share = tie(send(select[0], mid_low), cot_rows, route_share)
    arrived = [trade(sent)]
    sent, arrived[0] = tie(send(select[1], mid_low), arrived[0])
    arrived.append(trade(sent))
    logits = dot_nn(mid_low, router_full)[:, :experts]
    live = (lax.broadcasted_iota(jnp.int32, (padded, 1), 0) % PAD_SEQ) < SEQ
    gate_probs = jnp.where(live, jax.nn.softmax(logits, axis=-1), 0.0)
    push = LOSS_WEIGHT * experts * route_share / all_tokens
    grad_logits = gate_probs * (push - jnp.sum(gate_probs * push, axis=-1, keepdims=True))
    grad_logits = jnp.pad(grad_logits, ((0, 0), (0, LANES - experts))).astype(BF)
    own = width // shards
    prob_sum = jnp.tile(jnp.pad(jnp.sum(gate_probs, axis=0), (0, own - experts)), shards)
    small = jnp.concatenate([prob_sum[None], dot_tn(grad_logits, mid_low)[:experts]], axis=0)
    small = jnp.pad(small, ((4, LANES - 4 - small.shape[0]), (0, 0)))

    places = jnp.stack([p for span in spans for p in chosen(*span)], axis=0)
    places = jnp.pad(places, ((0, LANES - places.shape[0]), (0, 0)), constant_values=-1).T
    arrived[0], grad_logits, small, places = tie(arrived[0], grad_logits, small, places)
    made = [
        run_expert(
            me,
            arrived[i].reshape(-1, width),
            cot_rows, start, full, w_in[0], w_out[0], experts,
        )
        for i, (start, _) in enumerate(spans)
    ]
    hidden, grad_pre, grad_made, gated, grad_rows, router_parts = zip(*made)
    grad_rows = [g.reshape(experts, -1, width) for g in grad_rows]
    backs = [trade(grad_rows[0])]
    gated = jnp.concatenate([g.reshape(experts, -1, width) for g in gated], axis=1)
    sent, backs[0], gated = tie(grad_rows[1], backs[0], gated)
    backs.append(trade(sent))
    mids = [a.reshape(-1, width) for a in arrived]
    mids[0], backs[0] = tie(mids[0], backs[0])
    place = jnp.stack([bit_of("shard", 1), bit_of("shard", 2)]).astype(jnp.int32)
    grads = weight_grads(place, mids, grad_made, grad_pre, hidden, shards)
    ins, outs = list(grads[:4]), list(grads[4:])
    parts = router_parts[0] + router_parts[1]
    small = small + jnp.pad(parts[: LANES - 5], ((5, 0), (0, 0)))
    gated, backs[1], ins[3], outs[3], small = tie(gated, backs[1], ins[3], outs[3], small)
    returned = trade(gated)

    backs = [b.reshape(-1, width) for b in backs]
    grad_after, grad_heads, grad_heads_out, sums_two = combine(
        places, backs, grad_logits, full, after_attention, cot_pad, ln2_gain, images
    )
    back = functools.partial(
        attend_back, place, qkv_rows, grad_heads_out, full, first_low, images, shards
    )
    grad_first, *share = back(0, (heads_out, grad_heads), False)
    send = (share[2].astype(F32) + other_core(share[0]).astype(F32)).astype(BF)
    total = reduce_chips(other_chip(send), share[3].astype(F32) + other_core(share[1]).astype(F32))
    rest = (grad_first, tok_pad, grad_after, ln1_gain.reshape(1, -1), sums_two, small)
    grad_tokens, *share = back(1, rest, True)
    share[0], share[1], returned, total = tie(share[0], share[1], returned, total)
    send = (share[2].astype(F32) + other_core(share[0]).astype(F32)).astype(BF)
    total, send, ins[2], outs[2] = tie(total, send, ins[2], outs[2])
    part = owners_parts(total)
    last = reduce_chips(other_chip(send), share[3].astype(F32) + other_core(share[1]).astype(F32))
    last = owners_parts(last)
    grad_expert_in, grad_expert_out = [
        reduce_chips(
            other_chip_in_turns(g[2], other_core(g[0])), g[3].astype(F32) + other_core(g[1]).astype(F32),
        )
        for g in (ins, outs)
    ]
    reduced = [owners_all_in_two(part), owners_all(last)]

    mixed = cut_rows(after_attention + dot_tn(select_all, returned.reshape(-1, width))).astype(BF)
    grad_qkv_weight, proj_total, vectors, balance_loss = assemble(
        *reduced, route_share, experts / all_tokens
    )
    balance_loss = balance_loss[0, 0]
    vectors = vectors[:, :own]
    return (
        mixed,
        balance_loss,
        grad_tokens,
        vectors[0],
        vectors[1],
        vectors[2],
        vectors[3],
        grad_qkv_weight,
        proj_total,
        vectors[5 : 5 + experts].T,
        grad_expert_in[None],
        grad_expert_out[None],
    )


def solution(mesh):
    rows = P(("expert", "shard"), None)
    in_specs = (
        rows, rows, P(), P(), P(), P(), P(),
        P("shard", None), P("shard", None), P("shard", None),
        P("expert", None, None), P("expert", None, None), rows,
    )
    out_specs = (
        rows, P(), rows, P("shard"), P("shard"), P("shard"), P("shard"),
        P("shard", None), P("shard", None), P("shard", None),
        P("expert", None, "shard"), P("expert", "shard", None),
    )
    return jax.shard_map(body, mesh=mesh, in_specs=in_specs, out_specs=out_specs, check_vma=False)
```

```python
import functools
import math

import jax
import jax.numpy as jnp
from jax import lax
from jax.experimental import pallas as pl
from jax.experimental.pallas import tpu as pltpu
from jax.sharding import PartitionSpec as P

HEADS = 12
SEQ = 197
PAD_SEQ = 208
LANES = 128

NORM_EPS = 1e-06
LOSS_WEIGHT = 0.01
NEG = -1e30
COUNT_BASE = 128
VMEM_LIMIT = 56 * 1024 * 1024
BF = jnp.bfloat16
F32 = jnp.float32


def dot_nn(left, right):
    return lax.dot_general(left, right, (((1,), (0,)), ((), ())), preferred_element_type=F32)


def dot_nt(left, right):
    return lax.dot_general(left, right, (((1,), (1,)), ((), ())), preferred_element_type=F32)


def dot_tn(left, right):
    return lax.dot_general(left, right, (((0,), (0,)), ((), ())), preferred_element_type=F32)


def norm_rows(values):
    row_mean = jnp.mean(values, axis=-1, keepdims=True)
    centered = values - row_mean
    variance = jnp.mean(centered * centered, axis=-1, keepdims=True)
    inverse = lax.rsqrt(variance + NORM_EPS)
    return centered * inverse, inverse


def norm_back(grad_rows, normed, inverse, norm_gain):
    scaled = grad_rows * norm_gain
    return inverse * (
        scaled
        - jnp.mean(scaled, axis=-1, keepdims=True)
        - normed * jnp.mean(scaled * normed, axis=-1, keepdims=True)
    )


def attend_kernel(tok_ref, gain_ref, bias_ref, *refs, shards):
    pieces, refs = refs[:shards], refs[shards:]
    first_ref, qkv_ref, heads_ref, full_ref, w_ref, sems = refs
    step = pl.program_id(0)
    width = tok_ref.shape[1]
    own = width // shards
    me = lax.axis_index("shard")

    def place(k):
        at = 0
        for bit in axis_bits(shards):
            mine = lax.rem(me // bit, 2)
            at = at + bit * (1 - mine if k & bit else mine)
        rows = pl.ds(pl.multiple_of(at * own, own), own)
        return pltpu.make_async_copy(pieces[k], w_ref.at[rows, :], sems.at[k])

    whole_copy = pltpu.make_async_copy(w_ref, full_ref, sems.at[shards])

    @pl.when(step == 0)
    def _():
        for k in range(shards):
            place(k).start()

    normed, _ = norm_rows(tok_ref[...].astype(F32))
    first = (normed * gain_ref[...] + bias_ref[...]).astype(BF)
    first_ref[...] = first

    @pl.when(step == 0)
    def _():
        for k in range(shards):
            place(k).wait()
        whole_copy.start()

    for part in range(3):
        cols = slice(part * width, (part + 1) * width)
        qkv_ref[:, cols] = dot_nn(first, w_ref[:, cols]).astype(BF)
    rows = tok_ref.shape[0]
    lane = lax.broadcasted_iota(jnp.int32, (rows, LANES), 1)
    key_at = lax.broadcasted_iota(jnp.int32, (rows, rows), 1)
    scale = 1.0 / math.sqrt(width // HEADS)
    for pair in range(width // LANES):
        queries = qkv_ref[:, pair * LANES : (pair + 1) * LANES]
        keys = qkv_ref[:, width + pair * LANES : width + (pair + 1) * LANES]
        values = qkv_ref[:, 2 * width + pair * LANES : 2 * width + (pair + 1) * LANES]
        mixed = None
        for half in range(2):
            mine = (lane < LANES // 2) if half == 0 else (lane >= LANES // 2)
            zero = jnp.zeros_like(queries)
            scores = dot_nt(jnp.where(mine, queries, zero), keys) * scale
            scores = jnp.where(key_at < SEQ, scores, NEG)
            peak = jnp.max(scores, axis=-1, keepdims=True)
            weights = jnp.exp(scores - peak)
            total = jnp.sum(weights, axis=-1, keepdims=True)
            weights = (weights / total).astype(BF)
            term = dot_nn(weights, jnp.where(mine, values, zero))
            mixed = term if mixed is None else mixed + term
        heads_ref[:, pair * LANES : (pair + 1) * LANES] = mixed.astype(BF)

    @pl.when(step == pl.num_programs(0) - 1)
    def _():
        whole_copy.wait()


def attend(tok_pad, gain, bias, pieces, images):
    rows, width = tok_pad.shape
    shards = len(pieces)
    own, cols = pieces[0].shape
    whole = lambda i: (0, 0)
    block = lambda i: (i, 0)
    return pl.pallas_call(
        functools.partial(attend_kernel, shards=shards),
        grid=(images,),
        in_specs=[
            pl.BlockSpec((PAD_SEQ, width), block),
            pl.BlockSpec((1, width), whole),
            pl.BlockSpec((1, width), whole),
        ]
        + [pl.BlockSpec(memory_space=pl.ANY)] * shards,
        out_specs=[
            pl.BlockSpec((PAD_SEQ, width), block),
            pl.BlockSpec((PAD_SEQ, 3 * width), block),
            pl.BlockSpec((PAD_SEQ, width), block),
            pl.BlockSpec(memory_space=pl.ANY),
        ],
        out_shape=[
            jax.ShapeDtypeStruct((rows, width), BF),
            jax.ShapeDtypeStruct((rows, 3 * width), BF),
            jax.ShapeDtypeStruct((rows, width), BF),
            jax.ShapeDtypeStruct((shards * own, cols), BF),
        ],
        scratch_shapes=[
            pltpu.VMEM((shards * own, cols), BF),
            pltpu.SemaphoreType.DMA((shards + 1,)),
        ],
        compiler_params=pltpu.CompilerParams(vmem_limit_bytes=VMEM_LIMIT),
        cost_estimate=pl.CostEstimate(
            flops=rows * width * width, bytes_accessed=rows * width, transcendentals=0
        ),
    )(tok_pad, gain.reshape(1, -1), bias.reshape(1, -1), *pieces)


def owner_block(group, at, place):
    core, chip = place[0], place[1]
    return 4 * at + 2 * (chip if group % 2 else 1 - chip) + (core if group > 1 else 1 - core)


def heads_back(q_ref, k_ref, v_ref, g_ref, out_ref, at_rows, scale):
    rows, cols = q_ref.shape
    lane = lax.broadcasted_iota(jnp.int32, (rows, LANES), 1)
    key_at = lax.broadcasted_iota(jnp.int32, (rows, rows), 0)
    for pair in range(cols // LANES):
        at = slice(pair * LANES, (pair + 1) * LANES)
        queries, keys, values, grads = q_ref[:, at], k_ref[:, at], v_ref[:, at], g_ref[:, at]
        zero = jnp.zeros_like(queries)
        sums = None
        for half in range(2):
            mine = (lane < LANES // 2) if half == 0 else (lane >= LANES // 2)
            q_half = jnp.where(mine, queries, zero)
            g_half = jnp.where(mine, grads, zero)
            scores = dot_nt(keys, q_half) * scale
            scores = jnp.where(key_at < SEQ, scores, NEG)
            peak = jnp.max(scores, axis=0, keepdims=True)
            weights = jnp.exp(scores - peak)
            probs = weights / jnp.sum(weights, axis=0, keepdims=True)
            grad_attention = dot_nt(values, g_half)
            inner = jnp.sum(probs * grad_attention, axis=0, keepdims=True)
            grad_scores = (probs * (grad_attention - inner)).astype(BF)
            terms = (
                dot_tn(grad_scores, jnp.where(mine, keys, zero)),
                dot_nn(grad_scores, q_half),
                dot_nn(probs.astype(BF), g_half),
            )
            sums = terms if sums is None else tuple(a + b for a, b in zip(sums, terms))
        for part, value in enumerate((sums[0] * scale, sums[1] * scale, sums[2])):
            start = part * cols + pair * LANES
            out_ref[at_rows, start : start + LANES] = value.astype(BF)


def attend_back_kernel(
    core_ref, q_ref, k_ref, v_ref, g_ref, wq_ref, wk_ref, wv_ref, *refs, scale, final
):
    step = pl.program_id(0)
    rows, cols = q_ref.shape
    at_rows = pl.ds(pl.multiple_of(step * rows, rows), rows)
    late = 1 if final else 3
    sources, refs = refs[:late], refs[late:]
    held, sems, refs = refs[-late - 1 : -1], refs[-1], refs[: -late - 1]
    copies = [
        pltpu.make_async_copy(source, target, sems.at[at])
        for at, (source, target) in enumerate(zip(sources, held))
    ]

    @pl.when(step == 0)
    def _():
        for copy in copies:
            copy.start()

    if final:
        before_ref, tok_ref, after_ref, gain_ref, two_ref, vec_ref = refs[:6]
        out_ref, *share_refs, grads_ref, whole_ref, sums_ref = refs[6:]
    else:
        out_ref, *share_refs, grads_ref, whole_ref = refs
    heads_back(q_ref, k_ref, v_ref, g_ref, grads_ref, at_rows, scale)
    grad_first = None
    for part, w_ref in enumerate((wq_ref, wk_ref, wv_ref)):
        term = dot_nt(grads_ref[at_rows, part * cols : (part + 1) * cols], w_ref[...])
        grad_first = term if grad_first is None else grad_first + term
    if final:
        grad_first = grad_first + before_ref[...]
        normed, inverse = norm_rows(tok_ref[...].astype(F32))
        grad = after_ref[...] + norm_back(grad_first, normed, inverse, gain_ref[...])
        for image in range(out_ref.shape[0] // SEQ):

            @pl.when(step == image)
            def _():
                out_ref[image * SEQ : (image + 1) * SEQ, :] = grad[:SEQ]

        row = lax.broadcasted_iota(jnp.int32, sums_ref.shape, 0)
        gain_sum = jnp.sum(grad_first * normed, axis=0, keepdims=True)
        bias_sum = jnp.sum(grad_first, axis=0, keepdims=True)
        sums = jnp.where(row == 0, gain_sum, jnp.where(row == 1, bias_sum, 0.0))
        sums_ref[...] = jnp.where(step == 0, sums, sums_ref[...] + sums)
    else:
        out_ref[...] = grad_first

    @pl.when(step == pl.num_programs(0) - 1)
    def _():
        for copy in copies:
            copy.wait()
        whole_ref[:, : 3 * cols] = dot_tn(held[0][...], grads_ref[...])
        if final:
            sums = sums_ref[...] + pltpu.roll(two_ref[...], 2, 0)
            rest = jnp.zeros((LANES - sums.shape[0], sums.shape[1]), F32)
            whole_ref[:, 3 * cols :] = (jnp.concatenate([sums, rest], axis=0) + vec_ref[...]).T
        else:
            whole_ref[:, 3 * cols :] = dot_tn(held[1][...], held[2][...])
        count, own, _ = share_refs[0].shape
        for group, share_ref in enumerate(share_refs):
            for at in range(count):
                block = owner_block(group, at, core_ref)
                rows_of = pl.ds(pl.multiple_of(block * own, own), own)
                share_ref[at] = whole_ref[rows_of, :].astype(BF)


def attend_back(core, qkv, grad_heads_out, full, first, images, shards, group, extra, final):
    rows, width = grad_heads_out.shape
    cols = width // 2
    wide = 3 * cols + (LANES if final else width)
    own = width // shards
    late = 1 if final else 3
    at = lambda part: pl.BlockSpec((PAD_SEQ, cols), lambda i: (i, 2 * part + group))
    weight = lambda part: pl.BlockSpec((width, cols), lambda i: (0, 2 * part + group))
    held = lambda a: pl.BlockSpec(a.shape, lambda i: (0, 0))
    block = pl.BlockSpec((PAD_SEQ, width), lambda i: (i, 0))
    share = pl.BlockSpec((shards // 4, own, wide), lambda i: (0, 0, 0))
    share_shape = jax.ShapeDtypeStruct((shards // 4, own, wide), BF)
    return pl.pallas_call(
        functools.partial(
            attend_back_kernel, scale=1.0 / math.sqrt(width // HEADS), final=final
        ),
        grid=(images,),
        in_specs=[pl.BlockSpec(memory_space=pltpu.SMEM), at(0), at(1), at(2), at(0)]
        + [weight(0), weight(1), weight(2)]
        + [pl.BlockSpec(memory_space=pl.ANY)] * late
        + ([block, block, block] + [held(a) for a in extra[3:]] if final else []),
        out_specs=[
            pl.BlockSpec((images * SEQ, width), lambda i: (0, 0)) if final else block,
        ]
        + [share] * 4,
        out_shape=[
            jax.ShapeDtypeStruct((images * SEQ if final else rows, width), F32),
        ]
        + [share_shape] * 4,
        scratch_shapes=[pltpu.VMEM((rows, 3 * cols), BF), pltpu.VMEM((width, wide), F32)]
        + ([pltpu.VMEM((8, width), F32)] if final else [])
        + [pltpu.VMEM((rows, width), BF)] * late
        + [pltpu.SemaphoreType.DMA((late,))],
        compiler_params=pltpu.CompilerParams(vmem_limit_bytes=VMEM_LIMIT),
        cost_estimate=pl.CostEstimate(
            flops=40 * rows * PAD_SEQ * cols,
            bytes_accessed=rows * cols,
            transcendentals=0,
        ),
    )(core, qkv, qkv, qkv, grad_heads_out, full, full, full, first, *extra)


def assemble_kernel(
    low_ref, held_ref, got_ref, right_ref, share_ref,
    qkv_ref, proj_ref, router_ref, loss_ref, *vector_refs, scale,
):
    rows, width = proj_ref.shape
    cols = width // 2
    count, size, _ = held_ref.shape
    for at in range(count):
        for low in range(2):
            block = jnp.where(low_ref[0] == low, held_ref[at], got_ref[at]).astype(F32)
            inside = slice((2 * at + low) * size, (2 * at + low + 1) * size)
            for part in range(3):
                out = slice(part * width, part * width + cols)
                qkv_ref[inside, out] = block[:, part * cols : (part + 1) * cols]
            proj_ref[inside, :] = block[:, 3 * cols :]
    for part in range(3):
        out = slice(part * width + cols, (part + 1) * width)
        qkv_ref[:, out] = right_ref[:rows, part * cols : (part + 1) * cols].astype(F32)
    small = right_ref[:, 3 * cols :].astype(F32).T
    for at, vector_ref in enumerate(vector_refs):
        vector_ref[...] = small[at : at + 1, :rows]
    router_ref[...] = small[5 : 5 + router_ref.shape[0], :rows]
    product = small[4:5, :LANES] * share_ref[...]
    loss_ref[...] = jnp.broadcast_to(jnp.sum(product, axis=-1, keepdims=True) * scale, (1, LANES))


def assemble(low, held, got, right, route_share, scale):
    rows, wide = right.shape
    experts = route_share.shape[1]
    width = 2 * held.shape[2] // 5
    spec = pl.BlockSpec(memory_space=pltpu.VMEM)
    share = jnp.pad(route_share, ((0, 0), (0, LANES - experts)))
    right = jnp.pad(right, ((0, max(rows, LANES) - rows), (0, 0)))
    return pl.pallas_call(
        functools.partial(assemble_kernel, scale=scale),
        in_specs=[pl.BlockSpec(memory_space=pltpu.SMEM)] + [spec] * 4,
        out_specs=[spec] * 8,
        out_shape=[
            jax.ShapeDtypeStruct((rows, 3 * width), F32),
            jax.ShapeDtypeStruct((rows, width), F32),
            jax.ShapeDtypeStruct((experts, rows), F32),
            jax.ShapeDtypeStruct((1, LANES), F32),
        ]
        + [jax.ShapeDtypeStruct((1, rows), F32)] * 4,
    )(low, held, got, right, share)


def expert_kernel(
    me_ref, x_ref, cots_ref, wr_ref, win_ref, wout_ref, win_rows_ref, wout_cols_ref,
    hid_ref, gp_ref, gm_ref, mg_ref, rows_ref, gr_ref,
    hid_all, gp_all, p_ref, gain_ref, routed_ref, c_ref,
    *, experts, up_steps, down_steps, start,
):
    step = pl.program_id(0)
    rows = x_ref.shape[0]
    tile = win_ref.shape[1]
    piece = win_rows_ref.shape[0]
    lane = lax.broadcasted_iota(jnp.int32, (rows, LANES), 1)
    mine = lane == me_ref[0]

    def gate():
        return jnp.sum(jnp.where(mine, p_ref[...], 0.0), axis=-1, keepdims=True)

    @pl.when(step == 0)
    def _():
        logits = jnp.where(lane < experts, dot_nn(x_ref[...], wr_ref[...]), NEG)
        top = jnp.max(logits, axis=-1, keepdims=True)
        weights = jnp.exp(logits - top)
        p_ref[...] = weights / jnp.sum(weights, axis=-1, keepdims=True)
        size = rows // cots_ref.shape[0]
        cots = cots_ref[:, start : start + size, :].astype(F32).reshape(rows, -1)
        c_ref[...] = cots.astype(BF)
        gm_ref[...] = (gate() * cots).astype(BF)

    @pl.when(step < up_steps)
    def _():
        col = pl.ds(pl.multiple_of(step * tile, tile), tile)
        pre = dot_nn(x_ref[...], win_ref[...])
        back = dot_nt(gm_ref[...], wout_ref[...])
        cdf = 0.5 * (1.0 + lax.erf(pre * (1.0 / math.sqrt(2.0))))
        density = jnp.exp(-0.5 * pre * pre) * (1.0 / math.sqrt(2.0 * math.pi))
        hidden = (pre * cdf).astype(BF)
        grad_pre = (back * (cdf + pre * density)).astype(BF)
        hid_ref[...] = hidden
        gp_ref[...] = grad_pre
        hid_all[:, col] = hidden
        gp_all[:, col] = grad_pre

    @pl.when((step >= up_steps) & (step < up_steps + down_steps))
    def _():
        part = step - up_steps
        col = pl.ds(pl.multiple_of(part * piece, piece), piece)
        made = dot_nn(hid_all[...], wout_cols_ref[...])
        mg_ref[...] = (gate() * made).astype(BF)
        gain = c_ref[:, col].astype(F32) * made.astype(BF).astype(F32)
        gain = jnp.broadcast_to(jnp.sum(gain, axis=-1, keepdims=True), (rows, LANES))
        gain_ref[...] = jnp.where(part == 0, gain, gain_ref[...] + gain)

    @pl.when(step == up_steps + down_steps)
    def _():
        probs = p_ref[...]
        routed = gain_ref[...] * gate() * (jnp.where(mine, 1.0, 0.0) - probs)
        routed_ref[...] = routed.astype(BF)
        gr_ref[...] = dot_tn(routed_ref[...], x_ref[...])

    @pl.when(step >= up_steps + down_steps)
    def _():
        part = step - up_steps - down_steps
        router = wr_ref[pl.ds(pl.multiple_of(part * piece, piece), piece), :]
        back = dot_nt(gp_all[...], win_rows_ref[...]) + dot_nt(routed_ref[...], router)
        rows_ref[...] = back.astype(BF)


def run_expert(me, x, cots, start, w_router, w_in, w_out, experts):
    rows, width = x.shape
    hidden = w_in.shape[1]
    tile, piece = 512, 256
    up_steps, down_steps = hidden // tile, width // piece
    whole = lambda j: (0, 0)
    up = lambda j: jnp.minimum(j, up_steps - 1)
    made = lambda j: jnp.clip(j - up_steps, 0, down_steps - 1)
    back = lambda j: jnp.clip(j - up_steps - down_steps, 0, down_steps - 1)
    big = jax.ShapeDtypeStruct((rows, hidden), BF)
    small = jax.ShapeDtypeStruct((rows, width), BF)
    return pl.pallas_call(
        functools.partial(
            expert_kernel, experts=experts, up_steps=up_steps, down_steps=down_steps, start=start
        ),
        grid=(up_steps + 2 * down_steps,),
        in_specs=[
            pl.BlockSpec(memory_space=pltpu.SMEM),
            pl.BlockSpec((rows, width), whole),
            pl.BlockSpec(cots.shape, lambda j: (0, 0, 0)),
            pl.BlockSpec((width, LANES), lambda j: (0, w_router.shape[1] // LANES - 1)),
            pl.BlockSpec((width, tile), lambda j: (0, up(j))),
            pl.BlockSpec((tile, width), lambda j: (up(j), 0)),
            pl.BlockSpec((piece, hidden), lambda j: (back(j), 0)),
            pl.BlockSpec((hidden, piece), lambda j: (0, made(j))),
        ],
        out_specs=[
            pl.BlockSpec((rows, tile), lambda j: (0, up(j))),
            pl.BlockSpec((rows, tile), lambda j: (0, up(j))),
            pl.BlockSpec((rows, width), whole),
            pl.BlockSpec((rows, piece), lambda j: (0, made(j))),
            pl.BlockSpec((rows, piece), lambda j: (0, back(j))),
            pl.BlockSpec((LANES, width), whole),
        ],
        out_shape=[big, big, small, small, small, jax.ShapeDtypeStruct((LANES, width), F32)],
        scratch_shapes=[
            pltpu.VMEM((rows, hidden), BF),
            pltpu.VMEM((rows, hidden), BF),
            pltpu.VMEM((rows, LANES), F32),
            pltpu.VMEM((rows, LANES), F32),
            pltpu.VMEM((rows, LANES), BF),
            pltpu.VMEM((rows, width), BF),
        ],
        compiler_params=pltpu.CompilerParams(vmem_limit_bytes=VMEM_LIMIT),
        cost_estimate=pl.CostEstimate(
            flops=16 * rows * width * hidden,
            bytes_accessed=rows * hidden,
            transcendentals=0,
        ),
    )(me, x, cots, w_router, w_in, w_out, w_in, w_out)


def weight_grad_kernel(place_ref, x_a, x_b, gm_a, gm_b, gp_a, gp_b, hid_a, hid_b, *out_refs):
    grad_in = (dot_tn(x_a[...], gp_a[...]) + dot_tn(x_b[...], gp_b[...])).astype(BF)
    grad_out = (dot_tn(hid_a[...], gm_a[...]) + dot_tn(hid_b[...], gm_b[...])).astype(BF)
    each = pl.num_programs(0) // 4
    for group in range(4):

        @pl.when(pl.program_id(0) // each == group)
        def _():
            out_refs[group][0] = grad_in
            out_refs[4 + group][0] = grad_out


def weight_grads(place, x, grad_made, grad_pre, hidden, shards):
    width, hid = x[0].shape[1], hidden[0].shape[1]
    tile, each = hid // shards, shards // 4
    count = x[0].shape[0] + x[1].shape[0]

    def source(j, place_ref):
        group, at = j // each, lax.rem(j, each)
        core = jnp.where(group > 1, place_ref[0], 1 - place_ref[0])
        chip = jnp.where(lax.rem(group, 2) == 1, place_ref[1], 1 - place_ref[1])
        return (0, 4 * at + 2 * chip + core)

    held = lambda a: pl.BlockSpec(a.shape, lambda j, place_ref: (0, 0))
    tiled = lambda a: pl.BlockSpec((a.shape[0], tile), source)

    def out(group, *block):
        at = lambda j, place_ref: (jnp.clip(j - group * each, 0, each - 1), 0, 0)
        return pl.BlockSpec((1,) + block, at)

    return pl.pallas_call(
        weight_grad_kernel,
        grid_spec=pltpu.PrefetchScalarGridSpec(
            num_scalar_prefetch=1,
            grid=(shards,),
            in_specs=[held(a) for a in (*x, *grad_made)]
            + [tiled(a) for a in (*grad_pre, *hidden)],
            out_specs=[out(group, width, tile) for group in range(4)]
            + [out(group, tile, width) for group in range(4)],
        ),
        out_shape=[jax.ShapeDtypeStruct((each, width, tile), BF)] * 4
        + [jax.ShapeDtypeStruct((each, tile, width), BF)] * 4,
        compiler_params=pltpu.CompilerParams(vmem_limit_bytes=VMEM_LIMIT),
        cost_estimate=pl.CostEstimate(
            flops=8 * count * width * hid, bytes_accessed=width * hid, transcendentals=0
        ),
    )(place, *x, *grad_made, *grad_pre, *hidden)


def combine_kernel(
    at_ref, back_a_ref, back_b_ref, glog_ref, router_ref, proj_ref, after_ref, cot_ref, gain_ref,
    grad_ref, low_ref, heads_ref, sums_ref,
):
    rows = at_ref.shape[0]

    def picked(first, back_ref):
        slot = lax.broadcasted_iota(jnp.int32, (rows, back_ref.shape[0]), 1)
        match = (slot == at_ref[:, first : first + 1]) | (slot == at_ref[:, first + 1 : first + 2])
        return dot_nn(jnp.where(match, 1.0, 0.0).astype(BF), back_ref[...])

    grad_mid = picked(0, back_a_ref) + picked(2, back_b_ref) + dot_nt(glog_ref[...], router_ref[...])
    normed, inverse = norm_rows(after_ref[...])
    grad = cot_ref[...].astype(F32) + norm_back(grad_mid, normed, inverse, gain_ref[...])
    grad_ref[...] = grad
    low = grad.astype(BF)
    low_ref[...] = low
    heads_ref[...] = dot_nt(low, proj_ref[...]).astype(BF)
    row = lax.broadcasted_iota(jnp.int32, sums_ref.shape, 0)
    gain_sum = jnp.sum(grad_mid * normed, axis=0, keepdims=True)
    bias_sum = jnp.sum(grad_mid, axis=0, keepdims=True)
    sums = jnp.where(row == 0, gain_sum, jnp.where(row == 1, bias_sum, 0.0))

    @pl.when(pl.program_id(0) == 0)
    def _():
        sums_ref[...] = sums

    @pl.when(pl.program_id(0) > 0)
    def _():
        sums_ref[...] += sums


def combine(places, backs, grad_logits, full, after_attention, cot_pad, gain, images):
    rows, width = after_attention.shape
    block = lambda cols: pl.BlockSpec((PAD_SEQ, cols), lambda i: (i, 0))
    held = lambda a: pl.BlockSpec(a.shape, lambda i: (0, 0))
    return pl.pallas_call(
        combine_kernel,
        grid=(images,),
        in_specs=[
            block(LANES),
            held(backs[0]),
            held(backs[1]),
            block(LANES),
            pl.BlockSpec((width, LANES), lambda i: (0, 4 * width // LANES)),
            pl.BlockSpec((width, width), lambda i: (0, 3)),
            block(width),
            block(width),
            pl.BlockSpec((1, width), lambda i: (0, 0)),
        ],
        out_specs=[block(width)] * 3 + [pl.BlockSpec((8, width), lambda i: (0, 0))],
        out_shape=[
            jax.ShapeDtypeStruct((rows, width), F32),
            jax.ShapeDtypeStruct((rows, width), BF),
            jax.ShapeDtypeStruct((rows, width), BF),
            jax.ShapeDtypeStruct((8, width), F32),
        ],
        compiler_params=pltpu.CompilerParams(vmem_limit_bytes=VMEM_LIMIT),
        cost_estimate=pl.CostEstimate(
            flops=28 * rows * width * width, bytes_accessed=rows * width, transcendentals=0
        ),
    )(places, *backs, grad_logits, full, full, after_attention, cot_pad, gain.reshape(1, -1))


def axis_bits(size):
    return [1 << b for b in range(size.bit_length() - 1)]


def exchange(value, axis, bit):
    size = lax.axis_size(axis)
    return lax.ppermute(value, axis, [(i, i ^ bit) for i in range(size)])


def bit_of(axis, bit):
    return (lax.axis_index(axis) // bit) % 2


def gather_pieces(block, axis):
    pieces = {0: block}
    for bit in reversed(axis_bits(lax.axis_size(axis))):
        for k in list(pieces):
            pieces[k | bit] = exchange(pieces[k], axis, bit)
    return [pieces[k] for k in sorted(pieces)]


def other_core(value):
    return exchange(value, "shard", 1)


def other_chip(value):
    return exchange(value, "shard", 2)


def other_chip_in_turns(pairs):
    got = [[], []]
    last = None
    for at, start, stop in ((0, 0, 3), (1, 0, 2), (0, 3, 6), (1, 2, 6)):
        far, near = pairs[at]
        size = far.shape[1] // 6
        rows = slice(start * size, stop * size)
        send = (far[:, rows].astype(F32) + near[:, rows].astype(F32)).astype(BF)
        if last is not None:
            send, got[last][-1] = tie(send, got[last][-1])
        got[at].append(other_chip(send))
        last = at
    return [jnp.concatenate(g, axis=1) for g in got]


def reduce_chips(got, stay):
    held = stay + got.astype(F32)
    for bit in axis_bits(lax.axis_size("shard"))[2:]:
        view = held.reshape((-1, 2) + held.shape[1:])
        mine = bit_of("shard", bit)
        pick = lambda which: lax.dynamic_index_in_dim(view, which, 1, keepdims=False)
        held = pick(mine) + exchange(pick(1 - mine).astype(BF), "shard", bit).astype(F32)
    return held[0]


def owners_parts(held):
    owners = lax.axis_size("expert")
    rows, cols = held.shape
    got = trade(held.astype(BF).reshape(owners, rows // owners, cols))
    return jnp.sum(got.astype(F32), axis=0).astype(BF)


def owners_all(part):
    owners = lax.axis_size("expert")
    rows, cols = part.shape
    return trade(jnp.broadcast_to(part[None], (owners, rows, cols))).reshape(owners * rows, cols)


def owners_all_in_two(part):
    owners = lax.axis_size("expert")
    rows, cols = part.shape
    groups = [list(range(low, owners, 2)) for low in range(2)]
    held = lax.all_to_all(
        jnp.broadcast_to(part[None], (owners // 2, rows, cols)),
        "expert", split_axis=0, concat_axis=0, tiled=True, axis_index_groups=groups,
    )
    return held, exchange(held, "expert", 1)


def trade(view):
    return lax.all_to_all(view, "expert", split_axis=0, concat_axis=0, tiled=True)


def tie(*values):
    return lax.optimization_barrier(values)


def body(
    tokens, routes, capacity, ln1_gain, ln1_bias, ln2_gain, ln2_bias,
    w_qkv, w_proj, w_router, w_in, w_out, cotangent,
):
    count, width = tokens.shape
    experts = capacity.shape[0]
    owners = lax.axis_size("expert")
    shards = lax.axis_size("shard")
    images = count // SEQ
    padded = images * PAD_SEQ
    slot_count = 8 * ((2 * count + 8 * experts - 1) // (8 * experts))
    all_tokens = count * owners * shards
    me = lax.axis_index("expert").astype(jnp.int32).reshape(1)

    def pad_rows(values, fill=0):
        spread = values.reshape((images, SEQ) + values.shape[1:])
        room = [(0, 0), (0, PAD_SEQ - SEQ)] + [(0, 0)] * (values.ndim - 1)
        return jnp.pad(spread, room, constant_values=fill).reshape((padded,) + values.shape[1:])

    def cut_rows(values):
        spread = values.reshape((images, PAD_SEQ) + values.shape[1:])
        return spread[:, :SEQ].reshape((count,) + values.shape[1:])

    labels = jnp.arange(experts, dtype=jnp.int32)[:, None]
    first, second = routes[:, 0][None, :], routes[:, 1][None, :]
    hit_first, hit_second = first == labels, second == labels
    hits = jnp.concatenate([hit_first, hit_second], axis=0).astype(BF)
    order = lax.broadcasted_iota(jnp.int32, (count, count), 0) < lax.broadcasted_iota(
        jnp.int32, (count, count), 1
    )
    before = dot_nn(hits, order.astype(BF))
    totals = jnp.sum(hits.astype(F32), axis=1, keepdims=True)
    before_first = before[:experts]

    counts = (totals[:experts] + totals[experts:]).reshape(1, experts)
    high = jnp.floor(counts * (1.0 / COUNT_BASE))
    note = jnp.concatenate([high, counts - COUNT_BASE * high], axis=1).astype(BF)
    note = jnp.pad(note, ((0, w_router.shape[0] - 1), (0, 0)))
    room = jnp.zeros((w_router.shape[0], LANES - 3 * experts), BF)
    pieces = gather_pieces(
        jnp.concatenate([w_qkv, w_proj, w_router, note, room], axis=1), "shard"
    )

    before_second = before[experts:] + totals[:experts]
    limits = capacity[:, None].astype(F32)

    def slots(hit, ahead, choice):
        slot = jnp.sum(jnp.where(hit, ahead, 0.0), axis=0)
        limit = jnp.sum(jnp.where(hit, limits, 0.0), axis=0)
        kept = slot < limit
        slot = slot.astype(jnp.int32)
        return choice[0], slot, kept

    choices = [slots(hit_first, before_first, first), slots(hit_second, before_second, second)]
    head = 8 * ((slot_count + 15) // 16)
    spans = ((0, head), (head, slot_count - head))

    def chosen(start, size):
        found = []
        for choice, slot, kept in choices:
            inside = slot - start
            valid = kept & (inside >= 0) & (inside < size)
            found.append(pad_rows(jnp.where(valid, choice * size + inside, -1), -1))
        return found

    def selector(start, size):
        at = lax.broadcasted_iota(jnp.int32, (experts * size, 1), 0)
        first, second = chosen(start, size)
        return ((at == first[None, :]) | (at == second[None, :])).astype(BF)

    def send(select, rows):
        return dot_nn(select, rows).astype(BF).reshape(experts, -1, width)

    select_all = selector(0, slot_count)
    select = [selector(start, size) for start, size in spans]
    cot_pad = pad_rows(cotangent)
    cot_rows = trade(send(select_all, cot_pad))

    tok_pad = pad_rows(tokens)
    first_low, qkv_rows, heads_out, full = attend(tok_pad, ln1_gain, ln1_bias, pieces, images)
    proj_full = full[:, 3 * width : 4 * width]
    router_full = full[:, 4 * width :]
    notes = router_full[:: width // shards, experts : 3 * experts].astype(F32)
    notes = jnp.sum(notes, axis=0, keepdims=True)
    counts = COUNT_BASE * notes[:, :experts] + notes[:, experts:]
    counts = jnp.pad(counts, ((0, 0), (0, LANES - experts)))
    for bit in axis_bits(owners):
        counts = counts + exchange(counts, "expert", bit)
    route_share = counts[:, :experts] / (2.0 * all_tokens)
    token_rows = tok_pad.astype(F32)
    after_attention = token_rows + dot_nn(heads_out, proj_full)
    normed_two, inverse_two = norm_rows(after_attention)
    mid_low = (normed_two * ln2_gain + ln2_bias).astype(BF)

    sent, cot_rows, route_share = tie(send(select[0], mid_low), cot_rows, route_share)
    arrived = [trade(sent)]
    sent, arrived[0] = tie(send(select[1], mid_low), arrived[0])
    arrived.append(trade(sent))
    logits = dot_nn(mid_low, router_full)[:, :experts]
    live = (lax.broadcasted_iota(jnp.int32, (padded, 1), 0) % PAD_SEQ) < SEQ
    gate_probs = jnp.where(live, jax.nn.softmax(logits, axis=-1), 0.0)
    push = LOSS_WEIGHT * experts * route_share / all_tokens
    grad_logits = gate_probs * (push - jnp.sum(gate_probs * push, axis=-1, keepdims=True))
    grad_logits = jnp.pad(grad_logits, ((0, 0), (0, LANES - experts))).astype(BF)
    own = width // shards
    prob_sum = jnp.tile(jnp.pad(jnp.sum(gate_probs, axis=0), (0, own - experts)), shards)
    small = jnp.concatenate([prob_sum[None], dot_tn(grad_logits, mid_low)[:experts]], axis=0)
    small = jnp.pad(small, ((4, LANES - 4 - small.shape[0]), (0, 0)))

    places = jnp.stack([p for span in spans for p in chosen(*span)], axis=0)
    places = jnp.pad(places, ((0, LANES - places.shape[0]), (0, 0)), constant_values=-1).T
    arrived[0], grad_logits, small, places = tie(arrived[0], grad_logits, small, places)
    made = [
        run_expert(
            me,
            arrived[i].reshape(-1, width),
            cot_rows, start, full, w_in[0], w_out[0], experts,
        )
        for i, (start, _) in enumerate(spans)
    ]
    hidden, grad_pre, grad_made, gated, grad_rows, router_parts = zip(*made)
    grad_rows = [g.reshape(experts, -1, width) for g in grad_rows]
    backs = [trade(grad_rows[0])]
    gated = jnp.concatenate([g.reshape(experts, -1, width) for g in gated], axis=1)
    sent, backs[0], gated = tie(grad_rows[1], backs[0], gated)
    backs.append(trade(sent))
    mids = [a.reshape(-1, width) for a in arrived]
    mids[0], backs[0] = tie(mids[0], backs[0])
    place = jnp.stack([bit_of("shard", 1), bit_of("shard", 2)]).astype(jnp.int32)
    grads = weight_grads(place, mids, grad_made, grad_pre, hidden, shards)
    ins, outs = list(grads[:4]), list(grads[4:])
    parts = router_parts[0] + router_parts[1]
    small = small + jnp.pad(parts[: LANES - 5], ((5, 0), (0, 0)))
    gated, backs[1], ins[3], outs[3], small = tie(gated, backs[1], ins[3], outs[3], small)
    returned = trade(gated)

    backs = [b.reshape(-1, width) for b in backs]
    grad_after, grad_heads, grad_heads_out, sums_two = combine(
        places, backs, grad_logits, full, after_attention, cot_pad, ln2_gain, images
    )
    back = functools.partial(
        attend_back, place, qkv_rows, grad_heads_out, full, first_low, images, shards
    )
    grad_first, *share = back(0, (heads_out, grad_heads), False)
    send = (share[2].astype(F32) + other_core(share[0]).astype(F32)).astype(BF)
    total = reduce_chips(other_chip(send), share[3].astype(F32) + other_core(share[1]).astype(F32))
    rest = (grad_first, tok_pad, grad_after, ln1_gain.reshape(1, -1), sums_two, small)
    grad_tokens, *share = back(1, rest, True)
    share[0], share[1], returned, total = tie(share[0], share[1], returned, total)
    send = (share[2].astype(F32) + other_core(share[0]).astype(F32)).astype(BF)
    total, send, ins[2], outs[2] = tie(total, send, ins[2], outs[2])
    part = owners_parts(total)
    last = reduce_chips(other_chip(send), share[3].astype(F32) + other_core(share[1]).astype(F32))
    last = owners_parts(last)
    both = (outs, ins)
    got = other_chip_in_turns([(p[2], other_core(p[0])) for p in both])
    grad_expert_out, grad_expert_in = [
        reduce_chips(g, p[3].astype(F32) + other_core(p[1]).astype(F32)) for g, p in zip(got, both)
    ]
    first_half, second_half = owners_all_in_two(part), owners_all(last)

    mixed = cut_rows(after_attention + dot_tn(select_all, returned.reshape(-1, width))).astype(BF)
    grad_qkv_weight, proj_total, router_total, balance_loss, *vectors = assemble(
        (me % 2).astype(jnp.int32), *first_half, second_half, route_share, experts / all_tokens
    )
    balance_loss = balance_loss[0, 0]
    vectors = [v[0] for v in vectors]
    return (
        mixed,
        balance_loss,
        grad_tokens,
        vectors[0],
        vectors[1],
        vectors[2],
        vectors[3],
        grad_qkv_weight,
        proj_total,
        router_total.T,
        grad_expert_in[None],
        grad_expert_out[None],
    )


def solution(mesh):
    rows = P(("expert", "shard"), None)
    in_specs = (
        rows, rows, P(), P(), P(), P(), P(),
        P("shard", None), P("shard", None), P("shard", None),
        P("expert", None, None), P("expert", None, None), rows,
    )
    out_specs = (
        rows, P(), rows, P("shard"), P("shard"), P("shard"), P("shard"),
        P("shard", None), P("shard", None), P("shard", None),
        P("expert", None, "shard"), P("expert", "shard", None),
    )
    return jax.shard_map(body, mesh=mesh, in_specs=in_specs, out_specs=out_specs, check_vma=False)
```

```python
import functools
import math

import jax
import jax.numpy as jnp
from jax import lax
from jax.experimental import pallas as pl
from jax.experimental.pallas import tpu as pltpu
from jax.sharding import PartitionSpec as P

HEADS = 12
SEQ = 197
PAD_SEQ = 208
LANES = 128

NORM_EPS = 1e-06
LOSS_WEIGHT = 0.01
NEG = -1e30
COUNT_BASE = 128
VMEM_LIMIT = 56 * 1024 * 1024
BF = jnp.bfloat16
F32 = jnp.float32


def dot_nn(left, right):
    return lax.dot_general(left, right, (((1,), (0,)), ((), ())), preferred_element_type=F32)


def dot_nt(left, right):
    return lax.dot_general(left, right, (((1,), (1,)), ((), ())), preferred_element_type=F32)


def dot_tn(left, right):
    return lax.dot_general(left, right, (((0,), (0,)), ((), ())), preferred_element_type=F32)


def norm_rows(values):
    row_mean = jnp.mean(values, axis=-1, keepdims=True)
    centered = values - row_mean
    variance = jnp.mean(centered * centered, axis=-1, keepdims=True)
    inverse = lax.rsqrt(variance + NORM_EPS)
    return centered * inverse, inverse


def norm_back(grad_rows, normed, inverse, norm_gain):
    scaled = grad_rows * norm_gain
    return inverse * (
        scaled
        - jnp.mean(scaled, axis=-1, keepdims=True)
        - normed * jnp.mean(scaled * normed, axis=-1, keepdims=True)
    )


def attend_kernel(tok_ref, gain_ref, bias_ref, *refs, shards):
    pieces, refs = refs[:shards], refs[shards:]
    first_ref, qkv_ref, heads_ref, full_ref, w_ref, sems = refs
    step = pl.program_id(0)
    width = tok_ref.shape[1]
    own = width // shards
    me = lax.axis_index("shard")

    def place(k):
        at = 0
        for bit in axis_bits(shards):
            mine = lax.rem(me // bit, 2)
            at = at + bit * (1 - mine if k & bit else mine)
        rows = pl.ds(pl.multiple_of(at * own, own), own)
        return pltpu.make_async_copy(pieces[k], w_ref.at[rows, :], sems.at[k])

    whole_copy = pltpu.make_async_copy(w_ref, full_ref, sems.at[shards])

    @pl.when(step == 0)
    def _():
        for k in range(shards):
            place(k).start()

    normed, _ = norm_rows(tok_ref[...].astype(F32))
    first = (normed * gain_ref[...] + bias_ref[...]).astype(BF)
    first_ref[...] = first

    @pl.when(step == 0)
    def _():
        for k in range(shards):
            place(k).wait()
        whole_copy.start()

    for part in range(3):
        cols = slice(part * width, (part + 1) * width)
        qkv_ref[:, cols] = dot_nn(first, w_ref[:, cols]).astype(BF)
    rows = tok_ref.shape[0]
    lane = lax.broadcasted_iota(jnp.int32, (rows, LANES), 1)
    key_at = lax.broadcasted_iota(jnp.int32, (rows, rows), 1)
    scale = 1.0 / math.sqrt(width // HEADS)
    for pair in range(width // LANES):
        queries = qkv_ref[:, pair * LANES : (pair + 1) * LANES]
        keys = qkv_ref[:, width + pair * LANES : width + (pair + 1) * LANES]
        values = qkv_ref[:, 2 * width + pair * LANES : 2 * width + (pair + 1) * LANES]
        mixed = None
        for half in range(2):
            mine = (lane < LANES // 2) if half == 0 else (lane >= LANES // 2)
            zero = jnp.zeros_like(queries)
            scores = dot_nt(jnp.where(mine, queries, zero), keys) * scale
            scores = jnp.where(key_at < SEQ, scores, NEG)
            peak = jnp.max(scores, axis=-1, keepdims=True)
            weights = jnp.exp(scores - peak)
            total = jnp.sum(weights, axis=-1, keepdims=True)
            weights = (weights / total).astype(BF)
            term = dot_nn(weights, jnp.where(mine, values, zero))
            mixed = term if mixed is None else mixed + term
        heads_ref[:, pair * LANES : (pair + 1) * LANES] = mixed.astype(BF)

    @pl.when(step == pl.num_programs(0) - 1)
    def _():
        whole_copy.wait()


def attend(tok_pad, gain, bias, pieces, images):
    rows, width = tok_pad.shape
    shards = len(pieces)
    own, cols = pieces[0].shape
    whole = lambda i: (0, 0)
    block = lambda i: (i, 0)
    return pl.pallas_call(
        functools.partial(attend_kernel, shards=shards),
        grid=(images,),
        in_specs=[
            pl.BlockSpec((PAD_SEQ, width), block),
            pl.BlockSpec((1, width), whole),
            pl.BlockSpec((1, width), whole),
        ]
        + [pl.BlockSpec(memory_space=pl.ANY)] * shards,
        out_specs=[
            pl.BlockSpec((PAD_SEQ, width), block),
            pl.BlockSpec((PAD_SEQ, 3 * width), block),
            pl.BlockSpec((PAD_SEQ, width), block),
            pl.BlockSpec(memory_space=pl.ANY),
        ],
        out_shape=[
            jax.ShapeDtypeStruct((rows, width), BF),
            jax.ShapeDtypeStruct((rows, 3 * width), BF),
            jax.ShapeDtypeStruct((rows, width), BF),
            jax.ShapeDtypeStruct((shards * own, cols), BF),
        ],
        scratch_shapes=[
            pltpu.VMEM((shards * own, cols), BF),
            pltpu.SemaphoreType.DMA((shards + 1,)),
        ],
        compiler_params=pltpu.CompilerParams(vmem_limit_bytes=VMEM_LIMIT),
        cost_estimate=pl.CostEstimate(
            flops=rows * width * width, bytes_accessed=rows * width, transcendentals=0
        ),
    )(tok_pad, gain.reshape(1, -1), bias.reshape(1, -1), *pieces)


def owner_block(group, at, place):
    core, chip = place[0], place[1]
    return 4 * at + 2 * (chip if group % 2 else 1 - chip) + (core if group > 1 else 1 - core)


def heads_back(q_ref, k_ref, v_ref, g_ref, out_ref, at_rows, scale):
    rows, cols = q_ref.shape
    lane = lax.broadcasted_iota(jnp.int32, (rows, LANES), 1)
    key_at = lax.broadcasted_iota(jnp.int32, (rows, rows), 0)
    for pair in range(cols // LANES):
        at = slice(pair * LANES, (pair + 1) * LANES)
        queries, keys, values, grads = q_ref[:, at], k_ref[:, at], v_ref[:, at], g_ref[:, at]
        zero = jnp.zeros_like(queries)
        sums = None
        for half in range(2):
            mine = (lane < LANES // 2) if half == 0 else (lane >= LANES // 2)
            q_half = jnp.where(mine, queries, zero)
            g_half = jnp.where(mine, grads, zero)
            scores = dot_nt(keys, q_half) * scale
            scores = jnp.where(key_at < SEQ, scores, NEG)
            peak = jnp.max(scores, axis=0, keepdims=True)
            weights = jnp.exp(scores - peak)
            probs = weights / jnp.sum(weights, axis=0, keepdims=True)
            grad_attention = dot_nt(values, g_half)
            inner = jnp.sum(probs * grad_attention, axis=0, keepdims=True)
            grad_scores = (probs * (grad_attention - inner)).astype(BF)
            terms = (
                dot_tn(grad_scores, jnp.where(mine, keys, zero)),
                dot_nn(grad_scores, q_half),
                dot_nn(probs.astype(BF), g_half),
            )
            sums = terms if sums is None else tuple(a + b for a, b in zip(sums, terms))
        for part, value in enumerate((sums[0] * scale, sums[1] * scale, sums[2])):
            start = part * cols + pair * LANES
            out_ref[at_rows, start : start + LANES] = value.astype(BF)


def attend_back_kernel(
    core_ref, q_ref, k_ref, v_ref, g_ref, wq_ref, wk_ref, wv_ref, *refs, scale, final
):
    step = pl.program_id(0)
    rows, cols = q_ref.shape
    at_rows = pl.ds(pl.multiple_of(step * rows, rows), rows)
    late = 1 if final else 3
    sources, refs = refs[:late], refs[late:]
    held, sems, refs = refs[-late - 1 : -1], refs[-1], refs[: -late - 1]
    copies = [
        pltpu.make_async_copy(source, target, sems.at[at])
        for at, (source, target) in enumerate(zip(sources, held))
    ]

    @pl.when(step == 0)
    def _():
        for copy in copies:
            copy.start()

    if final:
        before_ref, tok_ref, after_ref, gain_ref, two_ref, vec_ref = refs[:6]
        out_ref, *share_refs, grads_ref, whole_ref, sums_ref = refs[6:]
    else:
        out_ref, *share_refs, grads_ref, whole_ref = refs
    heads_back(q_ref, k_ref, v_ref, g_ref, grads_ref, at_rows, scale)
    grad_first = None
    for part, w_ref in enumerate((wq_ref, wk_ref, wv_ref)):
        term = dot_nt(grads_ref[at_rows, part * cols : (part + 1) * cols], w_ref[...])
        grad_first = term if grad_first is None else grad_first + term
    if final:
        grad_first = grad_first + before_ref[...]
        normed, inverse = norm_rows(tok_ref[...].astype(F32))
        grad = after_ref[...] + norm_back(grad_first, normed, inverse, gain_ref[...])
        for image in range(out_ref.shape[0] // SEQ):

            @pl.when(step == image)
            def _():
                out_ref[image * SEQ : (image + 1) * SEQ, :] = grad[:SEQ]

        row = lax.broadcasted_iota(jnp.int32, sums_ref.shape, 0)
        gain_sum = jnp.sum(grad_first * normed, axis=0, keepdims=True)
        bias_sum = jnp.sum(grad_first, axis=0, keepdims=True)
        sums = jnp.where(row == 0, gain_sum, jnp.where(row == 1, bias_sum, 0.0))
        sums_ref[...] = jnp.where(step == 0, sums, sums_ref[...] + sums)
    else:
        out_ref[...] = grad_first

    @pl.when(step == pl.num_programs(0) - 1)
    def _():
        for copy in copies:
            copy.wait()
        whole_ref[:, : 3 * cols] = dot_tn(held[0][...], grads_ref[...])
        if final:
            sums = sums_ref[...] + pltpu.roll(two_ref[...], 2, 0)
            rest = jnp.zeros((LANES - sums.shape[0], sums.shape[1]), F32)
            whole_ref[:, 3 * cols :] = (jnp.concatenate([sums, rest], axis=0) + vec_ref[...]).T
        else:
            whole_ref[:, 3 * cols :] = dot_tn(held[1][...], held[2][...])
        count, own, _ = share_refs[0].shape
        for group, share_ref in enumerate(share_refs):
            for at in range(count):
                block = owner_block(group, at, core_ref)
                rows_of = pl.ds(pl.multiple_of(block * own, own), own)
                share_ref[at] = whole_ref[rows_of, :].astype(BF)


def attend_back(core, qkv, grad_heads_out, full, first, images, shards, group, extra, final):
    rows, width = grad_heads_out.shape
    cols = width // 2
    wide = 3 * cols + (LANES if final else width)
    own = width // shards
    late = 1 if final else 3
    at = lambda part: pl.BlockSpec((PAD_SEQ, cols), lambda i: (i, 2 * part + group))
    weight = lambda part: pl.BlockSpec((width, cols), lambda i: (0, 2 * part + group))
    held = lambda a: pl.BlockSpec(a.shape, lambda i: (0, 0))
    block = pl.BlockSpec((PAD_SEQ, width), lambda i: (i, 0))
    share = pl.BlockSpec((shards // 4, own, wide), lambda i: (0, 0, 0))
    share_shape = jax.ShapeDtypeStruct((shards // 4, own, wide), BF)
    return pl.pallas_call(
        functools.partial(
            attend_back_kernel, scale=1.0 / math.sqrt(width // HEADS), final=final
        ),
        grid=(images,),
        in_specs=[pl.BlockSpec(memory_space=pltpu.SMEM), at(0), at(1), at(2), at(0)]
        + [weight(0), weight(1), weight(2)]
        + [pl.BlockSpec(memory_space=pl.ANY)] * late
        + ([block, block, block] + [held(a) for a in extra[3:]] if final else []),
        out_specs=[
            pl.BlockSpec((images * SEQ, width), lambda i: (0, 0)) if final else block,
        ]
        + [share] * 4,
        out_shape=[
            jax.ShapeDtypeStruct((images * SEQ if final else rows, width), F32),
        ]
        + [share_shape] * 4,
        scratch_shapes=[pltpu.VMEM((rows, 3 * cols), BF), pltpu.VMEM((width, wide), F32)]
        + ([pltpu.VMEM((8, width), F32)] if final else [])
        + [pltpu.VMEM((rows, width), BF)] * late
        + [pltpu.SemaphoreType.DMA((late,))],
        compiler_params=pltpu.CompilerParams(vmem_limit_bytes=VMEM_LIMIT),
        cost_estimate=pl.CostEstimate(
            flops=40 * rows * PAD_SEQ * cols,
            bytes_accessed=rows * cols,
            transcendentals=0,
        ),
    )(core, qkv, qkv, qkv, grad_heads_out, full, full, full, first, *extra)


def assemble_kernel(
    low_ref, held_ref, got_ref, right_ref, share_ref,
    qkv_ref, proj_ref, router_ref, loss_ref, *vector_refs, scale,
):
    rows, width = proj_ref.shape
    cols = width // 2
    count, size, _ = held_ref.shape
    for at in range(count):
        for low in range(2):
            block = jnp.where(low_ref[0] == low, held_ref[at], got_ref[at]).astype(F32)
            inside = slice((2 * at + low) * size, (2 * at + low + 1) * size)
            for part in range(3):
                out = slice(part * width, part * width + cols)
                qkv_ref[inside, out] = block[:, part * cols : (part + 1) * cols]
            proj_ref[inside, :] = block[:, 3 * cols :]
    for part in range(3):
        out = slice(part * width + cols, (part + 1) * width)
        qkv_ref[:, out] = right_ref[:rows, part * cols : (part + 1) * cols].astype(F32)
    small = right_ref[:, 3 * cols :].astype(F32).T
    for at, vector_ref in enumerate(vector_refs):
        vector_ref[...] = small[at : at + 1, :rows]
    router_ref[...] = small[5 : 5 + router_ref.shape[0], :rows]
    product = small[4:5, :LANES] * share_ref[...]
    loss_ref[...] = jnp.broadcast_to(jnp.sum(product, axis=-1, keepdims=True) * scale, (1, LANES))


def assemble(low, held, got, right, route_share, scale):
    rows, wide = right.shape
    experts = route_share.shape[1]
    width = 2 * held.shape[2] // 5
    spec = pl.BlockSpec(memory_space=pltpu.VMEM)
    share = jnp.pad(route_share, ((0, 0), (0, LANES - experts)))
    right = jnp.pad(right, ((0, max(rows, LANES) - rows), (0, 0)))
    return pl.pallas_call(
        functools.partial(assemble_kernel, scale=scale),
        in_specs=[pl.BlockSpec(memory_space=pltpu.SMEM)] + [spec] * 4,
        out_specs=[spec] * 8,
        out_shape=[
            jax.ShapeDtypeStruct((rows, 3 * width), F32),
            jax.ShapeDtypeStruct((rows, width), F32),
            jax.ShapeDtypeStruct((experts, rows), F32),
            jax.ShapeDtypeStruct((1, LANES), F32),
        ]
        + [jax.ShapeDtypeStruct((1, rows), F32)] * 4,
    )(low, held, got, right, share)


def expert_kernel(
    me_ref, x_ref, cots_ref, wr_ref, win_ref, wout_ref, win_rows_ref, wout_cols_ref,
    hid_ref, gp_ref, gm_ref, mg_ref, rows_ref, gr_ref,
    hid_all, gp_all, p_ref, gain_ref, routed_ref, c_ref,
    *, experts, up_steps, down_steps, start,
):
    step = pl.program_id(0)
    rows = x_ref.shape[0]
    tile = win_ref.shape[1]
    piece = win_rows_ref.shape[0]
    lane = lax.broadcasted_iota(jnp.int32, (rows, LANES), 1)
    mine = lane == me_ref[0]

    def gate():
        return jnp.sum(jnp.where(mine, p_ref[...], 0.0), axis=-1, keepdims=True)

    @pl.when(step == 0)
    def _():
        logits = jnp.where(lane < experts, dot_nn(x_ref[...], wr_ref[...]), NEG)
        top = jnp.max(logits, axis=-1, keepdims=True)
        weights = jnp.exp(logits - top)
        p_ref[...] = weights / jnp.sum(weights, axis=-1, keepdims=True)
        size = rows // cots_ref.shape[0]
        cots = cots_ref[:, start : start + size, :].astype(F32).reshape(rows, -1)
        c_ref[...] = cots.astype(BF)
        gm_ref[...] = (gate() * cots).astype(BF)

    @pl.when(step < up_steps)
    def _():
        col = pl.ds(pl.multiple_of(step * tile, tile), tile)
        pre = dot_nn(x_ref[...], win_ref[...])
        back = dot_nt(gm_ref[...], wout_ref[...])
        cdf = 0.5 * (1.0 + lax.erf(pre * (1.0 / math.sqrt(2.0))))
        density = jnp.exp(-0.5 * pre * pre) * (1.0 / math.sqrt(2.0 * math.pi))
        hidden = (pre * cdf).astype(BF)
        grad_pre = (back * (cdf + pre * density)).astype(BF)
        hid_ref[...] = hidden
        gp_ref[...] = grad_pre
        hid_all[:, col] = hidden
        gp_all[:, col] = grad_pre

    @pl.when((step >= up_steps) & (step < up_steps + down_steps))
    def _():
        part = step - up_steps
        col = pl.ds(pl.multiple_of(part * piece, piece), piece)
        made = dot_nn(hid_all[...], wout_cols_ref[...])
        mg_ref[...] = (gate() * made).astype(BF)
        gain = c_ref[:, col].astype(F32) * made.astype(BF).astype(F32)
        gain = jnp.broadcast_to(jnp.sum(gain, axis=-1, keepdims=True), (rows, LANES))
        gain_ref[...] = jnp.where(part == 0, gain, gain_ref[...] + gain)

    @pl.when(step == up_steps + down_steps)
    def _():
        probs = p_ref[...]
        routed = gain_ref[...] * gate() * (jnp.where(mine, 1.0, 0.0) - probs)
        routed_ref[...] = routed.astype(BF)
        gr_ref[...] = dot_tn(routed_ref[...], x_ref[...])

    @pl.when(step >= up_steps + down_steps)
    def _():
        part = step - up_steps - down_steps
        router = wr_ref[pl.ds(pl.multiple_of(part * piece, piece), piece), :]
        back = dot_nt(gp_all[...], win_rows_ref[...]) + dot_nt(routed_ref[...], router)
        rows_ref[...] = back.astype(BF)


def run_expert(me, x, cots, start, w_router, w_in, w_out, experts):
    rows, width = x.shape
    hidden = w_in.shape[1]
    tile, piece = 512, 256
    up_steps, down_steps = hidden // tile, width // piece
    whole = lambda j: (0, 0)
    up = lambda j: jnp.minimum(j, up_steps - 1)
    made = lambda j: jnp.clip(j - up_steps, 0, down_steps - 1)
    back = lambda j: jnp.clip(j - up_steps - down_steps, 0, down_steps - 1)
    big = jax.ShapeDtypeStruct((rows, hidden), BF)
    small = jax.ShapeDtypeStruct((rows, width), BF)
    return pl.pallas_call(
        functools.partial(
            expert_kernel, experts=experts, up_steps=up_steps, down_steps=down_steps, start=start
        ),
        grid=(up_steps + 2 * down_steps,),
        in_specs=[
            pl.BlockSpec(memory_space=pltpu.SMEM),
            pl.BlockSpec((rows, width), whole),
            pl.BlockSpec(cots.shape, lambda j: (0, 0, 0)),
            pl.BlockSpec((width, LANES), lambda j: (0, w_router.shape[1] // LANES - 1)),
            pl.BlockSpec((width, tile), lambda j: (0, up(j))),
            pl.BlockSpec((tile, width), lambda j: (up(j), 0)),
            pl.BlockSpec((piece, hidden), lambda j: (back(j), 0)),
            pl.BlockSpec((hidden, piece), lambda j: (0, made(j))),
        ],
        out_specs=[
            pl.BlockSpec((rows, tile), lambda j: (0, up(j))),
            pl.BlockSpec((rows, tile), lambda j: (0, up(j))),
            pl.BlockSpec((rows, width), whole),
            pl.BlockSpec((rows, piece), lambda j: (0, made(j))),
            pl.BlockSpec((rows, piece), lambda j: (0, back(j))),
            pl.BlockSpec((LANES, width), whole),
        ],
        out_shape=[big, big, small, small, small, jax.ShapeDtypeStruct((LANES, width), F32)],
        scratch_shapes=[
            pltpu.VMEM((rows, hidden), BF),
            pltpu.VMEM((rows, hidden), BF),
            pltpu.VMEM((rows, LANES), F32),
            pltpu.VMEM((rows, LANES), F32),
            pltpu.VMEM((rows, LANES), BF),
            pltpu.VMEM((rows, width), BF),
        ],
        compiler_params=pltpu.CompilerParams(vmem_limit_bytes=VMEM_LIMIT),
        cost_estimate=pl.CostEstimate(
            flops=16 * rows * width * hidden,
            bytes_accessed=rows * hidden,
            transcendentals=0,
        ),
    )(me, x, cots, w_router, w_in, w_out, w_in, w_out)


def weight_grad_kernel(place_ref, x_a, x_b, gm_a, gm_b, gp_a, gp_b, hid_a, hid_b, *out_refs):
    grad_in = (dot_tn(x_a[...], gp_a[...]) + dot_tn(x_b[...], gp_b[...])).astype(BF)
    grad_out = (dot_tn(hid_a[...], gm_a[...]) + dot_tn(hid_b[...], gm_b[...])).astype(BF)
    each = pl.num_programs(0) // 4
    for group in range(4):

        @pl.when(pl.program_id(0) // each == group)
        def _():
            out_refs[group][0] = grad_in
            out_refs[4 + group][0] = grad_out


def weight_grads(place, x, grad_made, grad_pre, hidden, shards):
    width, hid = x[0].shape[1], hidden[0].shape[1]
    tile, each = hid // shards, shards // 4
    count = x[0].shape[0] + x[1].shape[0]

    def source(j, place_ref):
        group, at = j // each, lax.rem(j, each)
        core = jnp.where(group > 1, place_ref[0], 1 - place_ref[0])
        chip = jnp.where(lax.rem(group, 2) == 1, place_ref[1], 1 - place_ref[1])
        return (0, 4 * at + 2 * chip + core)

    held = lambda a: pl.BlockSpec(a.shape, lambda j, place_ref: (0, 0))
    tiled = lambda a: pl.BlockSpec((a.shape[0], tile), source)

    def out(group, *block):
        at = lambda j, place_ref: (jnp.clip(j - group * each, 0, each - 1), 0, 0)
        return pl.BlockSpec((1,) + block, at)

    return pl.pallas_call(
        weight_grad_kernel,
        grid_spec=pltpu.PrefetchScalarGridSpec(
            num_scalar_prefetch=1,
            grid=(shards,),
            in_specs=[held(a) for a in (*x, *grad_made)]
            + [tiled(a) for a in (*grad_pre, *hidden)],
            out_specs=[out(group, width, tile) for group in range(4)]
            + [out(group, tile, width) for group in range(4)],
        ),
        out_shape=[jax.ShapeDtypeStruct((each, width, tile), BF)] * 4
        + [jax.ShapeDtypeStruct((each, tile, width), BF)] * 4,
        compiler_params=pltpu.CompilerParams(vmem_limit_bytes=VMEM_LIMIT),
        cost_estimate=pl.CostEstimate(
            flops=8 * count * width * hid, bytes_accessed=width * hid, transcendentals=0
        ),
    )(place, *x, *grad_made, *grad_pre, *hidden)


def combine_kernel(
    at_ref, back_a_ref, back_b_ref, glog_ref, router_ref, proj_ref, after_ref, cot_ref, gain_ref,
    grad_ref, low_ref, heads_ref, sums_ref,
):
    rows = at_ref.shape[0]

    def picked(first, back_ref):
        slot = lax.broadcasted_iota(jnp.int32, (rows, back_ref.shape[0]), 1)
        match = (slot == at_ref[:, first : first + 1]) | (slot == at_ref[:, first + 1 : first + 2])
        return dot_nn(jnp.where(match, 1.0, 0.0).astype(BF), back_ref[...])

    grad_mid = picked(0, back_a_ref) + picked(2, back_b_ref) + dot_nt(glog_ref[...], router_ref[...])
    normed, inverse = norm_rows(after_ref[...])
    grad = cot_ref[...].astype(F32) + norm_back(grad_mid, normed, inverse, gain_ref[...])
    grad_ref[...] = grad
    low = grad.astype(BF)
    low_ref[...] = low
    heads_ref[...] = dot_nt(low, proj_ref[...]).astype(BF)
    row = lax.broadcasted_iota(jnp.int32, sums_ref.shape, 0)
    gain_sum = jnp.sum(grad_mid * normed, axis=0, keepdims=True)
    bias_sum = jnp.sum(grad_mid, axis=0, keepdims=True)
    sums = jnp.where(row == 0, gain_sum, jnp.where(row == 1, bias_sum, 0.0))

    @pl.when(pl.program_id(0) == 0)
    def _():
        sums_ref[...] = sums

    @pl.when(pl.program_id(0) > 0)
    def _():
        sums_ref[...] += sums


def combine(places, backs, grad_logits, full, after_attention, cot_pad, gain, images):
    rows, width = after_attention.shape
    block = lambda cols: pl.BlockSpec((PAD_SEQ, cols), lambda i: (i, 0))
    held = lambda a: pl.BlockSpec(a.shape, lambda i: (0, 0))
    return pl.pallas_call(
        combine_kernel,
        grid=(images,),
        in_specs=[
            block(LANES),
            held(backs[0]),
            held(backs[1]),
            block(LANES),
            pl.BlockSpec((width, LANES), lambda i: (0, 4 * width // LANES)),
            pl.BlockSpec((width, width), lambda i: (0, 3)),
            block(width),
            block(width),
            pl.BlockSpec((1, width), lambda i: (0, 0)),
        ],
        out_specs=[block(width)] * 3 + [pl.BlockSpec((8, width), lambda i: (0, 0))],
        out_shape=[
            jax.ShapeDtypeStruct((rows, width), F32),
            jax.ShapeDtypeStruct((rows, width), BF),
            jax.ShapeDtypeStruct((rows, width), BF),
            jax.ShapeDtypeStruct((8, width), F32),
        ],
        compiler_params=pltpu.CompilerParams(vmem_limit_bytes=VMEM_LIMIT),
        cost_estimate=pl.CostEstimate(
            flops=28 * rows * width * width, bytes_accessed=rows * width, transcendentals=0
        ),
    )(places, *backs, grad_logits, full, full, after_attention, cot_pad, gain.reshape(1, -1))


def axis_bits(size):
    return [1 << b for b in range(size.bit_length() - 1)]


def exchange(value, axis, bit):
    size = lax.axis_size(axis)
    return lax.ppermute(value, axis, [(i, i ^ bit) for i in range(size)])


def bit_of(axis, bit):
    return (lax.axis_index(axis) // bit) % 2


def gather_pieces(block, axis):
    pieces = {0: block}
    for bit in reversed(axis_bits(lax.axis_size(axis))):
        for k in list(pieces):
            pieces[k | bit] = exchange(pieces[k], axis, bit)
    return [pieces[k] for k in sorted(pieces)]


def other_core(value):
    return exchange(value, "shard", 1)


def other_chip(value):
    return exchange(value, "shard", 2)


def other_chip_in_turns(pairs):
    got = [[], []]
    last = None
    for at, start, stop in ((0, 0, 3), (1, 0, 4), (0, 3, 6), (1, 4, 6)):
        far, near = pairs[at]
        size = far.shape[1] // 6
        rows = slice(start * size, stop * size)
        send = (far[:, rows].astype(F32) + near[:, rows].astype(F32)).astype(BF)
        if last is not None:
            send, got[last][-1] = tie(send, got[last][-1])
        got[at].append(other_chip(send))
        last = at
    return [jnp.concatenate(g, axis=1) for g in got]


def reduce_chips(got, stay):
    held = stay + got.astype(F32)
    for bit in axis_bits(lax.axis_size("shard"))[2:]:
        view = held.reshape((-1, 2) + held.shape[1:])
        mine = bit_of("shard", bit)
        pick = lambda which: lax.dynamic_index_in_dim(view, which, 1, keepdims=False)
        held = pick(mine) + exchange(pick(1 - mine).astype(BF), "shard", bit).astype(F32)
    return held[0]


def owners_parts(held):
    owners = lax.axis_size("expert")
    rows, cols = held.shape
    got = trade(held.astype(BF).reshape(owners, rows // owners, cols))
    return jnp.sum(got.astype(F32), axis=0).astype(BF)


def owners_all(part):
    owners = lax.axis_size("expert")
    rows, cols = part.shape
    return trade(jnp.broadcast_to(part[None], (owners, rows, cols))).reshape(owners * rows, cols)


def owners_all_in_two(part):
    owners = lax.axis_size("expert")
    rows, cols = part.shape
    groups = [list(range(low, owners, 2)) for low in range(2)]
    held = lax.all_to_all(
        jnp.broadcast_to(part[None], (owners // 2, rows, cols)),
        "expert", split_axis=0, concat_axis=0, tiled=True, axis_index_groups=groups,
    )
    return held, exchange(held, "expert", 1)


def trade(view):
    return lax.all_to_all(view, "expert", split_axis=0, concat_axis=0, tiled=True)


def tie(*values):
    return lax.optimization_barrier(values)


def body(
    tokens, routes, capacity, ln1_gain, ln1_bias, ln2_gain, ln2_bias,
    w_qkv, w_proj, w_router, w_in, w_out, cotangent,
):
    count, width = tokens.shape
    experts = capacity.shape[0]
    owners = lax.axis_size("expert")
    shards = lax.axis_size("shard")
    images = count // SEQ
    padded = images * PAD_SEQ
    slot_count = 8 * ((2 * count + 8 * experts - 1) // (8 * experts))
    all_tokens = count * owners * shards
    me = lax.axis_index("expert").astype(jnp.int32).reshape(1)

    def pad_rows(values, fill=0):
        spread = values.reshape((images, SEQ) + values.shape[1:])
        room = [(0, 0), (0, PAD_SEQ - SEQ)] + [(0, 0)] * (values.ndim - 1)
        return jnp.pad(spread, room, constant_values=fill).reshape((padded,) + values.shape[1:])

    def cut_rows(values):
        spread = values.reshape((images, PAD_SEQ) + values.shape[1:])
        return spread[:, :SEQ].reshape((count,) + values.shape[1:])

    labels = jnp.arange(experts, dtype=jnp.int32)[:, None]
    first, second = routes[:, 0][None, :], routes[:, 1][None, :]
    hit_first, hit_second = first == labels, second == labels
    hits = jnp.concatenate([hit_first, hit_second], axis=0).astype(BF)
    order = lax.broadcasted_iota(jnp.int32, (count, count), 0) < lax.broadcasted_iota(
        jnp.int32, (count, count), 1
    )
    before = dot_nn(hits, order.astype(BF))
    totals = jnp.sum(hits.astype(F32), axis=1, keepdims=True)
    before_first = before[:experts]

    counts = (totals[:experts] + totals[experts:]).reshape(1, experts)
    high = jnp.floor(counts * (1.0 / COUNT_BASE))
    note = jnp.concatenate([high, counts - COUNT_BASE * high], axis=1).astype(BF)
    note = jnp.pad(note, ((0, w_router.shape[0] - 1), (0, 0)))
    room = jnp.zeros((w_router.shape[0], LANES - 3 * experts), BF)
    pieces = gather_pieces(
        jnp.concatenate([w_qkv, w_proj, w_router, note, room], axis=1), "shard"
    )

    before_second = before[experts:] + totals[:experts]
    limits = capacity[:, None].astype(F32)

    def slots(hit, ahead, choice):
        slot = jnp.sum(jnp.where(hit, ahead, 0.0), axis=0)
        limit = jnp.sum(jnp.where(hit, limits, 0.0), axis=0)
        kept = slot < limit
        slot = slot.astype(jnp.int32)
        return choice[0], slot, kept

    choices = [slots(hit_first, before_first, first), slots(hit_second, before_second, second)]
    head = 8 * ((slot_count + 15) // 16)
    spans = ((0, head), (head, slot_count - head))

    def chosen(start, size):
        found = []
        for choice, slot, kept in choices:
            inside = slot - start
            valid = kept & (inside >= 0) & (inside < size)
            found.append(pad_rows(jnp.where(valid, choice * size + inside, -1), -1))
        return found

    def selector(start, size):
        at = lax.broadcasted_iota(jnp.int32, (experts * size, 1), 0)
        first, second = chosen(start, size)
        return ((at == first[None, :]) | (at == second[None, :])).astype(BF)

    def send(select, rows):
        return dot_nn(select, rows).astype(BF).reshape(experts, -1, width)

    select_all = selector(0, slot_count)
    select = [selector(start, size) for start, size in spans]
    cot_pad = pad_rows(cotangent)
    cot_rows = trade(send(select_all, cot_pad))

    tok_pad = pad_rows(tokens)
    first_low, qkv_rows, heads_out, full = attend(tok_pad, ln1_gain, ln1_bias, pieces, images)
    proj_full = full[:, 3 * width : 4 * width]
    router_full = full[:, 4 * width :]
    notes = router_full[:: width // shards, experts : 3 * experts].astype(F32)
    notes = jnp.sum(notes, axis=0, keepdims=True)
    counts = COUNT_BASE * notes[:, :experts] + notes[:, experts:]
    counts = jnp.pad(counts, ((0, 0), (0, LANES - experts)))
    for bit in axis_bits(owners):
        counts = counts + exchange(counts, "expert", bit)
    route_share = counts[:, :experts] / (2.0 * all_tokens)
    token_rows = tok_pad.astype(F32)
    after_attention = token_rows + dot_nn(heads_out, proj_full)
    normed_two, inverse_two = norm_rows(after_attention)
    mid_low = (normed_two * ln2_gain + ln2_bias).astype(BF)

    sent, cot_rows, route_share = tie(send(select[0], mid_low), cot_rows, route_share)
    arrived = [trade(sent)]
    sent, arrived[0] = tie(send(select[1], mid_low), arrived[0])
    arrived.append(trade(sent))
    logits = dot_nn(mid_low, router_full)[:, :experts]
    live = (lax.broadcasted_iota(jnp.int32, (padded, 1), 0) % PAD_SEQ) < SEQ
    gate_probs = jnp.where(live, jax.nn.softmax(logits, axis=-1), 0.0)
    push = LOSS_WEIGHT * experts * route_share / all_tokens
    grad_logits = gate_probs * (push - jnp.sum(gate_probs * push, axis=-1, keepdims=True))
    grad_logits = jnp.pad(grad_logits, ((0, 0), (0, LANES - experts))).astype(BF)
    own = width // shards
    prob_sum = jnp.tile(jnp.pad(jnp.sum(gate_probs, axis=0), (0, own - experts)), shards)
    small = jnp.concatenate([prob_sum[None], dot_tn(grad_logits, mid_low)[:experts]], axis=0)
    small = jnp.pad(small, ((4, LANES - 4 - small.shape[0]), (0, 0)))

    places = jnp.stack([p for span in spans for p in chosen(*span)], axis=0)
    places = jnp.pad(places, ((0, LANES - places.shape[0]), (0, 0)), constant_values=-1).T
    arrived[0], grad_logits, small, places = tie(arrived[0], grad_logits, small, places)
    made = [
        run_expert(
            me,
            arrived[i].reshape(-1, width),
            cot_rows, start, full, w_in[0], w_out[0], experts,
        )
        for i, (start, _) in enumerate(spans)
    ]
    hidden, grad_pre, grad_made, gated, grad_rows, router_parts = zip(*made)
    grad_rows = [g.reshape(experts, -1, width) for g in grad_rows]
    backs = [trade(grad_rows[0])]
    gated = jnp.concatenate([g.reshape(experts, -1, width) for g in gated], axis=1)
    sent, backs[0], gated = tie(grad_rows[1], backs[0], gated)
    backs.append(trade(sent))
    mids = [a.reshape(-1, width) for a in arrived]
    mids[0], backs[0] = tie(mids[0], backs[0])
    place = jnp.stack([bit_of("shard", 1), bit_of("shard", 2)]).astype(jnp.int32)
    grads = weight_grads(place, mids, grad_made, grad_pre, hidden, shards)
    ins, outs = list(grads[:4]), list(grads[4:])
    parts = router_parts[0] + router_parts[1]
    small = small + jnp.pad(parts[: LANES - 5], ((5, 0), (0, 0)))
    gated, backs[1], ins[3], outs[3], small = tie(gated, backs[1], ins[3], outs[3], small)
    returned = trade(gated)

    backs = [b.reshape(-1, width) for b in backs]
    grad_after, grad_heads, grad_heads_out, sums_two = combine(
        places, backs, grad_logits, full, after_attention, cot_pad, ln2_gain, images
    )
    back = functools.partial(
        attend_back, place, qkv_rows, grad_heads_out, full, first_low, images, shards
    )
    grad_first, *share = back(0, (heads_out, grad_heads), False)
    send = (share[2].astype(F32) + other_core(share[0]).astype(F32)).astype(BF)
    total = reduce_chips(other_chip(send), share[3].astype(F32) + other_core(share[1]).astype(F32))
    rest = (grad_first, tok_pad, grad_after, ln1_gain.reshape(1, -1), sums_two, small)
    grad_tokens, *share = back(1, rest, True)
    share[0], share[1], returned, total = tie(share[0], share[1], returned, total)
    send = (share[2].astype(F32) + other_core(share[0]).astype(F32)).astype(BF)
    total, send, ins[2], outs[2] = tie(total, send, ins[2], outs[2])
    part = owners_parts(total)
    last = reduce_chips(other_chip(send), share[3].astype(F32) + other_core(share[1]).astype(F32))
    last = owners_parts(last)
    both = (outs, ins)
    got = other_chip_in_turns([(p[2], other_core(p[0])) for p in both])
    grad_expert_out, grad_expert_in = [
        reduce_chips(g, p[3].astype(F32) + other_core(p[1]).astype(F32)) for g, p in zip(got, both)
    ]
    mixed = cut_rows(after_attention + dot_tn(select_all, returned.reshape(-1, width))).astype(BF)
    part, mixed = tie(part, mixed)
    first_half, second_half = owners_all_in_two(part), owners_all(last)
    second_half, grad_expert_in = tie(second_half, grad_expert_in)

    grad_qkv_weight, proj_total, router_total, balance_loss, *vectors = assemble(
        (me % 2).astype(jnp.int32), *first_half, second_half, route_share, experts / all_tokens
    )
    balance_loss = balance_loss[0, 0]
    vectors = [v[0] for v in vectors]
    return (
        mixed,
        balance_loss,
        grad_tokens,
        vectors[0],
        vectors[1],
        vectors[2],
        vectors[3],
        grad_qkv_weight,
        proj_total,
        router_total.T,
        grad_expert_in[None],
        grad_expert_out[None],
    )


def solution(mesh):
    rows = P(("expert", "shard"), None)
    in_specs = (
        rows, rows, P(), P(), P(), P(), P(),
        P("shard", None), P("shard", None), P("shard", None),
        P("expert", None, None), P("expert", None, None), rows,
    )
    out_specs = (
        rows, P(), rows, P("shard"), P("shard"), P("shard"), P("shard"),
        P("shard", None), P("shard", None), P("shard", None),
        P("expert", None, "shard"), P("expert", "shard", None),
    )
    return jax.shard_map(body, mesh=mesh, in_specs=in_specs, out_specs=out_specs, check_vma=False)
```

```python
import functools
import math

import jax
import jax.numpy as jnp
from jax import lax
from jax.experimental import pallas as pl
from jax.experimental.pallas import tpu as pltpu
from jax.sharding import PartitionSpec as P

HEADS = 12
SEQ = 197
PAD_SEQ = 208
LANES = 128

NORM_EPS = 1e-06
LOSS_WEIGHT = 0.01
NEG = -1e30
COUNT_BASE = 128
VMEM_LIMIT = 56 * 1024 * 1024
BF = jnp.bfloat16
F32 = jnp.float32


def dot_nn(left, right):
    return lax.dot_general(left, right, (((1,), (0,)), ((), ())), preferred_element_type=F32)


def dot_nt(left, right):
    return lax.dot_general(left, right, (((1,), (1,)), ((), ())), preferred_element_type=F32)


def dot_tn(left, right):
    return lax.dot_general(left, right, (((0,), (0,)), ((), ())), preferred_element_type=F32)


def norm_rows(values):
    row_mean = jnp.mean(values, axis=-1, keepdims=True)
    centered = values - row_mean
    variance = jnp.mean(centered * centered, axis=-1, keepdims=True)
    inverse = lax.rsqrt(variance + NORM_EPS)
    return centered * inverse, inverse


def norm_back(grad_rows, normed, inverse, norm_gain):
    scaled = grad_rows * norm_gain
    return inverse * (
        scaled
        - jnp.mean(scaled, axis=-1, keepdims=True)
        - normed * jnp.mean(scaled * normed, axis=-1, keepdims=True)
    )


def attend_kernel(tok_ref, gain_ref, bias_ref, *refs, shards):
    pieces, refs = refs[:shards], refs[shards:]
    first_ref, qkv_ref, heads_ref, full_ref, w_ref, sems = refs
    step = pl.program_id(0)
    width = tok_ref.shape[1]
    own = width // shards
    me = lax.axis_index("shard")

    def place(k):
        at = 0
        for bit in axis_bits(shards):
            mine = lax.rem(me // bit, 2)
            at = at + bit * (1 - mine if k & bit else mine)
        rows = pl.ds(pl.multiple_of(at * own, own), own)
        return pltpu.make_async_copy(pieces[k], w_ref.at[rows, :], sems.at[k])

    whole_copy = pltpu.make_async_copy(w_ref, full_ref, sems.at[shards])

    @pl.when(step == 0)
    def _():
        for k in range(shards):
            place(k).start()

    normed, _ = norm_rows(tok_ref[...].astype(F32))
    first = (normed * gain_ref[...] + bias_ref[...]).astype(BF)
    first_ref[...] = first

    @pl.when(step == 0)
    def _():
        for k in range(shards):
            place(k).wait()
        whole_copy.start()

    for part in range(3):
        cols = slice(part * width, (part + 1) * width)
        qkv_ref[:, cols] = dot_nn(first, w_ref[:, cols]).astype(BF)
    rows = tok_ref.shape[0]
    lane = lax.broadcasted_iota(jnp.int32, (rows, LANES), 1)
    key_at = lax.broadcasted_iota(jnp.int32, (rows, rows), 1)
    scale = 1.0 / math.sqrt(width // HEADS)
    for pair in range(width // LANES):
        queries = qkv_ref[:, pair * LANES : (pair + 1) * LANES]
        keys = qkv_ref[:, width + pair * LANES : width + (pair + 1) * LANES]
        values = qkv_ref[:, 2 * width + pair * LANES : 2 * width + (pair + 1) * LANES]
        mixed = None
        for half in range(2):
            mine = (lane < LANES // 2) if half == 0 else (lane >= LANES // 2)
            zero = jnp.zeros_like(queries)
            scores = dot_nt(jnp.where(mine, queries, zero), keys) * scale
            scores = jnp.where(key_at < SEQ, scores, NEG)
            peak = jnp.max(scores, axis=-1, keepdims=True)
            weights = jnp.exp(scores - peak)
            total = jnp.sum(weights, axis=-1, keepdims=True)
            weights = (weights / total).astype(BF)
            term = dot_nn(weights, jnp.where(mine, values, zero))
            mixed = term if mixed is None else mixed + term
        heads_ref[:, pair * LANES : (pair + 1) * LANES] = mixed.astype(BF)

    @pl.when(step == pl.num_programs(0) - 1)
    def _():
        whole_copy.wait()


def attend(tok_pad, gain, bias, pieces, images):
    rows, width = tok_pad.shape
    shards = len(pieces)
    own, cols = pieces[0].shape
    whole = lambda i: (0, 0)
    block = lambda i: (i, 0)
    return pl.pallas_call(
        functools.partial(attend_kernel, shards=shards),
        grid=(images,),
        in_specs=[
            pl.BlockSpec((PAD_SEQ, width), block),
            pl.BlockSpec((1, width), whole),
            pl.BlockSpec((1, width), whole),
        ]
        + [pl.BlockSpec(memory_space=pl.ANY)] * shards,
        out_specs=[
            pl.BlockSpec((PAD_SEQ, width), block),
            pl.BlockSpec((PAD_SEQ, 3 * width), block),
            pl.BlockSpec((PAD_SEQ, width), block),
            pl.BlockSpec(memory_space=pl.ANY),
        ],
        out_shape=[
            jax.ShapeDtypeStruct((rows, width), BF),
            jax.ShapeDtypeStruct((rows, 3 * width), BF),
            jax.ShapeDtypeStruct((rows, width), BF),
            jax.ShapeDtypeStruct((shards * own, cols), BF),
        ],
        scratch_shapes=[
            pltpu.VMEM((shards * own, cols), BF),
            pltpu.SemaphoreType.DMA((shards + 1,)),
        ],
        compiler_params=pltpu.CompilerParams(vmem_limit_bytes=VMEM_LIMIT),
        cost_estimate=pl.CostEstimate(
            flops=rows * width * width, bytes_accessed=rows * width, transcendentals=0
        ),
    )(tok_pad, gain.reshape(1, -1), bias.reshape(1, -1), *pieces)


def owner_block(group, at, place):
    core, chip = place[0], place[1]
    return 4 * at + 2 * (chip if group % 2 else 1 - chip) + (core if group > 1 else 1 - core)


def heads_back(q_ref, k_ref, v_ref, g_ref, out_ref, at_rows, scale):
    rows, cols = q_ref.shape
    lane = lax.broadcasted_iota(jnp.int32, (rows, LANES), 1)
    key_at = lax.broadcasted_iota(jnp.int32, (rows, rows), 0)
    for pair in range(cols // LANES):
        at = slice(pair * LANES, (pair + 1) * LANES)
        queries, keys, values, grads = q_ref[:, at], k_ref[:, at], v_ref[:, at], g_ref[:, at]
        zero = jnp.zeros_like(queries)
        sums = None
        for half in range(2):
            mine = (lane < LANES // 2) if half == 0 else (lane >= LANES // 2)
            q_half = jnp.where(mine, queries, zero)
            g_half = jnp.where(mine, grads, zero)
            scores = dot_nt(keys, q_half) * scale
            scores = jnp.where(key_at < SEQ, scores, NEG)
            peak = jnp.max(scores, axis=0, keepdims=True)
            weights = jnp.exp(scores - peak)
            probs = weights / jnp.sum(weights, axis=0, keepdims=True)
            grad_attention = dot_nt(values, g_half)
            inner = jnp.sum(probs * grad_attention, axis=0, keepdims=True)
            grad_scores = (probs * (grad_attention - inner)).astype(BF)
            terms = (
                dot_tn(grad_scores, jnp.where(mine, keys, zero)),
                dot_nn(grad_scores, q_half),
                dot_nn(probs.astype(BF), g_half),
            )
            sums = terms if sums is None else tuple(a + b for a, b in zip(sums, terms))
        for part, value in enumerate((sums[0] * scale, sums[1] * scale, sums[2])):
            start = part * cols + pair * LANES
            out_ref[at_rows, start : start + LANES] = value.astype(BF)


def attend_back_kernel(
    core_ref, q_ref, k_ref, v_ref, g_ref, wq_ref, wk_ref, wv_ref, *refs, scale, final
):
    step = pl.program_id(0)
    rows, cols = q_ref.shape
    at_rows = pl.ds(pl.multiple_of(step * rows, rows), rows)
    late = 1 if final else 3
    sources, refs = refs[:late], refs[late:]
    held, sems, refs = refs[-late - 1 : -1], refs[-1], refs[: -late - 1]
    copies = [
        pltpu.make_async_copy(source, target, sems.at[at])
        for at, (source, target) in enumerate(zip(sources, held))
    ]

    @pl.when(step == 0)
    def _():
        for copy in copies:
            copy.start()

    if final:
        before_ref, tok_ref, after_ref, gain_ref, two_ref, vec_ref = refs[:6]
        out_ref, *share_refs, grads_ref, whole_ref, sums_ref = refs[6:]
    else:
        out_ref, *share_refs, grads_ref, whole_ref = refs
    heads_back(q_ref, k_ref, v_ref, g_ref, grads_ref, at_rows, scale)
    grad_first = None
    for part, w_ref in enumerate((wq_ref, wk_ref, wv_ref)):
        term = dot_nt(grads_ref[at_rows, part * cols : (part + 1) * cols], w_ref[...])
        grad_first = term if grad_first is None else grad_first + term
    if final:
        grad_first = grad_first + before_ref[...]
        normed, inverse = norm_rows(tok_ref[...].astype(F32))
        grad = after_ref[...] + norm_back(grad_first, normed, inverse, gain_ref[...])
        for image in range(out_ref.shape[0] // SEQ):

            @pl.when(step == image)
            def _():
                out_ref[image * SEQ : (image + 1) * SEQ, :] = grad[:SEQ]

        row = lax.broadcasted_iota(jnp.int32, sums_ref.shape, 0)
        gain_sum = jnp.sum(grad_first * normed, axis=0, keepdims=True)
        bias_sum = jnp.sum(grad_first, axis=0, keepdims=True)
        sums = jnp.where(row == 0, gain_sum, jnp.where(row == 1, bias_sum, 0.0))
        sums_ref[...] = jnp.where(step == 0, sums, sums_ref[...] + sums)
    else:
        out_ref[...] = grad_first

    @pl.when(step == pl.num_programs(0) - 1)
    def _():
        for copy in copies:
            copy.wait()
        whole_ref[:, : 3 * cols] = dot_tn(held[0][...], grads_ref[...])
        if final:
            sums = sums_ref[...] + pltpu.roll(two_ref[...], 2, 0)
            rest = jnp.zeros((LANES - sums.shape[0], sums.shape[1]), F32)
            whole_ref[:, 3 * cols :] = (jnp.concatenate([sums, rest], axis=0) + vec_ref[...]).T
        else:
            whole_ref[:, 3 * cols :] = dot_tn(held[1][...], held[2][...])
        count, own, _ = share_refs[0].shape
        for group, share_ref in enumerate(share_refs):
            for at in range(count):
                block = owner_block(group, at, core_ref)
                rows_of = pl.ds(pl.multiple_of(block * own, own), own)
                share_ref[at] = whole_ref[rows_of, :].astype(BF)


def attend_back(core, qkv, grad_heads_out, full, first, images, shards, group, extra, final):
    rows, width = grad_heads_out.shape
    cols = width // 2
    wide = 3 * cols + (LANES if final else width)
    own = width // shards
    late = 1 if final else 3
    at = lambda part: pl.BlockSpec((PAD_SEQ, cols), lambda i: (i, 2 * part + group))
    weight = lambda part: pl.BlockSpec((width, cols), lambda i: (0, 2 * part + group))
    held = lambda a: pl.BlockSpec(a.shape, lambda i: (0, 0))
    block = pl.BlockSpec((PAD_SEQ, width), lambda i: (i, 0))
    share = pl.BlockSpec((shards // 4, own, wide), lambda i: (0, 0, 0))
    share_shape = jax.ShapeDtypeStruct((shards // 4, own, wide), BF)
    return pl.pallas_call(
        functools.partial(
            attend_back_kernel, scale=1.0 / math.sqrt(width // HEADS), final=final
        ),
        grid=(images,),
        in_specs=[pl.BlockSpec(memory_space=pltpu.SMEM), at(0), at(1), at(2), at(0)]
        + [weight(0), weight(1), weight(2)]
        + [pl.BlockSpec(memory_space=pl.ANY)] * late
        + ([block, block, block] + [held(a) for a in extra[3:]] if final else []),
        out_specs=[
            pl.BlockSpec((images * SEQ, width), lambda i: (0, 0)) if final else block,
        ]
        + [share] * 4,
        out_shape=[
            jax.ShapeDtypeStruct((images * SEQ if final else rows, width), F32),
        ]
        + [share_shape] * 4,
        scratch_shapes=[pltpu.VMEM((rows, 3 * cols), BF), pltpu.VMEM((width, wide), F32)]
        + ([pltpu.VMEM((8, width), F32)] if final else [])
        + [pltpu.VMEM((rows, width), BF)] * late
        + [pltpu.SemaphoreType.DMA((late,))],
        compiler_params=pltpu.CompilerParams(vmem_limit_bytes=VMEM_LIMIT),
        cost_estimate=pl.CostEstimate(
            flops=40 * rows * PAD_SEQ * cols,
            bytes_accessed=rows * cols,
            transcendentals=0,
        ),
    )(core, qkv, qkv, qkv, grad_heads_out, full, full, full, first, *extra)


def assemble_kernel(
    low_ref, held_ref, got_ref, right_ref, share_ref,
    qkv_ref, proj_ref, router_ref, loss_ref, *vector_refs, scale,
):
    rows, width = proj_ref.shape
    cols = width // 2
    count, size, _ = held_ref.shape
    for at in range(count):
        for low in range(2):
            block = jnp.where(low_ref[0] == low, held_ref[at], got_ref[at]).astype(F32)
            inside = slice((2 * at + low) * size, (2 * at + low + 1) * size)
            for part in range(3):
                out = slice(part * width, part * width + cols)
                qkv_ref[inside, out] = block[:, part * cols : (part + 1) * cols]
            proj_ref[inside, :] = block[:, 3 * cols :]
    for part in range(3):
        out = slice(part * width + cols, (part + 1) * width)
        qkv_ref[:, out] = right_ref[:rows, part * cols : (part + 1) * cols].astype(F32)
    small = right_ref[:, 3 * cols :].astype(F32).T
    for at, vector_ref in enumerate(vector_refs):
        vector_ref[...] = small[at : at + 1, :rows]
    router_ref[...] = small[5 : 5 + router_ref.shape[0], :rows]
    product = small[4:5, :LANES] * share_ref[...]
    loss_ref[...] = jnp.broadcast_to(jnp.sum(product, axis=-1, keepdims=True) * scale, (1, LANES))


def assemble(low, held, got, right, route_share, scale):
    rows, wide = right.shape
    experts = route_share.shape[1]
    width = 2 * held.shape[2] // 5
    spec = pl.BlockSpec(memory_space=pltpu.VMEM)
    share = jnp.pad(route_share, ((0, 0), (0, LANES - experts)))
    right = jnp.pad(right, ((0, max(rows, LANES) - rows), (0, 0)))
    return pl.pallas_call(
        functools.partial(assemble_kernel, scale=scale),
        in_specs=[pl.BlockSpec(memory_space=pltpu.SMEM)] + [spec] * 4,
        out_specs=[spec] * 8,
        out_shape=[
            jax.ShapeDtypeStruct((rows, 3 * width), F32),
            jax.ShapeDtypeStruct((rows, width), F32),
            jax.ShapeDtypeStruct((experts, rows), F32),
            jax.ShapeDtypeStruct((1, LANES), F32),
        ]
        + [jax.ShapeDtypeStruct((1, rows), F32)] * 4,
    )(low, held, got, right, share)


def expert_kernel(
    me_ref, x_ref, cots_ref, wr_ref, win_ref, wout_ref, win_rows_ref, wout_cols_ref,
    hid_ref, gp_ref, gm_ref, mg_ref, rows_ref, gr_ref,
    hid_all, gp_all, p_ref, gain_ref, routed_ref, c_ref,
    *, experts, up_steps, down_steps, start,
):
    step = pl.program_id(0)
    rows = x_ref.shape[0]
    tile = win_ref.shape[1]
    piece = win_rows_ref.shape[0]
    lane = lax.broadcasted_iota(jnp.int32, (rows, LANES), 1)
    mine = lane == me_ref[0]

    def gate():
        return jnp.sum(jnp.where(mine, p_ref[...], 0.0), axis=-1, keepdims=True)

    @pl.when(step == 0)
    def _():
        logits = jnp.where(lane < experts, dot_nn(x_ref[...], wr_ref[...]), NEG)
        top = jnp.max(logits, axis=-1, keepdims=True)
        weights = jnp.exp(logits - top)
        p_ref[...] = weights / jnp.sum(weights, axis=-1, keepdims=True)
        size = rows // cots_ref.shape[0]
        cots = cots_ref[:, start : start + size, :].astype(F32).reshape(rows, -1)
        c_ref[...] = cots.astype(BF)
        gm_ref[...] = (gate() * cots).astype(BF)

    @pl.when(step < up_steps)
    def _():
        col = pl.ds(pl.multiple_of(step * tile, tile), tile)
        pre = dot_nn(x_ref[...], win_ref[...])
        back = dot_nt(gm_ref[...], wout_ref[...])
        cdf = 0.5 * (1.0 + lax.erf(pre * (1.0 / math.sqrt(2.0))))
        density = jnp.exp(-0.5 * pre * pre) * (1.0 / math.sqrt(2.0 * math.pi))
        hidden = (pre * cdf).astype(BF)
        grad_pre = (back * (cdf + pre * density)).astype(BF)
        hid_ref[...] = hidden
        gp_ref[...] = grad_pre
        hid_all[:, col] = hidden
        gp_all[:, col] = grad_pre

    @pl.when((step >= up_steps) & (step < up_steps + down_steps))
    def _():
        part = step - up_steps
        col = pl.ds(pl.multiple_of(part * piece, piece), piece)
        made = dot_nn(hid_all[...], wout_cols_ref[...])
        mg_ref[...] = (gate() * made).astype(BF)
        gain = c_ref[:, col].astype(F32) * made.astype(BF).astype(F32)
        gain = jnp.broadcast_to(jnp.sum(gain, axis=-1, keepdims=True), (rows, LANES))
        gain_ref[...] = jnp.where(part == 0, gain, gain_ref[...] + gain)

    @pl.when(step == up_steps + down_steps)
    def _():
        probs = p_ref[...]
        routed = gain_ref[...] * gate() * (jnp.where(mine, 1.0, 0.0) - probs)
        routed_ref[...] = routed.astype(BF)
        gr_ref[...] = dot_tn(routed_ref[...], x_ref[...])

    @pl.when(step >= up_steps + down_steps)
    def _():
        part = step - up_steps - down_steps
        router = wr_ref[pl.ds(pl.multiple_of(part * piece, piece), piece), :]
        back = dot_nt(gp_all[...], win_rows_ref[...]) + dot_nt(routed_ref[...], router)
        rows_ref[...] = back.astype(BF)


def run_expert(me, x, cots, start, w_router, w_in, w_out, experts):
    rows, width = x.shape
    hidden = w_in.shape[1]
    tile, piece = 512, 256
    up_steps, down_steps = hidden // tile, width // piece
    whole = lambda j: (0, 0)
    up = lambda j: jnp.minimum(j, up_steps - 1)
    made = lambda j: jnp.clip(j - up_steps, 0, down_steps - 1)
    back = lambda j: jnp.clip(j - up_steps - down_steps, 0, down_steps - 1)
    big = jax.ShapeDtypeStruct((rows, hidden), BF)
    small = jax.ShapeDtypeStruct((rows, width), BF)
    return pl.pallas_call(
        functools.partial(
            expert_kernel, experts=experts, up_steps=up_steps, down_steps=down_steps, start=start
        ),
        grid=(up_steps + 2 * down_steps,),
        in_specs=[
            pl.BlockSpec(memory_space=pltpu.SMEM),
            pl.BlockSpec((rows, width), whole),
            pl.BlockSpec(cots.shape, lambda j: (0, 0, 0)),
            pl.BlockSpec((width, LANES), lambda j: (0, w_router.shape[1] // LANES - 1)),
            pl.BlockSpec((width, tile), lambda j: (0, up(j))),
            pl.BlockSpec((tile, width), lambda j: (up(j), 0)),
            pl.BlockSpec((piece, hidden), lambda j: (back(j), 0)),
            pl.BlockSpec((hidden, piece), lambda j: (0, made(j))),
        ],
        out_specs=[
            pl.BlockSpec((rows, tile), lambda j: (0, up(j))),
            pl.BlockSpec((rows, tile), lambda j: (0, up(j))),
            pl.BlockSpec((rows, width), whole),
            pl.BlockSpec((rows, piece), lambda j: (0, made(j))),
            pl.BlockSpec((rows, piece), lambda j: (0, back(j))),
            pl.BlockSpec((LANES, width), whole),
        ],
        out_shape=[big, big, small, small, small, jax.ShapeDtypeStruct((LANES, width), F32)],
        scratch_shapes=[
            pltpu.VMEM((rows, hidden), BF),
            pltpu.VMEM((rows, hidden), BF),
            pltpu.VMEM((rows, LANES), F32),
            pltpu.VMEM((rows, LANES), F32),
            pltpu.VMEM((rows, LANES), BF),
            pltpu.VMEM((rows, width), BF),
        ],
        compiler_params=pltpu.CompilerParams(vmem_limit_bytes=VMEM_LIMIT),
        cost_estimate=pl.CostEstimate(
            flops=16 * rows * width * hidden,
            bytes_accessed=rows * hidden,
            transcendentals=0,
        ),
    )(me, x, cots, w_router, w_in, w_out, w_in, w_out)


def weight_grad_kernel(place_ref, x_a, x_b, gm_a, gm_b, gp_a, gp_b, hid_a, hid_b, *out_refs):
    grad_in = (dot_tn(x_a[...], gp_a[...]) + dot_tn(x_b[...], gp_b[...])).astype(BF)
    grad_out = (dot_tn(hid_a[...], gm_a[...]) + dot_tn(hid_b[...], gm_b[...])).astype(BF)
    each = pl.num_programs(0) // 4
    for group in range(4):

        @pl.when(pl.program_id(0) // each == group)
        def _():
            out_refs[group][0] = grad_in
            out_refs[4 + group][0] = grad_out


def weight_grads(place, x, grad_made, grad_pre, hidden, shards):
    width, hid = x[0].shape[1], hidden[0].shape[1]
    tile, each = hid // shards, shards // 4
    count = x[0].shape[0] + x[1].shape[0]

    def source(j, place_ref):
        group, at = j // each, lax.rem(j, each)
        core = jnp.where(group > 1, place_ref[0], 1 - place_ref[0])
        chip = jnp.where(lax.rem(group, 2) == 1, place_ref[1], 1 - place_ref[1])
        return (0, 4 * at + 2 * chip + core)

    held = lambda a: pl.BlockSpec(a.shape, lambda j, place_ref: (0, 0))
    tiled = lambda a: pl.BlockSpec((a.shape[0], tile), source)

    def out(group, *block):
        at = lambda j, place_ref: (jnp.clip(j - group * each, 0, each - 1), 0, 0)
        return pl.BlockSpec((1,) + block, at)

    return pl.pallas_call(
        weight_grad_kernel,
        grid_spec=pltpu.PrefetchScalarGridSpec(
            num_scalar_prefetch=1,
            grid=(shards,),
            in_specs=[held(a) for a in (*x, *grad_made)]
            + [tiled(a) for a in (*grad_pre, *hidden)],
            out_specs=[out(group, width, tile) for group in range(4)]
            + [out(group, tile, width) for group in range(4)],
        ),
        out_shape=[jax.ShapeDtypeStruct((each, width, tile), BF)] * 4
        + [jax.ShapeDtypeStruct((each, tile, width), BF)] * 4,
        compiler_params=pltpu.CompilerParams(vmem_limit_bytes=VMEM_LIMIT),
        cost_estimate=pl.CostEstimate(
            flops=8 * count * width * hid, bytes_accessed=width * hid, transcendentals=0
        ),
    )(place, *x, *grad_made, *grad_pre, *hidden)


def combine_kernel(
    at_ref, back_a_ref, back_b_ref, glog_ref, router_ref, proj_ref, after_ref, cot_ref, gain_ref,
    grad_ref, low_ref, heads_ref, sums_ref,
):
    rows = at_ref.shape[0]

    def picked(first, back_ref):
        slot = lax.broadcasted_iota(jnp.int32, (rows, back_ref.shape[0]), 1)
        match = (slot == at_ref[:, first : first + 1]) | (slot == at_ref[:, first + 1 : first + 2])
        return dot_nn(jnp.where(match, 1.0, 0.0).astype(BF), back_ref[...])

    grad_mid = picked(0, back_a_ref) + picked(2, back_b_ref) + dot_nt(glog_ref[...], router_ref[...])
    normed, inverse = norm_rows(after_ref[...])
    grad = cot_ref[...].astype(F32) + norm_back(grad_mid, normed, inverse, gain_ref[...])
    grad_ref[...] = grad
    low = grad.astype(BF)
    low_ref[...] = low
    heads_ref[...] = dot_nt(low, proj_ref[...]).astype(BF)
    row = lax.broadcasted_iota(jnp.int32, sums_ref.shape, 0)
    gain_sum = jnp.sum(grad_mid * normed, axis=0, keepdims=True)
    bias_sum = jnp.sum(grad_mid, axis=0, keepdims=True)
    sums = jnp.where(row == 0, gain_sum, jnp.where(row == 1, bias_sum, 0.0))

    @pl.when(pl.program_id(0) == 0)
    def _():
        sums_ref[...] = sums

    @pl.when(pl.program_id(0) > 0)
    def _():
        sums_ref[...] += sums


def combine(places, backs, grad_logits, full, after_attention, cot_pad, gain, images):
    rows, width = after_attention.shape
    block = lambda cols: pl.BlockSpec((PAD_SEQ, cols), lambda i: (i, 0))
    held = lambda a: pl.BlockSpec(a.shape, lambda i: (0, 0))
    return pl.pallas_call(
        combine_kernel,
        grid=(images,),
        in_specs=[
            block(LANES),
            held(backs[0]),
            held(backs[1]),
            block(LANES),
            pl.BlockSpec((width, LANES), lambda i: (0, 4 * width // LANES)),
            pl.BlockSpec((width, width), lambda i: (0, 3)),
            block(width),
            block(width),
            pl.BlockSpec((1, width), lambda i: (0, 0)),
        ],
        out_specs=[block(width)] * 3 + [pl.BlockSpec((8, width), lambda i: (0, 0))],
        out_shape=[
            jax.ShapeDtypeStruct((rows, width), F32),
            jax.ShapeDtypeStruct((rows, width), BF),
            jax.ShapeDtypeStruct((rows, width), BF),
            jax.ShapeDtypeStruct((8, width), F32),
        ],
        compiler_params=pltpu.CompilerParams(vmem_limit_bytes=VMEM_LIMIT),
        cost_estimate=pl.CostEstimate(
            flops=28 * rows * width * width, bytes_accessed=rows * width, transcendentals=0
        ),
    )(places, *backs, grad_logits, full, full, after_attention, cot_pad, gain.reshape(1, -1))


def axis_bits(size):
    return [1 << b for b in range(size.bit_length() - 1)]


def exchange(value, axis, bit):
    size = lax.axis_size(axis)
    return lax.ppermute(value, axis, [(i, i ^ bit) for i in range(size)])


def bit_of(axis, bit):
    return (lax.axis_index(axis) // bit) % 2


def gather_pieces(block, axis):
    pieces = {0: block}
    for bit in reversed(axis_bits(lax.axis_size(axis))):
        for k in list(pieces):
            pieces[k | bit] = exchange(pieces[k], axis, bit)
    return [pieces[k] for k in sorted(pieces)]


def other_core(value):
    return exchange(value, "shard", 1)


def other_chip(value):
    return exchange(value, "shard", 2)


def other_chip_in_turns(pairs):
    got = [[], []]
    last = None
    for at, start, stop in ((0, 0, 3), (1, 0, 4), (0, 3, 6), (1, 4, 6)):
        far, near = pairs[at]
        size = far.shape[1] // 6
        rows = slice(start * size, stop * size)
        send = (far[:, rows].astype(F32) + near[:, rows].astype(F32)).astype(BF)
        if last is not None:
            send, got[last][-1] = tie(send, got[last][-1])
        got[at].append(other_chip(send))
        last = at
    return [jnp.concatenate(g, axis=1) for g in got]


def reduce_chips(got, stay):
    held = stay + got.astype(F32)
    for bit in axis_bits(lax.axis_size("shard"))[2:]:
        view = held.reshape((-1, 2) + held.shape[1:])
        mine = bit_of("shard", bit)
        pick = lambda which: lax.dynamic_index_in_dim(view, which, 1, keepdims=False)
        held = pick(mine) + exchange(pick(1 - mine).astype(BF), "shard", bit).astype(F32)
    return held[0]


def owners_parts(held):
    owners = lax.axis_size("expert")
    rows, cols = held.shape
    got = trade(held.astype(BF).reshape(owners, rows // owners, cols))
    return jnp.sum(got.astype(F32), axis=0).astype(BF)


def owners_all(part):
    owners = lax.axis_size("expert")
    rows, cols = part.shape
    return trade(jnp.broadcast_to(part[None], (owners, rows, cols))).reshape(owners * rows, cols)


def owners_all_in_two(part):
    owners = lax.axis_size("expert")
    rows, cols = part.shape
    groups = [list(range(low, owners, 2)) for low in range(2)]
    held = lax.all_to_all(
        jnp.broadcast_to(part[None], (owners // 2, rows, cols)),
        "expert", split_axis=0, concat_axis=0, tiled=True, axis_index_groups=groups,
    )
    return held, exchange(held, "expert", 1)


def trade(view):
    return lax.all_to_all(view, "expert", split_axis=0, concat_axis=0, tiled=True)


def tie(*values):
    return lax.optimization_barrier(values)


def body(
    tokens, routes, capacity, ln1_gain, ln1_bias, ln2_gain, ln2_bias,
    w_qkv, w_proj, w_router, w_in, w_out, cotangent,
):
    count, width = tokens.shape
    experts = capacity.shape[0]
    owners = lax.axis_size("expert")
    shards = lax.axis_size("shard")
    images = count // SEQ
    padded = images * PAD_SEQ
    slot_count = 8 * ((2 * count + 8 * experts - 1) // (8 * experts))
    all_tokens = count * owners * shards
    me = lax.axis_index("expert").astype(jnp.int32).reshape(1)

    def pad_rows(values, fill=0):
        spread = values.reshape((images, SEQ) + values.shape[1:])
        room = [(0, 0), (0, PAD_SEQ - SEQ)] + [(0, 0)] * (values.ndim - 1)
        return jnp.pad(spread, room, constant_values=fill).reshape((padded,) + values.shape[1:])

    def cut_rows(values):
        spread = values.reshape((images, PAD_SEQ) + values.shape[1:])
        return spread[:, :SEQ].reshape((count,) + values.shape[1:])

    labels = jnp.arange(experts, dtype=jnp.int32)[:, None]
    first, second = routes[:, 0][None, :], routes[:, 1][None, :]
    hit_first, hit_second = first == labels, second == labels
    hits = jnp.concatenate([hit_first, hit_second], axis=0).astype(BF)
    order = lax.broadcasted_iota(jnp.int32, (count, count), 0) < lax.broadcasted_iota(
        jnp.int32, (count, count), 1
    )
    before = dot_nn(hits, order.astype(BF))
    totals = jnp.sum(hits.astype(F32), axis=1, keepdims=True)
    before_first = before[:experts]

    counts = (totals[:experts] + totals[experts:]).reshape(1, experts)
    high = jnp.floor(counts * (1.0 / COUNT_BASE))
    note = jnp.concatenate([high, counts - COUNT_BASE * high], axis=1).astype(BF)
    note = jnp.pad(note, ((0, w_router.shape[0] - 1), (0, 0)))
    room = jnp.zeros((w_router.shape[0], LANES - 3 * experts), BF)
    pieces = gather_pieces(
        jnp.concatenate([w_qkv, w_proj, w_router, note, room], axis=1), "shard"
    )

    before_second = before[experts:] + totals[:experts]
    limits = capacity[:, None].astype(F32)

    def slots(hit, ahead, choice):
        slot = jnp.sum(jnp.where(hit, ahead, 0.0), axis=0)
        limit = jnp.sum(jnp.where(hit, limits, 0.0), axis=0)
        kept = slot < limit
        slot = slot.astype(jnp.int32)
        return choice[0], slot, kept

    choices = [slots(hit_first, before_first, first), slots(hit_second, before_second, second)]
    head = 8 * ((slot_count + 15) // 16)
    spans = ((0, head), (head, slot_count - head))

    def chosen(start, size):
        found = []
        for choice, slot, kept in choices:
            inside = slot - start
            valid = kept & (inside >= 0) & (inside < size)
            found.append(pad_rows(jnp.where(valid, choice * size + inside, -1), -1))
        return found

    def selector(start, size):
        at = lax.broadcasted_iota(jnp.int32, (experts * size, 1), 0)
        first, second = chosen(start, size)
        return ((at == first[None, :]) | (at == second[None, :])).astype(BF)

    def send(select, rows):
        return dot_nn(select, rows).astype(BF).reshape(experts, -1, width)

    select_all = selector(0, slot_count)
    select = [selector(start, size) for start, size in spans]
    cot_pad = pad_rows(cotangent)
    cot_rows = trade(send(select_all, cot_pad))

    tok_pad = pad_rows(tokens)
    first_low, qkv_rows, heads_out, full = attend(tok_pad, ln1_gain, ln1_bias, pieces, images)
    proj_full = full[:, 3 * width : 4 * width]
    router_full = full[:, 4 * width :]
    notes = router_full[:: width // shards, experts : 3 * experts].astype(F32)
    notes = jnp.sum(notes, axis=0, keepdims=True)
    counts = COUNT_BASE * notes[:, :experts] + notes[:, experts:]
    counts = jnp.pad(counts, ((0, 0), (0, LANES - experts)))
    for bit in axis_bits(owners):
        counts = counts + exchange(counts, "expert", bit)
    route_share = counts[:, :experts] / (2.0 * all_tokens)
    token_rows = tok_pad.astype(F32)
    after_attention = token_rows + dot_nn(heads_out, proj_full)
    normed_two, inverse_two = norm_rows(after_attention)
    mid_low = (normed_two * ln2_gain + ln2_bias).astype(BF)

    sent, cot_rows, route_share = tie(send(select[0], mid_low), cot_rows, route_share)
    arrived = [trade(sent)]
    sent, arrived[0] = tie(send(select[1], mid_low), arrived[0])
    arrived.append(trade(sent))
    logits = dot_nn(mid_low, router_full)[:, :experts]
    live = (lax.broadcasted_iota(jnp.int32, (padded, 1), 0) % PAD_SEQ) < SEQ
    gate_probs = jnp.where(live, jax.nn.softmax(logits, axis=-1), 0.0)
    push = LOSS_WEIGHT * experts * route_share / all_tokens
    grad_logits = gate_probs * (push - jnp.sum(gate_probs * push, axis=-1, keepdims=True))
    grad_logits = jnp.pad(grad_logits, ((0, 0), (0, LANES - experts))).astype(BF)
    own = width // shards
    prob_sum = jnp.tile(jnp.pad(jnp.sum(gate_probs, axis=0), (0, own - experts)), shards)
    small = jnp.concatenate([prob_sum[None], dot_tn(grad_logits, mid_low)[:experts]], axis=0)
    small = jnp.pad(small, ((4, LANES - 4 - small.shape[0]), (0, 0)))

    places = jnp.stack([p for span in spans for p in chosen(*span)], axis=0)
    places = jnp.pad(places, ((0, LANES - places.shape[0]), (0, 0)), constant_values=-1).T
    arrived[0], grad_logits, small, places = tie(arrived[0], grad_logits, small, places)
    made = [
        run_expert(
            me,
            arrived[i].reshape(-1, width),
            cot_rows, start, full, w_in[0], w_out[0], experts,
        )
        for i, (start, _) in enumerate(spans)
    ]
    hidden, grad_pre, grad_made, gated, grad_rows, router_parts = zip(*made)
    grad_rows = [g.reshape(experts, -1, width) for g in grad_rows]
    backs = [trade(grad_rows[0])]
    gated = jnp.concatenate([g.reshape(experts, -1, width) for g in gated], axis=1)
    sent, backs[0], gated = tie(grad_rows[1], backs[0], gated)
    backs.append(trade(sent))
    mids = [a.reshape(-1, width) for a in arrived]
    mids[0], backs[0] = tie(mids[0], backs[0])
    place = jnp.stack([bit_of("shard", 1), bit_of("shard", 2)]).astype(jnp.int32)
    grads = weight_grads(place, mids, grad_made, grad_pre, hidden, shards)
    ins, outs = list(grads[:4]), list(grads[4:])
    parts = router_parts[0] + router_parts[1]
    small = small + jnp.pad(parts[: LANES - 5], ((5, 0), (0, 0)))
    gated, backs[1], ins[3], outs[3], small = tie(gated, backs[1], ins[3], outs[3], small)
    returned = trade(gated)

    backs = [b.reshape(-1, width) for b in backs]
    grad_after, grad_heads, grad_heads_out, sums_two = combine(
        places, backs, grad_logits, full, after_attention, cot_pad, ln2_gain, images
    )
    back = functools.partial(
        attend_back, place, qkv_rows, grad_heads_out, full, first_low, images, shards
    )
    grad_first, *share = back(0, (heads_out, grad_heads), False)
    send = (share[2].astype(F32) + other_core(share[0]).astype(F32)).astype(BF)
    total = reduce_chips(other_chip(send), share[3].astype(F32) + other_core(share[1]).astype(F32))
    rest = (grad_first, tok_pad, grad_after, ln1_gain.reshape(1, -1), sums_two, small)
    grad_tokens, *share = back(1, rest, True)
    share[0], share[1], returned, total = tie(share[0], share[1], returned, total)
    send = (share[2].astype(F32) + other_core(share[0]).astype(F32)).astype(BF)
    total, ins[2], outs[2] = tie(total, ins[2], outs[2])
    part = owners_parts(total)
    last = reduce_chips(other_chip(send), share[3].astype(F32) + other_core(share[1]).astype(F32))
    last = owners_parts(last)
    both = (outs, ins)
    got = other_chip_in_turns([(p[2], other_core(p[0])) for p in both])
    grad_expert_out, grad_expert_in = [
        reduce_chips(g, p[3].astype(F32) + other_core(p[1]).astype(F32)) for g, p in zip(got, both)
    ]
    mixed = cut_rows(after_attention + dot_tn(select_all, returned.reshape(-1, width))).astype(BF)
    part, mixed = tie(part, mixed)
    first_half, second_half = owners_all_in_two(part), owners_all(last)
    second_half, grad_expert_in = tie(second_half, grad_expert_in)

    grad_qkv_weight, proj_total, router_total, balance_loss, *vectors = assemble(
        (me % 2).astype(jnp.int32), *first_half, second_half, route_share, experts / all_tokens
    )
    balance_loss = balance_loss[0, 0]
    vectors = [v[0] for v in vectors]
    return (
        mixed,
        balance_loss,
        grad_tokens,
        vectors[0],
        vectors[1],
        vectors[2],
        vectors[3],
        grad_qkv_weight,
        proj_total,
        router_total.T,
        grad_expert_in[None],
        grad_expert_out[None],
    )


def solution(mesh):
    rows = P(("expert", "shard"), None)
    in_specs = (
        rows, rows, P(), P(), P(), P(), P(),
        P("shard", None), P("shard", None), P("shard", None),
        P("expert", None, None), P("expert", None, None), rows,
    )
    out_specs = (
        rows, P(), rows, P("shard"), P("shard"), P("shard"), P("shard"),
        P("shard", None), P("shard", None), P("shard", None),
        P("expert", None, "shard"), P("expert", "shard", None),
    )
    return jax.shard_map(body, mesh=mesh, in_specs=in_specs, out_specs=out_specs, check_vma=False)
```
